128 devices in a mesh: facet: 32 (over z, y_hi, x), freq: 4 (over y_lo, core).
Axes of the slice: x: 4, y: 4 (y_hi: 2, y_lo: 2; y = y_hi * 2 + y_lo), z: 4, core: 2. Of those that a mesh axis runs over, the one named last changes fastest.
Arguments:
- visibilities: float32 [32, 10, 2, 128, 128], P('facet', None, None, 'freq'), may hold values from -6 to 6
- coords: float32 [32, 10, 3, 128], P('facet'), may hold values from -1500 to 1500, as said below
- corners: int32 [2, 32, 10], replicated, may hold values from 0 to 480
- owners: int32 [2], replicated, may hold values from 0 to 31, as said below
- assign: int32 [32, 20], P('facet'), may hold values from 0 to 19, as said below
- counts: int32 [32], P('facet'), may hold values from 2 to 20, as said below
Outputs:
- dirty: float32 [32, 512, 512], P('facet', 'freq')
The draws below stay inside these ranges and needn't reach their ends.
Inputs may be any that keep to these rules, and one draw needn't show every extreme that they name: `owners`: the two sets lie in different slots, one of them in the last slot. `assign`: each facet's row is a permutation of the 20 block numbers; only its first counts entries are gridded. `counts`: some facet grids all 20 blocks. `coords`: at every channel, u and v of each row of a block lie within 12 cells of the centre of that block's subgrid.
All inputs are finite; a program needn't handle non-finite values.
Results may differ from the reference program's by a relative error of at most 0.0037.
Values sent between devices are 32-bit elements; how exact they have to be, the bound alone decides.
A program may use at most 64 MiB of HBM per device.

```python
import math
import jax
import jax.numpy as jnp
from jax import lax

SUB = 32
G = 512
BLK = 128
CH = 32
BPC = 10
SMAX = 20
CHANS = 128
N_FACET = 32
N_FREQ = 4


def corner_table(key):
    return jax.random.randint(jax.random.fold_in(key, 11), (2, N_FACET, BPC), 0, G - SUB + 1).astype(jnp.int32)


def draw_corners(key, part):
    return corner_table(key)


def draw_coords(key, part):
    corner_cells = corner_table(key).astype(jnp.float32)
    centre_cells = jnp.transpose(corner_cells, (1, 2, 0))[:, :, :, None] + (SUB // 2 - G // 2)
    offsets = jax.random.uniform(jax.random.fold_in(key, 21), (N_FACET, BPC, 2, BLK), minval=-8.0, maxval=8.0)
    depth = jnp.clip(300.0 * jax.random.normal(jax.random.fold_in(key, 22), (N_FACET, BPC, 1, BLK)), -1500.0, 1500.0)
    planar = (centre_cells + offsets) / 1.01
    return jnp.concatenate([planar, depth], axis=2).astype(jnp.float32)


def draw_owners(key, part):
    other_slot = jax.random.randint(jax.random.fold_in(key, 13), (), 0, N_FACET - 1)
    last_slot = jnp.full((), N_FACET - 1, jnp.int32)
    flip = jax.random.randint(jax.random.fold_in(key, 17), (), 0, 2)
    first = jnp.where(flip == 1, last_slot, other_slot)
    second = jnp.where(flip == 1, other_slot, last_slot)
    return jnp.stack([first, second]).astype(jnp.int32)


def draw_assign(key, part):
    scores = jax.random.randint(jax.random.fold_in(key, 14), (N_FACET, SMAX), 0, 1048576) * SMAX
    scores = scores + jnp.arange(SMAX, dtype=jnp.int32)[None, :]
    return jnp.argsort(scores, axis=1, stable=True).astype(jnp.int32)


def draw_counts(key, part):
    divisor = jax.random.randint(jax.random.fold_in(key, 15), (N_FACET,), 1, 9)
    chosen = jax.random.randint(jax.random.fold_in(key, 16), (), 0, N_FACET)
    return jnp.where(jnp.arange(N_FACET) == chosen, SMAX, SMAX // divisor).astype(jnp.int32)


def level_of(stream_key, shape, shards, least, high):
    level = 1.0
    for dim, blocks in shards:
        steps = jax.random.uniform(jax.random.fold_in(jax.random.fold_in(stream_key, 6), dim), (blocks,), jnp.float32, least / len(shards), high / len(shards))
        level = level * jnp.repeat(jnp.exp(steps), shape[dim] // blocks).reshape((-1,) + (1,) * (len(shape) - 1 - dim))
    return level


def gaussian(stream_key, dims, deviation, limit, cuts=(), kind=jnp.bfloat16):
    array = jax.random.normal(stream_key, dims, jnp.float32) * deviation
    if len(cuts) > 0:
        array = level_of(stream_key, dims, cuts, -0.22, 0.18) * array
    return jnp.clip(array, min=-limit, max=limit).astype(kind)


def setup_inputs(seed: int = 0) -> dict:
    key_list = jax.random.split(jax.random.key(seed), 7)
    visibilities = gaussian(key_list[0], (N_FACET, BPC, 2, CHANS, BLK), 1.0, 6.0, ((0, 32), (3, 4)), jnp.float32)
    coords = draw_coords(jax.random.fold_in(key_list[6], 71), 0)
    corners = draw_corners(jax.random.fold_in(key_list[6], 71), 0)
    owners = draw_owners(jax.random.fold_in(key_list[6], 71), 0)
    assign = draw_assign(jax.random.fold_in(key_list[6], 71), 0)
    counts = draw_counts(jax.random.fold_in(key_list[6], 71), 0)
    return {"visibilities": visibilities, "coords": coords, "corners": corners, "owners": owners, "assign": assign, "counts": counts}


two_pi = 2.0 * math.pi
field_width = 0.02
band_spread = 0.02
batch_items = 8
highest = lax.Precision.HIGHEST

def facet_center(facet_id, facet_total):
    row_total = facet_total // 8
    column = (facet_id % 8).astype(jnp.float32) - 3.5
    row_pos = (facet_id // 8).astype(jnp.float32) - (row_total - 1) / 2.0
    radius = field_width * field_width * (column * column + row_pos * row_pos)
    w_shift = -radius / (1.0 + jnp.sqrt(1.0 - radius))
    return (column, row_pos, w_shift)

def subgrid_tables():
    offsets = jnp.arange(SUB, dtype=jnp.int32) - SUB // 2
    position = offsets.astype(jnp.float32)
    profile = 1.0 - 0.8 * (position / (SUB / 2.0)) ** 2
    taper_square = profile[:, None] * profile[None, :]
    phase_index = offsets[:, None] * offsets[None, :] % SUB
    phase_angle = -two_pi * phase_index.astype(jnp.float32) / SUB
    return (position, taper_square, jnp.cos(phase_angle), jnp.sin(phase_angle))

def image_tables():
    offsets = jnp.arange(G, dtype=jnp.int32) - G // 2
    phase_index = offsets[:, None] * offsets[None, :] % G
    phase_angle = two_pi * phase_index.astype(jnp.float32) / G
    return (jnp.cos(phase_angle), jnp.sin(phase_angle))

def subgrid_terms(vis_blocks, coord_blocks, freq_ratio, corner_u, corner_v, column, row_pos, w_shift, tables):
    position = tables[0]
    item_total = vis_blocks.shape[0]
    scaled = coord_blocks[:, :, None, :] * freq_ratio[None, None, :, None]
    u_cells = scaled[:, 0]
    v_cells = scaled[:, 1]
    w_waves = scaled[:, 2]
    rotation = two_pi * (u_cells * column[:, None, None] + v_cells * row_pos[:, None, None] + w_waves * w_shift[:, None, None])
    rot_real = jnp.cos(rotation)
    rot_imag = jnp.sin(rotation)
    vis_real = vis_blocks[:, 0] * rot_real - vis_blocks[:, 1] * rot_imag
    vis_imag = vis_blocks[:, 0] * rot_imag + vis_blocks[:, 1] * rot_real
    centre_shift = G // 2 - SUB // 2
    delta_u = (u_cells + (centre_shift - corner_u).astype(jnp.float32)[:, None, None]).reshape(item_total, 1, -1)
    delta_v = (v_cells + (centre_shift - corner_v).astype(jnp.float32)[:, None, None]).reshape(item_total, 1, -1)
    angle_u = two_pi / SUB * delta_u * position[None, :, None]
    left_factor = jnp.concatenate([jnp.cos(angle_u), jnp.sin(angle_u)], axis=2).astype(jnp.bfloat16)
    angle_v = two_pi / SUB * delta_v * position[None, :, None]
    wave_real = jnp.cos(angle_v)
    wave_imag = jnp.sin(angle_v)
    flat_real = vis_real.reshape(item_total, 1, -1)
    flat_imag = vis_imag.reshape(item_total, 1, -1)
    right_real = flat_real * wave_real - flat_imag * wave_imag
    right_imag = flat_real * wave_imag + flat_imag * wave_real
    upper_rows = jnp.concatenate([right_real, -right_imag], axis=2)
    lower_rows = jnp.concatenate([right_imag, right_real], axis=2)
    right_factor = jnp.concatenate([upper_rows, lower_rows], axis=1).astype(jnp.bfloat16)
    return (left_factor, right_factor)

def subgrid_finish(product, tables):
    taper_square, dft_real, dft_imag = (tables[1], tables[2], tables[3])
    image_real = product[:, :, :SUB] * taper_square
    image_imag = product[:, :, SUB:] * taper_square
    half_real = jnp.einsum('pl,slm->spm', dft_real, image_real, precision=highest) - jnp.einsum('pl,slm->spm', dft_imag, image_imag, precision=highest)
    half_imag = jnp.einsum('pl,slm->spm', dft_real, image_imag, precision=highest) + jnp.einsum('pl,slm->spm', dft_imag, image_real, precision=highest)
    uv_real = jnp.einsum('spm,qm->spq', half_real, dft_real, precision=highest) - jnp.einsum('spm,qm->spq', half_imag, dft_imag, precision=highest)
    uv_imag = jnp.einsum('spm,qm->spq', half_real, dft_imag, precision=highest) + jnp.einsum('spm,qm->spq', half_imag, dft_real, precision=highest)
    return jnp.stack([uv_real, uv_imag], axis=1)

def add_pieces(uv_grid, pieces, corner_u, corner_v, weights):
    zero_index = jnp.zeros((), jnp.int32)
    for item in range(batch_items):
        anchor = (zero_index, corner_u[item].astype(jnp.int32), corner_v[item].astype(jnp.int32))
        current = lax.dynamic_slice(uv_grid, anchor, (2, SUB, SUB))
        uv_grid = lax.dynamic_update_slice(uv_grid, current + pieces[item] * weights[item], anchor)
    return uv_grid

def reference(visibilities, coords, corners, owners, assign, counts):
    tables = subgrid_tables()
    channel_total = CH * N_FREQ
    freq_ratio = 1.0 + band_spread * jnp.arange(channel_total, dtype=jnp.float32) / channel_total
    vis_all = visibilities[owners].reshape(2 * BPC, 2, channel_total, BLK)
    coord_all = coords[owners].reshape(2 * BPC, 3, BLK)
    corner_all = corners[:, owners, :].reshape(2, 2 * BPC)
    cos_table, sin_table = image_tables()
    image_scale = 1.0 / (SUB * SUB * math.sqrt(SMAX * BLK * channel_total))

    def one_facet(facet_id):
        column, row_pos, w_shift = facet_center(facet_id, N_FACET)
        item_count = counts[facet_id]
        block_list = assign[facet_id]

        def grid_step(batch_index, uv_grid):
            item_index = batch_index * batch_items + jnp.arange(batch_items, dtype=jnp.int32)
            weights = (item_index < item_count).astype(jnp.float32)
            block_index = jnp.take(block_list, jnp.minimum(item_index, SMAX - 1))
            corner_u = jnp.take(corner_all[0], block_index)
            corner_v = jnp.take(corner_all[1], block_index)
            left_factor, right_factor = subgrid_terms(jnp.take(vis_all, block_index, axis=0), jnp.take(coord_all, block_index, axis=0), freq_ratio, corner_u, corner_v, jnp.full((batch_items,), column), jnp.full((batch_items,), row_pos), jnp.full((batch_items,), w_shift), tables)
            product = jnp.einsum('slk,smk->slm', left_factor.astype(jnp.float32), right_factor.astype(jnp.float32), precision=highest)
            pieces = subgrid_finish(product, tables)
            return add_pieces(uv_grid, pieces, corner_u, corner_v, weights)
        batch_total = (item_count + batch_items - 1) // batch_items
        uv_grid = lax.fori_loop(0, batch_total, grid_step, jnp.zeros((2, G, G), jnp.float32))
        half_real = jnp.dot(cos_table, uv_grid[0], precision=highest, preferred_element_type=jnp.float32) - jnp.dot(sin_table, uv_grid[1], precision=highest, preferred_element_type=jnp.float32)
        half_imag = jnp.dot(cos_table, uv_grid[1], precision=highest, preferred_element_type=jnp.float32) + jnp.dot(sin_table, uv_grid[0], precision=highest, preferred_element_type=jnp.float32)
        image_part = jnp.dot(half_real, cos_table, precision=highest, preferred_element_type=jnp.float32) - jnp.dot(half_imag, sin_table, precision=highest, preferred_element_type=jnp.float32)
        return image_part * image_scale
    return lax.map(one_facet, jnp.arange(N_FACET, dtype=jnp.int32))
```

```python
import functools
import math

import jax
import jax.numpy as jnp
import numpy as np
from jax import lax
from jax.experimental import pallas as pl
from jax.experimental.pallas import tpu as pltpu
from jax.sharding import PartitionSpec as P

SUB = 32
G = 512
BPC = 10
CH = 32
N_FACET = 32
N_FREQ = 4
BLK = 128
CHANS = CH * N_FREQ
CHUNK = 8
MESH = pl.DeviceIdType.MESH
f32 = jnp.float32
bf16 = jnp.bfloat16

DELTA = (
    (0, 0, 0),
    (1, 0, 0),
    (3, 0, 0),
    (0, 0, 1),
    (0, 0, 3),
    (1, 0, 1),
    (1, 0, 3),
    (3, 0, 1),
    (3, 0, 3),
    (0, 1, 0),
)
LAST = N_FACET - 1
SLOTS = 11


def fit_sincos():
    s = 0.125 * (1.0 - np.cos(np.pi * (np.arange(400) + 0.5) / 400))
    t = np.sqrt(s)
    poly = np.polynomial.chebyshev
    domain = [0.0, 0.25]
    c = poly.Chebyshev.fit(s, np.cos(2 * np.pi * t), 7, domain=domain)
    n = poly.Chebyshev.fit(s, np.sin(2 * np.pi * t) / t, 7, domain=domain)
    to_power = lambda p: p.convert(kind=np.polynomial.Polynomial).coef
    return [float(v) for v in to_power(c)], [float(v) for v in to_power(n)]


COS_POLY, SIN_POLY = fit_sincos()


def sincos(cycles):
    t = cycles - jnp.floor(cycles + 0.5)
    s = t * t
    c = jnp.full_like(s, COS_POLY[-1])
    for k in COS_POLY[-2::-1]:
        c = c * s + k
    n = jnp.full_like(s, SIN_POLY[-1])
    for k in SIN_POLY[-2::-1]:
        n = n * s + k
    return c, n * t


def cmul(a, b):
    return a[0] * b[0] - a[1] * b[1], a[0] * b[1] + a[1] * b[0]


def both(a, b):
    rr, ii, ri, ir = a[0] * b[0], a[1] * b[1], a[0] * b[1], a[1] * b[0]
    return (rr - ii, ri + ir), (rr + ii, ir - ri)


def image_table():
    x = np.arange(G) - G // 2
    l = np.arange(SUB) - SUB // 2
    n = np.arange(SUB) - SUB // 2
    theta = x[:, None] / G - l[None, :] / SUB
    kernel = np.exp(2j * np.pi * n[None, None, :] * theta[:, :, None]).sum(axis=2)
    real = (kernel * np.exp(1j * np.pi * theta)).real
    real = real * (1.0 - 0.8 * (l / (SUB / 2.0)) ** 2)[None, :]
    upper, lower = real[:, SUB // 2 :], real[:, SUB // 2 - 1 :: -1]
    return np.concatenate([upper + lower, upper - lower], axis=1)


def shifted(f, delta, sign):
    z, y, x = f // 8, (f // 4) % 2, f % 4
    z = (z + (delta[0] if sign > 0 else 4 - delta[0])) % 4
    y = (y + delta[1]) % 2
    x = (x + (delta[2] if sign > 0 else 4 - delta[2])) % 4
    return z * 8 + y * 4 + x


def shifted_int(f, delta):
    return ((f // 8 + delta[0]) % 4) * 8 + ((f // 4 % 2 + delta[1]) % 2) * 4 + (f % 4 + delta[2]) % 4


LAST_POS = tuple(shifted_int(LAST, d) for d in DELTA)


def exchange_kernel(vis, coord, cand_vis, cand_coord, send_sem, recv_sem):
    f = lax.axis_index("facet")
    q = lax.axis_index("freq")
    barrier = pltpu.get_barrier_semaphore()
    for j in range(1, BPC):
        pl.semaphore_signal(
            barrier, inc=1, device_id=(shifted(f, DELTA[j], -1), q), device_id_type=MESH
        )
    own = [
        pltpu.make_async_copy(vis.at[0, 0], cand_vis.at[0], recv_sem.at[0, 0]),
        pltpu.make_async_copy(coord.at[0, 0], cand_coord.at[0], recv_sem.at[0, 1]),
    ]
    for c in own:
        c.start()
    pl.semaphore_wait(barrier, BPC - 1)
    copies = []
    for j in range(BPC - 1, 0, -1):
        to = (shifted(f, DELTA[j], 1), q)
        for n, (src, dst) in enumerate(((vis, cand_vis), (coord, cand_coord))):
            copies.append(
                pltpu.make_async_remote_copy(
                    src_ref=src.at[0, j],
                    dst_ref=dst.at[j],
                    send_sem=send_sem.at[j, n],
                    recv_sem=recv_sem.at[j, n],
                    device_id=to,
                    device_id_type=MESH,
                )
            )
            copies[-1].start()
    for c in own:
        c.wait()
    for c in copies:
        c.wait()


def exchange(vis, coord):
    return pl.pallas_call(
        exchange_kernel,
        out_shape=(
            jax.ShapeDtypeStruct((BPC, 2, CH, BLK), f32),
            jax.ShapeDtypeStruct((BPC, 3, BLK), f32),
        ),
        in_specs=[pl.BlockSpec(memory_space=pl.ANY)] * 2,
        out_specs=[pl.BlockSpec(memory_space=pl.ANY)] * 2,
        scratch_shapes=[
            pltpu.SemaphoreType.DMA((BPC, 2)),
            pltpu.SemaphoreType.DMA((BPC, 2)),
        ],
        compiler_params=pltpu.CompilerParams(collective_id=0, has_side_effects=True),
        name="exchange_blocks",
    )(vis, coord)


def prepare_unit(q, vis, coord, ou, ov, xs, ys, vs):
    channel = q * CH + lax.broadcasted_iota(jnp.int32, (CH, BLK), 0)
    ratio = 1.0 + 0.02 * channel.astype(f32) / CHANS
    u = coord[0:1, :] * ratio
    v = coord[1:2, :] * ratio
    w = coord[2:3, :] * ratio
    du = u + (240.5 - ou.astype(f32))
    dv = v + (240.5 - ov.astype(f32))
    zeta = []
    for d, ref in ((du, xs), (dv, ys)):
        base = sincos(d * (1.0 / 64.0))
        zeta.append(base)
        square = cmul(base, base)
        powers = [base]
        while len(powers) < 16:
            powers += [cmul(p, square) for p in powers]
            square = cmul(square, square)
        for i, (c, s) in enumerate(powers):
            ref[i * CH : (i + 1) * CH, :] = c
            ref[(i + 16) * CH : (i + 17) * CH, :] = s
    turn = cmul(zeta[0], zeta[1])
    value = cmul((vis[0], vis[1]), (turn[0], -turn[1]))
    pu = sincos(u * 0.5)
    pu2 = cmul(pu, pu)
    a_phase = [pu]
    for _ in range(3):
        a_phase.append(cmul(a_phase[-1], pu2))
    pv = sincos(v * 0.5)
    e_phase = [pv, cmul(pv, cmul(pv, pv))]
    for e in range(2):
        plus, minus = both(value, e_phase[e])
        for a in range(4):
            rho = 0.0004 * ((a + 0.5) ** 2 + (e + 0.5) ** 2)
            depth = sincos(w * (-rho / (1.0 + math.sqrt(1.0 - rho))))
            for row, turned in ((2 + e, plus), (1 - e, minus)):
                right, left = both(cmul(turned, depth), a_phase[a])
                for column, out in ((4 + a, right), (3 - a, left)):
                    facet = row * 8 + column
                    vs[facet * CH : (facet + 1) * CH, :] = out[0]
                    vs[(facet + 32) * CH : (facet + 33) * CH, :] = out[1]


def unit_products(xs, ys, vs, pbuf, vbuf, acc, turned, put):
    def chunk_step(k, carry):
        for cc in range(CHUNK):
            c = k * CHUNK + cc
            lanes = slice(cc * BLK, (cc + 1) * BLK)
            y = [ys[pl.ds(t * 8 * CH + c, 8, stride=CH), :] for t in range(4)]
            for i in range(32):
                x = jnp.broadcast_to(xs[pl.ds(i * CH + c, 1), :], (8, BLK))
                row = (i % 8) * 128 + (i // 8) * 32
                for h in range(2):
                    pair = jnp.concatenate([x * y[2 * h], x * y[2 * h + 1]], axis=0)
                    pbuf[row + 16 * h : row + 16 * h + 16, lanes] = pair.astype(bf16)
            for t in range(4):
                pair = jnp.concatenate(
                    [
                        vs[pl.ds((2 * t + h) * 8 * CH + c, 8, stride=CH), :]
                        for h in range(2)
                    ],
                    axis=0,
                )
                high = pair.astype(bf16)
                low = (pair - high.astype(f32)).astype(bf16)
                vbuf[16 * t : 16 * t + 16, lanes] = high
                vbuf[64 + 16 * t : 64 + 16 * t + 16, lanes] = low
        part = lax.dot_general(
            pbuf[...], vbuf[...], (((1,), (1,)), ((), ())), preferred_element_type=f32
        )

        @pl.when(k == 0)
        def _():
            acc[...] = part

        @pl.when(k > 0)
        def _():
            acc[...] = acc[...] + part

        return carry

    lax.fori_loop(0, CH // CHUNK, chunk_step, 0)
    for n in range(8):
        flipped = acc[n * 128 : (n + 1) * 128, :].T
        turned[n * 64 : (n + 1) * 64, :] = flipped[:64] + flipped[64:]
    for part in range(2):
        for facet in range(N_FACET):
            put(facet, part, turned[pl.ds(part * 32 + facet, 8, stride=64), :])


def units_kernel(
    owners, corners, cand_vis, cand_coord, out, vis, coord, xs, ys, vs, pbuf, vbuf, acc, turned, sem
):
    f = lax.axis_index("facet")
    q = lax.axis_index("freq")

    def unit(n, carry):
        owner = jnp.where(
            n == 1, LAST, jnp.where(owners[0] == LAST, owners[1], owners[0])
        ).astype(jnp.int32)
        block = jnp.int32(-1)
        for j in range(BPC):
            block = jnp.where(shifted(f, DELTA[j], -1) == owner, j, block)

        @pl.when(block >= 0)
        def _():
            copies = [
                pltpu.make_async_copy(cand_vis.at[block], vis, sem.at[0]),
                pltpu.make_async_copy(cand_coord.at[block], coord, sem.at[1]),
            ]
            for c in copies:
                c.start()
            for c in copies:
                c.wait()
            prepare_unit(
                q, vis, coord, corners[0, owner, block], corners[1, owner, block], xs, ys, vs
            )

            def put(facet, part, value):
                out[n, facet, part * 8 : (part + 1) * 8, :] = value

            unit_products(xs, ys, vs, pbuf, vbuf, acc, turned, put)

        return carry

    lax.fori_loop(0, 2, unit, 0)


def unit_scratch():
    return [
        pltpu.VMEM((32 * CH, BLK), f32),
        pltpu.VMEM((32 * CH, BLK), f32),
        pltpu.VMEM((64 * CH, BLK), f32),
        pltpu.VMEM((1024, CHUNK * BLK), bf16),
        pltpu.VMEM((128, CHUNK * BLK), bf16),
        pltpu.VMEM((1024, 128), f32),
        pltpu.VMEM((512, 128), f32),
    ]


def units(owners, corners, cand_vis, cand_coord):
    return pl.pallas_call(
        units_kernel,
        out_shape=jax.ShapeDtypeStruct((2, N_FACET, 16, 128), f32),
        in_specs=[pl.BlockSpec(memory_space=pltpu.SMEM)] * 2
        + [pl.BlockSpec(memory_space=pl.ANY)] * 2,
        out_specs=pl.BlockSpec(memory_space=pltpu.VMEM),
        scratch_shapes=[pltpu.VMEM((2, CH, BLK), f32), pltpu.VMEM((3, BLK), f32)]
        + unit_scratch()
        + [pltpu.SemaphoreType.DMA((2,))],
        name="grid_blocks",
    )(owners, corners, cand_vis, cand_coord)


def collect_kernel(res, out, from_a, from_b, total, send_sem, recv_a, recv_b, peer_send, peer_recv):
    f = lax.axis_index("facet")
    q = lax.axis_index("freq")
    x = f % 4
    last_block = jnp.int32(-1)
    for j in range(BPC):
        last_block = jnp.where(f == LAST_POS[j], j, last_block)
    is_last = last_block >= 0
    q_last = last_block % 4
    barrier = pltpu.get_barrier_semaphore()

    def signal(facet, freq):
        pl.semaphore_signal(barrier, inc=1, device_id=(facet, freq), device_id_type=MESH)

    def tell_a(n, carry):
        facet, freq = (n // 4) * 4 + q, n % 4

        @pl.when(jnp.logical_or(facet != f, freq != q))
        def _():
            signal(facet, freq)

        return carry

    lax.fori_loop(0, 32, tell_a, 0)
    for j in range(BPC):
        for freq in range(N_FREQ):

            @pl.when(
                jnp.logical_and(j % 4 == q, jnp.logical_or(f != LAST_POS[j], freq != q))
            )
            def _():
                signal(LAST_POS[j], freq)

    for d in range(1, N_FREQ):
        signal(f, (q + d) % N_FREQ)
    expected = 32 + 3 - jnp.where(x == q, 1, 0)
    expected = expected + jnp.where(is_last, 32 - jnp.where(q_last == q, 1, 0), 0)
    pl.semaphore_wait(barrier, expected)

    def copy_a(facet):
        return pltpu.make_async_remote_copy(
            src_ref=res.at[0, facet],
            dst_ref=from_a.at[f // 4, q],
            send_sem=send_sem.at[0, facet],
            recv_sem=recv_a.at[f // 4, q],
            device_id=(facet, x),
            device_id_type=MESH,
        )

    def copy_b(facet):
        return pltpu.make_async_remote_copy(
            src_ref=res.at[1, facet],
            dst_ref=from_b.at[last_block // 4, q],
            send_sem=send_sem.at[1, facet],
            recv_sem=recv_b.at[last_block // 4, q],
            device_id=(facet, q_last),
            device_id_type=MESH,
        )

    own_a = pltpu.make_async_copy(res.at[0, f], from_a.at[f // 4, q], recv_a.at[f // 4, q])
    own_b = pltpu.make_async_copy(
        res.at[1, f], from_b.at[last_block // 4, q], recv_b.at[last_block // 4, q]
    )

    def send_all(copy, own, to):
        def step(n, carry):
            facet = (f + n) % N_FACET
            here = jnp.logical_and(facet == f, to == q)

            @pl.when(jnp.logical_not(here))
            def _():
                copy(facet).start()

            @pl.when(here)
            def _():
                own.start()

            return carry

        lax.fori_loop(0, N_FACET, step, 0)

    def drain(copy, to):
        def step(facet, carry):
            @pl.when(jnp.logical_not(jnp.logical_and(facet == f, to == q)))
            def _():
                copy(facet).wait_send()

            return carry

        lax.fori_loop(0, N_FACET, step, 0)

    @pl.when(is_last)
    def _():
        send_all(copy_b, own_b, q_last)

    send_all(copy_a, own_a, x)

    def add_a(s, carry):
        for p in range(N_FREQ):
            pltpu.make_async_copy(from_a.at[s, p], from_a.at[s, p], recv_a.at[s, p]).wait()
        total[s] = (from_a[s, 0] + from_a[s, 1]) + (from_a[s, 2] + from_a[s, 3])
        return carry

    lax.fori_loop(0, 8, add_a, 0)
    for s in range(3):

        @pl.when(q + 4 * s < BPC)
        def _():
            for p in range(N_FREQ):
                pltpu.make_async_copy(from_b.at[s, p], from_b.at[s, p], recv_b.at[s, p]).wait()
            total[8 + s] = (from_b[s, 0] + from_b[s, 1]) + (from_b[s, 2] + from_b[s, 3])

    peers = []
    for d in range(1, N_FREQ):
        peers.append(
            pltpu.make_async_remote_copy(
                src_ref=total,
                dst_ref=out.at[q],
                send_sem=peer_send.at[d],
                recv_sem=peer_recv.at[d],
                device_id=(f, (q + d) % N_FREQ),
                device_id_type=MESH,
            )
        )
        peers[-1].start()
    mine = pltpu.make_async_copy(total, out.at[q], peer_send.at[0])
    mine.start()
    mine.wait()
    for d in range(1, N_FREQ):
        source = (q + N_FREQ - d) % N_FREQ
        pltpu.make_async_copy(total, out.at[source], peer_recv.at[d]).wait()
    for p in peers:
        p.wait_send()
    drain(copy_a, x)

    @pl.when(is_last)
    def _():
        drain(copy_b, q_last)


def collect(res):
    return pl.pallas_call(
        collect_kernel,
        out_shape=jax.ShapeDtypeStruct((N_FREQ, SLOTS, 16, 128), f32),
        in_specs=[pl.BlockSpec(memory_space=pl.ANY)],
        out_specs=pl.BlockSpec(memory_space=pl.ANY),
        scratch_shapes=[
            pltpu.VMEM((8, N_FREQ, 16, 128), f32),
            pltpu.VMEM((3, N_FREQ, 16, 128), f32),
            pltpu.VMEM((SLOTS, 16, 128), f32),
            pltpu.SemaphoreType.DMA((2, N_FACET)),
            pltpu.SemaphoreType.DMA((8, N_FREQ)),
            pltpu.SemaphoreType.DMA((3, N_FREQ)),
            pltpu.SemaphoreType.DMA((N_FREQ,)),
            pltpu.SemaphoreType.DMA((N_FREQ,)),
        ],
        compiler_params=pltpu.CompilerParams(collective_id=1, has_side_effects=True),
        name="collect_results",
    )(res)


def split(a):
    high = a.astype(bf16)
    return high, (a - high.astype(f32)).astype(bf16)


def image_kernel(
    owners, corners, assign, counts, got, table, table_t, out, weight, zr, zi, br, bi
):
    q = lax.axis_index("freq")
    lane = lax.broadcasted_iota(jnp.int32, (8, 128), 1)
    first_last = owners[0] == LAST
    other = jnp.where(first_last, owners[1], owners[0]).astype(jnp.int32)
    for b in range(2 * BPC):
        weight[b] = 0.0
    count = counts[0]
    for n in range(2 * BPC):
        weight[assign[0, n]] = jnp.where(n < count, 1.0, 0.0).astype(f32)
    corner_u, corner_v, weights, places = [], [], [], []
    for k in range(2 * BPC):
        j = k % BPC
        if k < BPC:
            owner = jnp.int32(LAST)
            places.append(jnp.int32((j % 4) * SLOTS + 8 + j // 4))
            base = jnp.where(first_last, 0, BPC)
        else:
            owner = other
            t = shifted(other, DELTA[j], 1)
            places.append((t % 4) * SLOTS + t // 4)
            base = jnp.where(first_last, BPC, 0)
        corner_u.append(corners[0, owner, j])
        corner_v.append(corners[1, owner, j])
        weights.append(weight[base + j])
    sine_lane = lane % 32 >= 16
    group = lane // 32
    for tile in range(5):
        parts = [[None] * 4, [None] * 4]
        for g in range(4):
            k = tile * 4 + g
            block = got[places[k]]
            re, im = block[:8] * weights[k], block[8:] * weights[k]
            for half in range(2):
                if half == 0:
                    new_re = jnp.where(sine_lane, -im, re)
                    new_im = jnp.where(sine_lane, re, im)
                else:
                    new_re = jnp.where(sine_lane, -re, -im)
                    new_im = jnp.where(sine_lane, -im, re)
                for i4 in (2 * half, 2 * half + 1):
                    shift = ((g - i4) * 32) % 128
                    for p, value in enumerate((new_re, new_im)):
                        if shift:
                            value = pltpu.roll(value, shift, 1)
                        old = parts[p][i4]
                        parts[p][i4] = value if old is None else jnp.where(group == g, value, old)
        for i4 in range(4):
            zr[i4 * 8 : (i4 + 1) * 8, tile * 128 : (tile + 1) * 128] = parts[0][i4]
            zi[i4 * 8 : (i4 + 1) * 8, tile * 128 : (tile + 1) * 128] = parts[1][i4]
    d_high, d_low = split(table[pl.ds(pl.multiple_of(q * 128, 128), 128), :])

    def apply(z):
        high, low = split(z)
        dot = functools.partial(jnp.dot, preferred_element_type=f32)
        return dot(d_high, high) + (dot(d_high, low) + dot(d_low, high))

    t_re, t_im = apply(zr[...]), apply(zi[...])

    def lanes_of(values):
        tiles = []
        one = lax.broadcasted_iota(jnp.int32, (1, 128), 1) // 32
        for tile in range(5):
            v = jnp.full((1, 128), values[tile * 4], jnp.int32)
            for g in range(1, 4):
                v = jnp.where(one == g, values[tile * 4 + g], v)
            tiles.append(v)
        return jnp.concatenate(tiles, axis=1)

    rows = q * 128 - 256 + lax.broadcasted_iota(jnp.int32, (128, 640), 0)
    turns = jnp.bitwise_and(rows * (2 * lanes_of(corner_u) - 481), 1023)
    p_re, p_im = sincos(turns.astype(f32) * (1.0 / 1024.0))
    l_re = t_re * p_re - t_im * p_im
    l_im = t_re * p_im + t_im * p_re
    columns = lax.broadcasted_iota(jnp.int32, (1, G), 1) - 256
    for k in range(2 * BPC):
        turns = jnp.bitwise_and(columns * (2 * corner_v[k] - 481), 1023)
        c, s = sincos(turns.astype(f32) * (1.0 / 1024.0))
        br[k * 32 : (k + 1) * 32, :] = table_t[...] * c
        bi[k * 32 : (k + 1) * 32, :] = table_t[...] * -s

    def product(a, b):
        ah, al = split(a)
        bh, bl = split(b)
        dot = functools.partial(jnp.dot, preferred_element_type=f32)
        return dot(ah, bh) + (dot(ah, bl) + dot(al, bh))

    out[0] = product(l_re, br[...]) + product(l_im, bi[...])


def image(owners, corners, assign, counts, got):
    d = image_table()
    scale = 1.0 / (SUB * SUB * math.sqrt(2 * BPC * BLK * CHANS))
    smem = pl.BlockSpec(memory_space=pltpu.SMEM)
    vmem = pl.BlockSpec(memory_space=pltpu.VMEM)
    return pl.pallas_call(
        image_kernel,
        out_shape=jax.ShapeDtypeStruct((1, G // N_FREQ, G), f32),
        in_specs=[smem] * 4 + [vmem] * 3,
        out_specs=vmem,
        scratch_shapes=[
            pltpu.SMEM((2 * BPC,), f32),
            pltpu.VMEM((32, 640), f32),
            pltpu.VMEM((32, 640), f32),
            pltpu.VMEM((640, G), f32),
            pltpu.VMEM((640, G), f32),
        ],
        name="make_image",
    )(
        owners,
        corners,
        assign,
        counts,
        got.reshape(N_FREQ * SLOTS, 16, 128),
        jnp.asarray(d * scale, f32),
        jnp.asarray(d.T, f32),
    )


def on_device(visibilities, coords, corners, owners, assign, counts):
    cand_vis, cand_coord = exchange(visibilities, coords)
    res = units(owners, corners, cand_vis, cand_coord)
    got = collect(res)
    return image(owners, corners, assign, counts, got)


def solution(mesh):
    placed = (
        P("facet", None, None, "freq", None),
        P("facet", None, None, None),
        P(),
        P(),
        P("facet", None),
        P("facet"),
    )
    return jax.shard_map(
        on_device, mesh=mesh, in_specs=placed, out_specs=P("facet", "freq", None), check_vma=False
    )
```

```python
import functools
import math

import jax
import jax.numpy as jnp
import numpy as np
from jax import lax
from jax.experimental import pallas as pl
from jax.experimental.pallas import tpu as pltpu
from jax.sharding import PartitionSpec as P

SUB = 32
G = 512
BPC = 10
CH = 32
N_FACET = 32
N_FREQ = 4
BLK = 128
CHANS = CH * N_FREQ
CHUNK = 8
MESH = pl.DeviceIdType.MESH
f32 = jnp.float32
bf16 = jnp.bfloat16

DELTA = (
    (0, 0, 0),
    (1, 0, 0),
    (3, 0, 0),
    (0, 0, 1),
    (0, 0, 3),
    (1, 0, 1),
    (1, 0, 3),
    (3, 0, 1),
    (3, 0, 3),
    (0, 1, 0),
)
LAST = N_FACET - 1
SLOTS = 11


def fit_sincos():
    s = 0.125 * (1.0 - np.cos(np.pi * (np.arange(400) + 0.5) / 400))
    t = np.sqrt(s)
    poly = np.polynomial.chebyshev
    domain = [0.0, 0.25]
    c = poly.Chebyshev.fit(s, np.cos(2 * np.pi * t), 7, domain=domain)
    n = poly.Chebyshev.fit(s, np.sin(2 * np.pi * t) / t, 7, domain=domain)
    to_power = lambda p: p.convert(kind=np.polynomial.Polynomial).coef
    return [float(v) for v in to_power(c)], [float(v) for v in to_power(n)]


COS_POLY, SIN_POLY = fit_sincos()


def sincos(cycles):
    t = cycles - jnp.floor(cycles + 0.5)
    s = t * t
    c = jnp.full_like(s, COS_POLY[-1])
    for k in COS_POLY[-2::-1]:
        c = c * s + k
    n = jnp.full_like(s, SIN_POLY[-1])
    for k in SIN_POLY[-2::-1]:
        n = n * s + k
    return c, n * t


def cmul(a, b):
    return a[0] * b[0] - a[1] * b[1], a[0] * b[1] + a[1] * b[0]


def both(a, b):
    rr, ii, ri, ir = a[0] * b[0], a[1] * b[1], a[0] * b[1], a[1] * b[0]
    return (rr - ii, ri + ir), (rr + ii, ir - ri)


def image_table():
    x = np.arange(G) - G // 2
    l = np.arange(SUB) - SUB // 2
    n = np.arange(SUB) - SUB // 2
    theta = x[:, None] / G - l[None, :] / SUB
    kernel = np.exp(2j * np.pi * n[None, None, :] * theta[:, :, None]).sum(axis=2)
    real = (kernel * np.exp(1j * np.pi * theta)).real
    real = real * (1.0 - 0.8 * (l / (SUB / 2.0)) ** 2)[None, :]
    upper, lower = real[:, SUB // 2 :], real[:, SUB // 2 - 1 :: -1]
    return np.concatenate([upper + lower, upper - lower], axis=1)


def shifted(f, delta, sign):
    z, y, x = f // 8, (f // 4) % 2, f % 4
    z = (z + (delta[0] if sign > 0 else 4 - delta[0])) % 4
    y = (y + delta[1]) % 2
    x = (x + (delta[2] if sign > 0 else 4 - delta[2])) % 4
    return z * 8 + y * 4 + x


def shifted_int(f, delta):
    return ((f // 8 + delta[0]) % 4) * 8 + ((f // 4 % 2 + delta[1]) % 2) * 4 + (f % 4 + delta[2]) % 4


LAST_POS = tuple(shifted_int(LAST, d) for d in DELTA)


def exchange_kernel(vis, coord, cand_vis, cand_coord, send_sem, recv_sem):
    f = lax.axis_index("facet")
    q = lax.axis_index("freq")
    barrier = pltpu.get_barrier_semaphore()
    for j in range(1, BPC):
        pl.semaphore_signal(
            barrier, inc=1, device_id=(shifted(f, DELTA[j], -1), q), device_id_type=MESH
        )
    own = [
        pltpu.make_async_copy(vis.at[0, 0], cand_vis.at[0], recv_sem.at[0, 0]),
        pltpu.make_async_copy(coord.at[0, 0], cand_coord.at[0], recv_sem.at[0, 1]),
    ]
    for c in own:
        c.start()
    pl.semaphore_wait(barrier, BPC - 1)
    copies = []
    for j in range(BPC - 1, 0, -1):
        to = (shifted(f, DELTA[j], 1), q)
        for n, (src, dst) in enumerate(((vis, cand_vis), (coord, cand_coord))):
            copies.append(
                pltpu.make_async_remote_copy(
                    src_ref=src.at[0, j],
                    dst_ref=dst.at[j],
                    send_sem=send_sem.at[j, n],
                    recv_sem=recv_sem.at[j, n],
                    device_id=to,
                    device_id_type=MESH,
                )
            )
            copies[-1].start()
    for c in own:
        c.wait()
    for c in copies:
        c.wait()


def exchange(vis, coord):
    return pl.pallas_call(
        exchange_kernel,
        out_shape=(
            jax.ShapeDtypeStruct((BPC, 2, CH, BLK), f32),
            jax.ShapeDtypeStruct((BPC, 3, BLK), f32),
        ),
        in_specs=[pl.BlockSpec(memory_space=pl.ANY)] * 2,
        out_specs=[pl.BlockSpec(memory_space=pl.ANY)] * 2,
        scratch_shapes=[
            pltpu.SemaphoreType.DMA((BPC, 2)),
            pltpu.SemaphoreType.DMA((BPC, 2)),
        ],
        compiler_params=pltpu.CompilerParams(collective_id=0, has_side_effects=True),
        name="exchange_blocks",
    )(vis, coord)


def unit_products(q, vis, coord, ou, ov, xrow, pbuf, vbuf, acc):
    step = 0.02 / CHANS
    start = 1.0 + (step * CH) * q.astype(f32)
    u, v, w = coord[0:1, :], coord[1:2, :], coord[2:3, :]
    ou = 240.5 - ou.astype(f32)
    ov = 240.5 - ov.astype(f32)
    row = lax.broadcasted_iota(jnp.int32, (8, BLK), 0).astype(f32)
    waves, turns = [], []
    for d, corner in ((u, ou), (v, ov)):
        for h in range(2):
            m = (2.0 * row + (16.0 * h + 1.0)) * (1.0 / 64.0)
            waves.append(sincos((d * start + corner) * m))
            turns.append(sincos((d * step) * m))
    a = row - 3.5
    spins, spin_turns = [], []
    for g in range(4):
        e = g - 1.5
        rho = 0.0004 * (a * a + e * e)
        shift = -rho / (1.0 + jnp.sqrt(1.0 - rho))
        cycles = u * a + v * e + w * shift - (u + v) * (1.0 / 64.0)
        spins.append(sincos(cycles * start - (ou + ov) * (1.0 / 64.0)))
        spin_turns.append(sincos(cycles * step))

    def generate(c, slot, cc):
        x0, x1, y0, y1 = waves
        for h, part in enumerate((x0[0], x1[0], x0[1], x1[1])):
            xrow[slot, cc, 8 * h : 8 * h + 8, :] = part
        y = (y0[0], y1[0], y0[1], y1[1])
        for i in range(32):
            x = jnp.broadcast_to(xrow[slot, cc, i : i + 1, :], (8, BLK))
            at = (i % 8) * 128 + (i // 8) * 32
            for h in range(2):
                pair = jnp.concatenate([x * y[2 * h], x * y[2 * h + 1]], axis=0)
                pbuf[slot, cc, at + 16 * h : at + 16 * h + 16, :] = pair.astype(bf16)
        re = jnp.broadcast_to(vis[0, c : c + 1, :], (8, BLK))
        im = jnp.broadcast_to(vis[1, c : c + 1, :], (8, BLK))
        rotated = [cmul((re, im), s) for s in spins]
        for part in range(2):
            for h in range(2):
                pair = jnp.concatenate([rotated[2 * h][part], rotated[2 * h + 1][part]], axis=0)
                high = pair.astype(bf16)
                low = (pair - high.astype(f32)).astype(bf16)
                at = part * 32 + h * 16
                vbuf[slot, cc, at : at + 16, :] = high
                vbuf[slot, cc, 64 + at : 64 + at + 16, :] = low
        for n in range(4):
            waves[n] = cmul(waves[n], turns[n])
            spins[n] = cmul(spins[n], spin_turns[n])

    def multiply(k, slot, n):
        columns = slice(n * 256, (n + 1) * 256)
        left = jnp.concatenate([vbuf[slot, cc] for cc in range(CHUNK)], axis=1)
        right = jnp.concatenate([pbuf[slot, cc, columns, :] for cc in range(CHUNK)], axis=1)
        part = lax.dot_general(
            left, right, (((1,), (1,)), ((), ())), preferred_element_type=f32
        )
        if k == 0:
            acc[:, columns] = part
        else:
            acc[:, columns] = acc[:, columns] + part

    chunks = CH // CHUNK
    for k in range(chunks + 1):
        for cc in range(CHUNK):
            if k < chunks:
                generate(k * CHUNK + cc, k % 2, cc)
            if k > 0 and cc % (CHUNK // 4) == 0:
                multiply(k - 1, (k - 1) % 2, cc // (CHUNK // 4))


def place_results(acc, turned, put):
    for n in range(8):
        lanes = slice(n * 128, (n + 1) * 128)
        turned[n * 64 : (n + 1) * 64, :] = acc[:64, lanes] + acc[64:, lanes]
    for part in range(2):
        for facet in range(N_FACET):
            put(facet, part, turned[pl.ds(part * 32 + facet, 8, stride=64), :])


def units_kernel(
    owners, corners, cand_vis, cand_coord, out, vis, coord, xrow, pbuf, vbuf, acc, turned, sem
):
    f = lax.axis_index("facet")
    q = lax.axis_index("freq")

    def unit(n, carry):
        owner = jnp.where(
            n == 1, LAST, jnp.where(owners[0] == LAST, owners[1], owners[0])
        ).astype(jnp.int32)
        block = jnp.int32(-1)
        for j in range(BPC):
            block = jnp.where(shifted(f, DELTA[j], -1) == owner, j, block)

        @pl.when(block >= 0)
        def _():
            copies = [
                pltpu.make_async_copy(cand_vis.at[block], vis, sem.at[0]),
                pltpu.make_async_copy(cand_coord.at[block], coord, sem.at[1]),
            ]
            for c in copies:
                c.start()
            for c in copies:
                c.wait()
            unit_products(
                q, vis, coord, corners[0, owner, block], corners[1, owner, block], xrow, pbuf, vbuf, acc
            )

            def put(facet, part, value):
                out[n, facet, part * 8 : (part + 1) * 8, :] = value

            place_results(acc, turned, put)

        return carry

    lax.fori_loop(0, 2, unit, 0)


def unit_scratch():
    return [
        pltpu.VMEM((2, CHUNK, 32, BLK), f32),
        pltpu.VMEM((2, CHUNK, 1024, BLK), bf16),
        pltpu.VMEM((2, CHUNK, 128, BLK), bf16),
        pltpu.VMEM((128, 1024), f32),
        pltpu.VMEM((512, 128), f32),
    ]


def units(owners, corners, cand_vis, cand_coord):
    return pl.pallas_call(
        units_kernel,
        out_shape=jax.ShapeDtypeStruct((2, N_FACET, 16, 128), f32),
        in_specs=[pl.BlockSpec(memory_space=pltpu.SMEM)] * 2
        + [pl.BlockSpec(memory_space=pl.ANY)] * 2,
        out_specs=pl.BlockSpec(memory_space=pltpu.VMEM),
        scratch_shapes=[pltpu.VMEM((2, CH, BLK), f32), pltpu.VMEM((3, BLK), f32)]
        + unit_scratch()
        + [pltpu.SemaphoreType.DMA((2,))],
        name="grid_blocks",
    )(owners, corners, cand_vis, cand_coord)


def collect_kernel(res, out, from_a, from_b, total, send_sem, recv_a, recv_b, peer_send, peer_recv):
    f = lax.axis_index("facet")
    q = lax.axis_index("freq")
    x = f % 4
    last_block = jnp.int32(-1)
    for j in range(BPC):
        last_block = jnp.where(f == LAST_POS[j], j, last_block)
    is_last = last_block >= 0
    q_last = last_block % 4
    barrier = pltpu.get_barrier_semaphore()

    def signal(facet, freq):
        pl.semaphore_signal(barrier, inc=1, device_id=(facet, freq), device_id_type=MESH)

    def tell_a(n, carry):
        facet, freq = (n // 4) * 4 + q, n % 4

        @pl.when(jnp.logical_or(facet != f, freq != q))
        def _():
            signal(facet, freq)

        return carry

    lax.fori_loop(0, 32, tell_a, 0)
    for j in range(BPC):
        for freq in range(N_FREQ):

            @pl.when(
                jnp.logical_and(j % 4 == q, jnp.logical_or(f != LAST_POS[j], freq != q))
            )
            def _():
                signal(LAST_POS[j], freq)

    for d in range(1, N_FREQ):
        signal(f, (q + d) % N_FREQ)
    expected = 32 + 3 - jnp.where(x == q, 1, 0)
    expected = expected + jnp.where(is_last, 32 - jnp.where(q_last == q, 1, 0), 0)
    pl.semaphore_wait(barrier, expected)

    def copy_a(facet):
        return pltpu.make_async_remote_copy(
            src_ref=res.at[0, facet],
            dst_ref=from_a.at[f // 4, q],
            send_sem=send_sem.at[0, facet],
            recv_sem=recv_a.at[f // 4, q],
            device_id=(facet, x),
            device_id_type=MESH,
        )

    def copy_b(facet):
        return pltpu.make_async_remote_copy(
            src_ref=res.at[1, facet],
            dst_ref=from_b.at[last_block // 4, q],
            send_sem=send_sem.at[1, facet],
            recv_sem=recv_b.at[last_block // 4, q],
            device_id=(facet, q_last),
            device_id_type=MESH,
        )

    own_a = pltpu.make_async_copy(res.at[0, f], from_a.at[f // 4, q], recv_a.at[f // 4, q])
    own_b = pltpu.make_async_copy(
        res.at[1, f], from_b.at[last_block // 4, q], recv_b.at[last_block // 4, q]
    )

    def send_all(copy, own, to):
        def step(n, carry):
            facet = (f + n) % N_FACET
            here = jnp.logical_and(facet == f, to == q)

            @pl.when(jnp.logical_not(here))
            def _():
                copy(facet).start()

            @pl.when(here)
            def _():
                own.start()

            return carry

        lax.fori_loop(0, N_FACET, step, 0)

    def drain(copy, to):
        def step(facet, carry):
            @pl.when(jnp.logical_not(jnp.logical_and(facet == f, to == q)))
            def _():
                copy(facet).wait_send()

            return carry

        lax.fori_loop(0, N_FACET, step, 0)

    @pl.when(is_last)
    def _():
        send_all(copy_b, own_b, q_last)

    send_all(copy_a, own_a, x)

    def add_a(s, carry):
        for p in range(N_FREQ):
            pltpu.make_async_copy(from_a.at[s, p], from_a.at[s, p], recv_a.at[s, p]).wait()
        total[s] = (from_a[s, 0] + from_a[s, 1]) + (from_a[s, 2] + from_a[s, 3])
        return carry

    lax.fori_loop(0, 8, add_a, 0)
    for s in range(3):

        @pl.when(q + 4 * s < BPC)
        def _():
            for p in range(N_FREQ):
                pltpu.make_async_copy(from_b.at[s, p], from_b.at[s, p], recv_b.at[s, p]).wait()
            total[8 + s] = (from_b[s, 0] + from_b[s, 1]) + (from_b[s, 2] + from_b[s, 3])

    peers = []
    for d in range(1, N_FREQ):
        peers.append(
            pltpu.make_async_remote_copy(
                src_ref=total,
                dst_ref=out.at[q],
                send_sem=peer_send.at[d],
                recv_sem=peer_recv.at[d],
                device_id=(f, (q + d) % N_FREQ),
                device_id_type=MESH,
            )
        )
        peers[-1].start()
    mine = pltpu.make_async_copy(total, out.at[q], peer_send.at[0])
    mine.start()
    mine.wait()
    for d in range(1, N_FREQ):
        source = (q + N_FREQ - d) % N_FREQ
        pltpu.make_async_copy(total, out.at[source], peer_recv.at[d]).wait()
    for p in peers:
        p.wait_send()
    drain(copy_a, x)

    @pl.when(is_last)
    def _():
        drain(copy_b, q_last)


def collect(res):
    return pl.pallas_call(
        collect_kernel,
        out_shape=jax.ShapeDtypeStruct((N_FREQ, SLOTS, 16, 128), f32),
        in_specs=[pl.BlockSpec(memory_space=pl.ANY)],
        out_specs=pl.BlockSpec(memory_space=pl.ANY),
        scratch_shapes=[
            pltpu.VMEM((8, N_FREQ, 16, 128), f32),
            pltpu.VMEM((3, N_FREQ, 16, 128), f32),
            pltpu.VMEM((SLOTS, 16, 128), f32),
            pltpu.SemaphoreType.DMA((2, N_FACET)),
            pltpu.SemaphoreType.DMA((8, N_FREQ)),
            pltpu.SemaphoreType.DMA((3, N_FREQ)),
            pltpu.SemaphoreType.DMA((N_FREQ,)),
            pltpu.SemaphoreType.DMA((N_FREQ,)),
        ],
        compiler_params=pltpu.CompilerParams(collective_id=1, has_side_effects=True),
        name="collect_results",
    )(res)


def split(a):
    high = a.astype(bf16)
    return high, (a - high.astype(f32)).astype(bf16)


def image_kernel(
    owners, corners, assign, counts, got, table, table_t, out, weight, zr, zi, br, bi
):
    q = lax.axis_index("freq")
    lane = lax.broadcasted_iota(jnp.int32, (8, 128), 1)
    first_last = owners[0] == LAST
    other = jnp.where(first_last, owners[1], owners[0]).astype(jnp.int32)
    for b in range(2 * BPC):
        weight[b] = 0.0
    count = counts[0]
    for n in range(2 * BPC):
        weight[assign[0, n]] = jnp.where(n < count, 1.0, 0.0).astype(f32)
    corner_u, corner_v, weights, places = [], [], [], []
    for k in range(2 * BPC):
        j = k % BPC
        if k < BPC:
            owner = jnp.int32(LAST)
            places.append(jnp.int32((j % 4) * SLOTS + 8 + j // 4))
            base = jnp.where(first_last, 0, BPC)
        else:
            owner = other
            t = shifted(other, DELTA[j], 1)
            places.append((t % 4) * SLOTS + t // 4)
            base = jnp.where(first_last, BPC, 0)
        corner_u.append(corners[0, owner, j])
        corner_v.append(corners[1, owner, j])
        weights.append(weight[base + j])
    sine_lane = lane % 32 >= 16
    group = lane // 32
    for tile in range(5):
        parts = [[None] * 4, [None] * 4]
        for g in range(4):
            k = tile * 4 + g
            block = got[places[k]]
            re, im = block[:8] * weights[k], block[8:] * weights[k]
            for half in range(2):
                if half == 0:
                    new_re = jnp.where(sine_lane, -im, re)
                    new_im = jnp.where(sine_lane, re, im)
                else:
                    new_re = jnp.where(sine_lane, -re, -im)
                    new_im = jnp.where(sine_lane, -im, re)
                for i4 in (2 * half, 2 * half + 1):
                    shift = ((g - i4) * 32) % 128
                    for p, value in enumerate((new_re, new_im)):
                        if shift:
                            value = pltpu.roll(value, shift, 1)
                        old = parts[p][i4]
                        parts[p][i4] = value if old is None else jnp.where(group == g, value, old)
        for i4 in range(4):
            zr[i4 * 8 : (i4 + 1) * 8, tile * 128 : (tile + 1) * 128] = parts[0][i4]
            zi[i4 * 8 : (i4 + 1) * 8, tile * 128 : (tile + 1) * 128] = parts[1][i4]
    d_high, d_low = split(table[pl.ds(pl.multiple_of(q * 128, 128), 128), :])

    def apply(z):
        high, low = split(z)
        dot = functools.partial(jnp.dot, preferred_element_type=f32)
        return dot(d_high, high) + (dot(d_high, low) + dot(d_low, high))

    t_re, t_im = apply(zr[...]), apply(zi[...])

    def lanes_of(values):
        tiles = []
        one = lax.broadcasted_iota(jnp.int32, (1, 128), 1) // 32
        for tile in range(5):
            v = jnp.full((1, 128), values[tile * 4], jnp.int32)
            for g in range(1, 4):
                v = jnp.where(one == g, values[tile * 4 + g], v)
            tiles.append(v)
        return jnp.concatenate(tiles, axis=1)

    rows = q * 128 - 256 + lax.broadcasted_iota(jnp.int32, (128, 640), 0)
    turns = jnp.bitwise_and(rows * (2 * lanes_of(corner_u) - 481), 1023)
    p_re, p_im = sincos(turns.astype(f32) * (1.0 / 1024.0))
    l_re = t_re * p_re - t_im * p_im
    l_im = t_re * p_im + t_im * p_re
    columns = lax.broadcasted_iota(jnp.int32, (1, G), 1) - 256
    for k in range(2 * BPC):
        turns = jnp.bitwise_and(columns * (2 * corner_v[k] - 481), 1023)
        c, s = sincos(turns.astype(f32) * (1.0 / 1024.0))
        br[k * 32 : (k + 1) * 32, :] = table_t[...] * c
        bi[k * 32 : (k + 1) * 32, :] = table_t[...] * -s

    def product(a, b):
        ah, al = split(a)
        bh, bl = split(b)
        dot = functools.partial(jnp.dot, preferred_element_type=f32)
        return dot(ah, bh) + (dot(ah, bl) + dot(al, bh))

    out[0] = product(l_re, br[...]) + product(l_im, bi[...])


def image(owners, corners, assign, counts, got):
    d = image_table()
    scale = 1.0 / (SUB * SUB * math.sqrt(2 * BPC * BLK * CHANS))
    smem = pl.BlockSpec(memory_space=pltpu.SMEM)
    vmem = pl.BlockSpec(memory_space=pltpu.VMEM)
    return pl.pallas_call(
        image_kernel,
        out_shape=jax.ShapeDtypeStruct((1, G // N_FREQ, G), f32),
        in_specs=[smem] * 4 + [vmem] * 3,
        out_specs=vmem,
        scratch_shapes=[
            pltpu.SMEM((2 * BPC,), f32),
            pltpu.VMEM((32, 640), f32),
            pltpu.VMEM((32, 640), f32),
            pltpu.VMEM((640, G), f32),
            pltpu.VMEM((640, G), f32),
        ],
        name="make_image",
    )(
        owners,
        corners,
        assign,
        counts,
        got.reshape(N_FREQ * SLOTS, 16, 128),
        jnp.asarray(d * scale, f32),
        jnp.asarray(d.T, f32),
    )


def on_device(visibilities, coords, corners, owners, assign, counts):
    cand_vis, cand_coord = exchange(visibilities, coords)
    res = units(owners, corners, cand_vis, cand_coord)
    got = collect(res)
    return image(owners, corners, assign, counts, got)


def solution(mesh):
    placed = (
        P("facet", None, None, "freq", None),
        P("facet", None, None, None),
        P(),
        P(),
        P("facet", None),
        P("facet"),
    )
    return jax.shard_map(
        on_device, mesh=mesh, in_specs=placed, out_specs=P("facet", "freq", None), check_vma=False
    )
```

```python
import functools
import math

import jax
import jax.numpy as jnp
import numpy as np
from jax import lax
from jax.experimental import pallas as pl
from jax.experimental.pallas import tpu as pltpu
from jax.sharding import PartitionSpec as P

SUB = 32
G = 512
BPC = 10
CH = 32
N_FACET = 32
N_FREQ = 4
BLK = 128
CHANS = CH * N_FREQ
CHUNK = 8
LO = True
MESH = pl.DeviceIdType.MESH
f32 = jnp.float32
bf16 = jnp.bfloat16

DELTA = (
    (0, 0, 0),
    (1, 0, 0),
    (3, 0, 0),
    (0, 0, 1),
    (0, 0, 3),
    (1, 0, 1),
    (1, 0, 3),
    (3, 0, 1),
    (3, 0, 3),
    (0, 1, 0),
)
LAST = N_FACET - 1
PER_SET = 3
SLOTS = 2 * PER_SET


def fit_sincos():
    s = 0.125 * (1.0 - np.cos(np.pi * (np.arange(400) + 0.5) / 400))
    t = np.sqrt(s)
    poly = np.polynomial.chebyshev
    domain = [0.0, 0.25]
    c = poly.Chebyshev.fit(s, np.cos(2 * np.pi * t), 7, domain=domain)
    n = poly.Chebyshev.fit(s, np.sin(2 * np.pi * t) / t, 7, domain=domain)
    to_power = lambda p: p.convert(kind=np.polynomial.Polynomial).coef
    return [float(v) for v in to_power(c)], [float(v) for v in to_power(n)]


COS_POLY, SIN_POLY = fit_sincos()


def sincos(cycles):
    t = cycles - jnp.floor(cycles + 0.5)
    s = t * t
    c = jnp.full_like(s, COS_POLY[-1])
    for k in COS_POLY[-2::-1]:
        c = c * s + k
    n = jnp.full_like(s, SIN_POLY[-1])
    for k in SIN_POLY[-2::-1]:
        n = n * s + k
    return c, n * t


def cmul(a, b):
    return a[0] * b[0] - a[1] * b[1], a[0] * b[1] + a[1] * b[0]


def both(a, b):
    rr, ii, ri, ir = a[0] * b[0], a[1] * b[1], a[0] * b[1], a[1] * b[0]
    return (rr - ii, ri + ir), (rr + ii, ir - ri)


def image_table():
    x = np.arange(G) - G // 2
    l = np.arange(SUB) - SUB // 2
    n = np.arange(SUB) - SUB // 2
    theta = x[:, None] / G - l[None, :] / SUB
    kernel = np.exp(2j * np.pi * n[None, None, :] * theta[:, :, None]).sum(axis=2)
    real = (kernel * np.exp(1j * np.pi * theta)).real
    real = real * (1.0 - 0.8 * (l / (SUB / 2.0)) ** 2)[None, :]
    upper, lower = real[:, SUB // 2 :], real[:, SUB // 2 - 1 :: -1]
    even, odd = upper + lower, upper - lower
    plain = np.concatenate([even, odd], axis=1)
    table = np.zeros((G, SUB))
    for row in range(SUB):
        m, one, two, t = row // 8, (row // 4) % 2, (row // 2) % 2, row % 2
        for s1 in (1, -1):
            for s2 in (1, -1):
                place = int(8 + s1 * (4 + s2 * (m + 0.5)) - 0.5)
                sign = {
                    (0, 0, 0): 1, (0, 1, 1): -s2, (1, 0, 1): -s1 * s2, (1, 1, 0): -s1,
                    (1, 0, 0): 1, (1, 1, 1): -s2, (0, 1, 0): s1, (0, 0, 1): s1 * s2,
                }[(one, two, t)]
                table[:, row] += sign * ((odd if (one + two + t) % 2 else even)[:, place])
    return table, plain


def shifted(f, delta, sign):
    z, y, x = f // 8, (f // 4) % 2, f % 4
    z = (z + (delta[0] if sign > 0 else 4 - delta[0])) % 4
    y = (y + delta[1]) % 2
    x = (x + (delta[2] if sign > 0 else 4 - delta[2])) % 4
    return z * 8 + y * 4 + x


def shifted_int(f, delta):
    return ((f // 8 + delta[0]) % 4) * 8 + ((f // 4 % 2 + delta[1]) % 2) * 4 + (f % 4 + delta[2]) % 4


def group_of(z, y, x):
    return (z + x + 2 * y) % N_FREQ


def group_at(f):
    return group_of(f // 8, (f // 4) % 2, f % 4)


GROUP = tuple(group_of(*d) for d in DELTA)
MEMBERS = tuple(tuple(j for j in range(BPC) if GROUP[j] == g) for g in range(N_FREQ))
RANK = tuple(MEMBERS[GROUP[j]].index(j) for j in range(BPC))
LAST_POS = tuple(shifted_int(LAST, d) for d in DELTA)


def unit_products(q, block, cand_vis, cand_coord, ou, ov, xrow, pbuf, vbuf, acc):
    step = 0.02 / CHANS
    start = 1.0 + (step * CH) * q.astype(f32)
    coord = cand_coord[block]
    u, v, w = coord[0:1, :], coord[1:2, :], coord[2:3, :]
    ou = 240.5 - ou.astype(f32)
    ov = 240.5 - ov.astype(f32)
    row = lax.broadcasted_iota(jnp.int32, (32, BLK), 0)

    def wave(d, corner, m, back=0.0):
        return sincos((d * start + corner) * m - back), sincos((d * step) * m)

    row8 = row[:8]
    x, x_turn = wave(
        u, ou, (2 * (row8 % 4) + 1).astype(f32) * (1.0 / 64.0), (row8 // 4).astype(f32) * 0.25
    )
    y, y_turn = wave(v, ov, (2 * row[:16] + 1).astype(f32) * (1.0 / 64.0))
    half, half_turn = wave(u, ou, jnp.full((8, BLK), 0.125, f32))
    a = (row % 8).astype(f32) - 3.5
    e = (row // 8).astype(f32) - 1.5
    rho = 0.0004 * (a * a + e * e)
    shift = -rho / (1.0 + jnp.sqrt(1.0 - rho))
    cycles = u * a + v * e + w * shift - (u + v) * (1.0 / 64.0)
    spin = sincos(cycles * start - (ou + ov) * (1.0 / 64.0))
    spin_turn = sincos(cycles * step)
    state = [x, y, half, spin]
    turns = [x_turn, y_turn, half_turn, spin_turn]
    rows4 = lambda t: jnp.concatenate([t] * 4, axis=0)

    def generate(c, slot, cc):
        x, y, half, spin = state
        xrow[slot, cc] = x[0]
        ys = jnp.concatenate(y, axis=0)
        for r in range(8):
            pbuf[slot, cc, r * 32 : (r + 1) * 32, :] = (
                jnp.broadcast_to(xrow[slot, cc, r : r + 1, :], (32, BLK)) * ys
            ).astype(bf16)
        re = jnp.broadcast_to(cand_vis[block, 0, c : c + 1, :], (32, BLK))
        im = jnp.broadcast_to(cand_vis[block, 1, c : c + 1, :], (32, BLK))
        rotated = cmul((re, im), spin)
        c2, s2 = half
        c1, s1 = c2 * c2 - s2 * s2, 2.0 * (c2 * s2)
        for n, factor in enumerate((c1 * c2, c1 * s2, s1 * c2, s1 * s2)):
            factor = rows4(factor)
            for part in range(2):
                value = rotated[part] * factor
                high = value.astype(bf16)
                at = n * 64 + part * 32
                vbuf[slot, cc, at : at + 32, :] = high
                if LO:
                    vbuf[slot, cc, 256 + at : 288 + at, :] = (value - high.astype(f32)).astype(bf16)
        for n in range(4):
            state[n] = cmul(state[n], turns[n])

    def multiply(k, slot):
        left = jnp.concatenate([vbuf[slot, cc] for cc in range(CHUNK)], axis=1)
        right = jnp.concatenate([pbuf[slot, cc] for cc in range(CHUNK)], axis=1)
        part = lax.dot_general(
            left, right, (((1,), (1,)), ((), ())), preferred_element_type=f32
        )
        acc[...] = part if k == 0 else acc[...] + part

    chunks = CH // CHUNK
    for k in range(chunks + 1):
        for cc in range(CHUNK):
            if k < chunks:
                generate(k * CHUNK + cc, k % 2, cc)
        if k > 0:
            multiply(k - 1, (k - 1) % 2)


def place_results(acc, turned, put):
    for n in range(4):
        for h in range(2):
            rows, lanes = slice(n * 64, (n + 1) * 64), slice(h * 128, (h + 1) * 128)
            value = acc[rows, lanes]
            if LO:
                value = value + acc[256 + n * 64 : 320 + n * 64, lanes]
            turned[(2 * n + h) * 64 : (2 * n + h + 1) * 64, :] = value
    for part in range(2):
        for facet in range(N_FACET):
            put(facet, part, turned[pl.ds(part * 32 + facet, 8, stride=64), :])


def unit_scratch():
    rows = 512 if LO else 256
    return [
        pltpu.VMEM((2, CHUNK, 8, BLK), f32),
        pltpu.VMEM((2, CHUNK, 256, BLK), bf16),
        pltpu.VMEM((2, CHUNK, rows, BLK), bf16),
        pltpu.VMEM((rows, 256), f32),
        pltpu.VMEM((512, 128), f32),
    ]


def pick(index, values):
    out = jnp.int32(values[0])
    for n, v in enumerate(values):
        if n:
            out = jnp.where(index == n, v, out)
    return out


def split(a):
    high = a.astype(bf16)
    return high, (a - high.astype(f32)).astype(bf16)


def dot3(a, b):
    dot = functools.partial(jnp.dot, preferred_element_type=f32)
    return dot(a[0], b[0]) + (dot(a[0], b[1]) + dot(a[1], b[0]))


def lanes_of(values):
    group = lax.broadcasted_iota(jnp.int32, (1, 128), 1) // 32
    tiles = []
    for tile in range(5):
        v = jnp.full((1, 128), values[tile * 4], jnp.int32)
        for g in range(1, 4):
            v = jnp.where(group == g, values[tile * 4 + g], v)
        tiles.append(v)
    return jnp.concatenate(tiles, axis=1)


def prepare_image(q, owners, corners, assign, counts, other, table_t, pre, pim, br, bi):
    first_last = owners[0] == LAST
    corner_u = [corners[0, LAST, j] for j in range(BPC)] + [corners[0, other, j] for j in range(BPC)]
    corner_v = [corners[1, LAST, j] for j in range(BPC)] + [corners[1, other, j] for j in range(BPC)]
    k_of = lax.broadcasted_iota(jnp.int32, (1, 640), 1) // 32
    block = jnp.where(first_last, k_of, jnp.where(k_of < BPC, k_of + BPC, k_of - BPC))
    weight = jnp.zeros((1, 640), f32)
    count = counts[0]
    for n in range(2 * BPC):
        live = jnp.where(n < count, 1.0, 0.0).astype(f32)
        weight = weight + jnp.where(block == assign[0, n], live, 0.0)
    rows = q * 128 - 256 + lax.broadcasted_iota(jnp.int32, (128, 640), 0)
    turns = jnp.bitwise_and(rows * (2 * lanes_of(corner_u) - 481), 1023)
    c, s = sincos(turns.astype(f32) * (1.0 / 1024.0))
    pre[...] = c * weight
    pim[...] = s * weight
    columns = lax.broadcasted_iota(jnp.int32, (1, G), 1) - 256
    for k in range(2 * BPC):
        turns = jnp.bitwise_and(columns * (2 * corner_v[k] - 481), 1023)
        c, s = sincos(turns.astype(f32) * (1.0 / 1024.0))
        for ref, value in ((br, table_t[...] * c), (bi, table_t[...] * -s)):
            high, low = split(value)
            ref[0, k * 32 : (k + 1) * 32, :] = high
            ref[1, k * 32 : (k + 1) * 32, :] = low


def make_image(q, other, got, table, pre, pim, br, bi, zr, zi, out):
    lane = lax.broadcasted_iota(jnp.int32, (8, 128), 1)
    sub = lax.broadcasted_iota(jnp.int32, (8, 128), 0)
    row_sine = (sub // 4 + (sub // 2) % 2 + sub % 2) % 2 == 1
    lane_sine = lane % 32 >= 16
    two = jnp.logical_and(row_sine, lane_sine)
    one = jnp.logical_and(jnp.logical_or(row_sine, lane_sine), jnp.logical_not(two))
    group = lane // 32
    home = group_at(other)
    for tile in range(5):
        parts = [[None] * 4, [None] * 4]
        for g in range(4):
            k = tile * 4 + g
            j = k % BPC
            if k < BPC:
                block = got[(group_at(LAST) + GROUP[j]) % N_FREQ * SLOTS + PER_SET + RANK[j]]
            else:
                block = got[(home + GROUP[j]) % N_FREQ * SLOTS + RANK[j]]
            re, im = block[:8], block[8:]
            new_re = jnp.where(one, -im, jnp.where(two, -re, re))
            new_im = jnp.where(one, re, jnp.where(two, -im, im))
            for i4 in range(4):
                shift = ((g - i4) * 32) % 128
                for p, value in enumerate((new_re, new_im)):
                    if shift:
                        value = pltpu.roll(value, shift, 1)
                    old = parts[p][i4]
                    parts[p][i4] = value if old is None else jnp.where(group == g, value, old)
        for i4 in range(4):
            zr[i4 * 8 : (i4 + 1) * 8, tile * 128 : (tile + 1) * 128] = parts[0][i4]
            zi[i4 * 8 : (i4 + 1) * 8, tile * 128 : (tile + 1) * 128] = parts[1][i4]
    d = split(table[pl.ds(pl.multiple_of(q * 128, 128), 128), :])
    t_re, t_im = dot3(d, split(zr[...])), dot3(d, split(zi[...]))
    l_re = t_re * pre[...] - t_im * pim[...]
    l_im = t_re * pim[...] + t_im * pre[...]
    out[0] = dot3(split(l_re), (br[0], br[1])) + dot3(split(l_im), (bi[0], bi[1]))


def fused_kernel(
    vis, coord, owners, corners, assign, counts, table, table_t, out,
    cand_vis, cand_coord, xrow, pbuf, vbuf, acc, turned, res, from_a, from_b, total, got,
    pre, pim, br, bi, zr, zi,
    move_send, move_recv, send_sem, recv_a, recv_b, peer_send, peer_recv,
):
    f = lax.axis_index("facet")
    q = lax.axis_index("freq")
    group = group_at(f)
    last_block = jnp.int32(-1)
    for j in range(BPC):
        last_block = jnp.where(f == LAST_POS[j], j, last_block)
    is_last = last_block >= 0
    last_rank = pick(last_block, RANK)
    other = jnp.where(owners[0] == LAST, owners[1], owners[0]).astype(jnp.int32)
    barrier = pltpu.get_barrier_semaphore()

    def signal(facet, freq):
        pl.semaphore_signal(barrier, inc=1, device_id=(facet, freq), device_id_type=MESH)

    for j in range(1, BPC):
        signal(shifted(f, DELTA[j], -1), q)

    def tell(n, carry):
        z, y, freq = n // 8, (n // 4) % 2, n % 4
        facet = z * 8 + y * 4 + (q + 8 - z - 2 * y) % 4

        @pl.when(jnp.logical_or(facet != f, freq != q))
        def _():
            signal(facet, freq)

        return carry

    lax.fori_loop(0, 32, tell, 0)
    for j in range(BPC):
        facet = LAST_POS[j]

        @pl.when(group_at(facet) == q)
        def _():
            for freq in range(N_FREQ):

                @pl.when(jnp.logical_or(f != facet, freq != q))
                def _():
                    signal(facet, freq)

    for d in range(1, N_FREQ):
        signal(f, (q + d) % N_FREQ)
    mine = jnp.where(group == q, 1, 0)
    expected = 9 + 32 + 3 - mine + jnp.where(is_last, 32 - mine, 0)
    own = [
        pltpu.make_async_copy(vis.at[0, 0], cand_vis.at[0], move_recv.at[0, 0]),
        pltpu.make_async_copy(coord.at[0, 0], cand_coord.at[0], move_recv.at[0, 1]),
    ]
    for c in own:
        c.start()
    pl.semaphore_wait(barrier, expected)
    moves = []
    for j in range(BPC - 1, 0, -1):
        to = (shifted(f, DELTA[j], 1), q)
        for n, (src, dst) in enumerate(((vis, cand_vis), (coord, cand_coord))):
            moves.append(
                pltpu.make_async_remote_copy(
                    src_ref=src.at[0, j],
                    dst_ref=dst.at[j],
                    send_sem=move_send.at[j, n],
                    recv_sem=move_recv.at[j, n],
                    device_id=to,
                    device_id_type=MESH,
                )
            )
            moves[-1].start()
    for c in own:
        c.wait()
    for c in moves:
        c.wait_recv()

    place = f // 4

    def result_copy(n, facet):
        dst, sem, at = (from_a, recv_a, place) if n == 0 else (from_b, recv_b, last_rank)
        return pltpu.make_async_remote_copy(
            src_ref=res.at[n, facet],
            dst_ref=dst.at[at, q],
            send_sem=send_sem.at[n, facet],
            recv_sem=sem.at[at, q],
            device_id=(facet, group),
            device_id_type=MESH,
        )

    def own_copy(n):
        dst, sem, at = (from_a, recv_a, place) if n == 0 else (from_b, recv_b, last_rank)
        return pltpu.make_async_copy(res.at[n, f], dst.at[at, q], sem.at[at, q])

    def send_all(n):
        def step(d, carry):
            facet = (f + d) % N_FACET
            here = jnp.logical_and(facet == f, group == q)

            @pl.when(jnp.logical_not(here))
            def _():
                result_copy(n, facet).start()

            @pl.when(here)
            def _():
                own_copy(n).start()

            return carry

        lax.fori_loop(0, N_FACET, step, 0)

    def drain(n):
        def step(facet, carry):
            @pl.when(jnp.logical_not(jnp.logical_and(facet == f, group == q)))
            def _():
                result_copy(n, facet).wait_send()

            return carry

        lax.fori_loop(0, N_FACET, step, 0)

    def unit(n, carry):
        owner = jnp.where(n == 1, LAST, other)
        block = jnp.int32(0)
        for j in range(1, BPC):
            block = jnp.where(shifted(f, DELTA[j], -1) == owner, j, block)
        unit_products(
            q, block, cand_vis, cand_coord, corners[0, owner, block], corners[1, owner, block],
            xrow, pbuf, vbuf, acc,
        )

        def put(facet, part, value):
            res[n, facet, part * 8 : (part + 1) * 8, :] = value

        place_results(acc, turned, put)

        @pl.when(n == 0)
        def _():
            send_all(0)

        @pl.when(n == 1)
        def _():
            send_all(1)

        return carry

    lax.fori_loop(0, 1 + jnp.where(is_last, 1, 0), unit, 0)

    prepare_image(q, owners, corners, assign, counts, other, table_t, pre, pim, br, bi)

    def settle(sem, dst, s):
        for p in range(N_FREQ):
            pltpu.make_async_copy(dst.at[s, p], dst.at[s, p], sem.at[s, p]).wait()

    for s in range(8):
        settle(recv_a, from_a, s)
    wanted = (q + N_FREQ - group_at(other)) % N_FREQ
    for s in range(PER_SET):
        at = jnp.int32(0)
        for g in range(N_FREQ):
            j = MEMBERS[g][min(s, len(MEMBERS[g]) - 1)]
            at = jnp.where(wanted == g, shifted(other, DELTA[j], 1) // 4, at)
        total[s] = (from_a[at, 0] + from_a[at, 1]) + (from_a[at, 2] + from_a[at, 3])
    wanted = (q + N_FREQ - group_at(LAST)) % N_FREQ
    for s in range(PER_SET):
        present = pick(wanted, [int(s < len(m)) for m in MEMBERS]) == 1

        @pl.when(present)
        def _():
            settle(recv_b, from_b, s)
            total[PER_SET + s] = (from_b[s, 0] + from_b[s, 1]) + (from_b[s, 2] + from_b[s, 3])

        @pl.when(jnp.logical_not(present))
        def _():
            total[PER_SET + s] = jnp.zeros((16, 128), f32)

    peers = []
    for d in range(1, N_FREQ):
        peers.append(
            pltpu.make_async_remote_copy(
                src_ref=total,
                dst_ref=got.at[pl.ds(q * SLOTS, SLOTS)],
                send_sem=peer_send.at[d],
                recv_sem=peer_recv.at[d],
                device_id=(f, (q + d) % N_FREQ),
                device_id_type=MESH,
            )
        )
        peers[-1].start()
    keep = pltpu.make_async_copy(total, got.at[pl.ds(q * SLOTS, SLOTS)], peer_send.at[0])
    keep.start()
    keep.wait()
    for d in range(1, N_FREQ):
        source = (q + N_FREQ - d) % N_FREQ
        pltpu.make_async_copy(total, got.at[pl.ds(source * SLOTS, SLOTS)], peer_recv.at[d]).wait()
    make_image(q, other, got, table, pre, pim, br, bi, zr, zi, out)
    for c in moves:
        c.wait_send()
    for p in peers:
        p.wait_send()
    drain(0)

    @pl.when(is_last)
    def _():
        drain(1)


def on_device(visibilities, coords, corners, owners, assign, counts):
    d, _ = image_table()
    plain = image_table()[1]
    scale = 1.0 / (SUB * SUB * math.sqrt(2 * BPC * BLK * CHANS))
    smem = pl.BlockSpec(memory_space=pltpu.SMEM)
    vmem = pl.BlockSpec(memory_space=pltpu.VMEM)
    hbm = pl.BlockSpec(memory_space=pl.ANY)
    dma = pltpu.SemaphoreType.DMA
    return pl.pallas_call(
        fused_kernel,
        out_shape=jax.ShapeDtypeStruct((1, G // N_FREQ, G), f32),
        in_specs=[hbm, hbm] + [smem] * 4 + [vmem] * 2,
        out_specs=vmem,
        scratch_shapes=[
            pltpu.VMEM((BPC, 2, CH, BLK), f32),
            pltpu.VMEM((BPC, 3, BLK), f32),
        ]
        + unit_scratch()
        + [
            pltpu.VMEM((2, N_FACET, 16, 128), f32),
            pltpu.VMEM((8, N_FREQ, 16, 128), f32),
            pltpu.VMEM((PER_SET, N_FREQ, 16, 128), f32),
            pltpu.VMEM((SLOTS, 16, 128), f32),
            pltpu.VMEM((N_FREQ * SLOTS, 16, 128), f32),
            pltpu.VMEM((128, 640), f32),
            pltpu.VMEM((128, 640), f32),
            pltpu.VMEM((2, 640, G), bf16),
            pltpu.VMEM((2, 640, G), bf16),
            pltpu.VMEM((32, 640), f32),
            pltpu.VMEM((32, 640), f32),
            dma((BPC, 2)),
            dma((BPC, 2)),
            dma((2, N_FACET)),
            dma((8, N_FREQ)),
            dma((PER_SET, N_FREQ)),
            dma((N_FREQ,)),
            dma((N_FREQ,)),
        ],
        compiler_params=pltpu.CompilerParams(collective_id=0, has_side_effects=True),
        name="grid_and_image",
    )(
        visibilities,
        coords,
        owners,
        corners,
        assign,
        counts,
        jnp.asarray(d * scale, f32),
        jnp.asarray(plain.T, f32),
    )


def solution(mesh):
    placed = (
        P("facet", None, None, "freq", None),
        P("facet", None, None, None),
        P(),
        P(),
        P("facet", None),
        P("facet"),
    )
    return jax.shard_map(
        on_device, mesh=mesh, in_specs=placed, out_specs=P("facet", "freq", None), check_vma=False
    )
```

```python
import functools
import math

import jax
import jax.numpy as jnp
import numpy as np
from jax import lax
from jax.experimental import pallas as pl
from jax.experimental.pallas import tpu as pltpu
from jax.sharding import PartitionSpec as P

SUB = 32
G = 512
BPC = 10
CH = 32
N_FACET = 32
N_FREQ = 4
BLK = 128
CHANS = CH * N_FREQ
CHUNK = 8
LO = False
MESH = pl.DeviceIdType.MESH
f32 = jnp.float32
bf16 = jnp.bfloat16

DELTA = (
    (0, 0, 0),
    (1, 0, 0),
    (3, 0, 0),
    (0, 0, 1),
    (0, 0, 3),
    (1, 0, 1),
    (1, 0, 3),
    (3, 0, 1),
    (3, 0, 3),
    (0, 1, 0),
)
LAST = N_FACET - 1
PER_SET = 3
SLOTS = 2 * PER_SET


def fit_sincos():
    s = 0.125 * (1.0 - np.cos(np.pi * (np.arange(400) + 0.5) / 400))
    t = np.sqrt(s)
    poly = np.polynomial.chebyshev
    domain = [0.0, 0.25]
    c = poly.Chebyshev.fit(s, np.cos(2 * np.pi * t), 7, domain=domain)
    n = poly.Chebyshev.fit(s, np.sin(2 * np.pi * t) / t, 7, domain=domain)
    to_power = lambda p: p.convert(kind=np.polynomial.Polynomial).coef
    return [float(v) for v in to_power(c)], [float(v) for v in to_power(n)]


COS_POLY, SIN_POLY = fit_sincos()


def sincos(cycles):
    t = cycles - jnp.floor(cycles + 0.5)
    s = t * t
    c = jnp.full_like(s, COS_POLY[-1])
    for k in COS_POLY[-2::-1]:
        c = c * s + k
    n = jnp.full_like(s, SIN_POLY[-1])
    for k in SIN_POLY[-2::-1]:
        n = n * s + k
    return c, n * t


def cmul(a, b):
    return a[0] * b[0] - a[1] * b[1], a[0] * b[1] + a[1] * b[0]


def both(a, b):
    rr, ii, ri, ir = a[0] * b[0], a[1] * b[1], a[0] * b[1], a[1] * b[0]
    return (rr - ii, ri + ir), (rr + ii, ir - ri)


def image_table():
    x = np.arange(G) - G // 2
    l = np.arange(SUB) - SUB // 2
    n = np.arange(SUB) - SUB // 2
    theta = x[:, None] / G - l[None, :] / SUB
    kernel = np.exp(2j * np.pi * n[None, None, :] * theta[:, :, None]).sum(axis=2)
    real = (kernel * np.exp(1j * np.pi * theta)).real
    real = real * (1.0 - 0.8 * (l / (SUB / 2.0)) ** 2)[None, :]
    upper, lower = real[:, SUB // 2 :], real[:, SUB // 2 - 1 :: -1]
    even, odd = upper + lower, upper - lower
    plain = np.concatenate([even, odd], axis=1)
    table = np.zeros((G, SUB))
    for row in range(SUB):
        m, one, two, t = row // 8, (row // 4) % 2, (row // 2) % 2, row % 2
        for s1 in (1, -1):
            for s2 in (1, -1):
                place = int(8 + s1 * (4 + s2 * (m + 0.5)) - 0.5)
                sign = {
                    (0, 0, 0): 1, (0, 1, 1): -s2, (1, 0, 1): -s1 * s2, (1, 1, 0): -s1,
                    (1, 0, 0): 1, (1, 1, 1): -s2, (0, 1, 0): s1, (0, 0, 1): s1 * s2,
                }[(one, two, t)]
                table[:, row] += sign * ((odd if (one + two + t) % 2 else even)[:, place])
    return table, plain


def shifted(f, delta, sign):
    z, y, x = f // 8, (f // 4) % 2, f % 4
    z = (z + (delta[0] if sign > 0 else 4 - delta[0])) % 4
    y = (y + delta[1]) % 2
    x = (x + (delta[2] if sign > 0 else 4 - delta[2])) % 4
    return z * 8 + y * 4 + x


def shifted_int(f, delta):
    return ((f // 8 + delta[0]) % 4) * 8 + ((f // 4 % 2 + delta[1]) % 2) * 4 + (f % 4 + delta[2]) % 4


def group_of(z, y, x):
    return (z + x + 2 * y) % N_FREQ


def group_at(f):
    return group_of(f // 8, (f // 4) % 2, f % 4)


GROUP = tuple(group_of(*d) for d in DELTA)
MEMBERS = tuple(tuple(j for j in range(BPC) if GROUP[j] == g) for g in range(N_FREQ))
RANK = tuple(MEMBERS[GROUP[j]].index(j) for j in range(BPC))
def hops(delta):
    return min(delta[0], 4 - delta[0]) + 2 * delta[1] + min(delta[2], 4 - delta[2])


SEND_ORDER = tuple(
    sorted(
        ((n * 13 % 32 // 8, n * 13 % 32 // 4 % 2, n * 13 % 4) for n in range(1, N_FACET)),
        key=lambda d: -hops(d),
    )
)
LAST_POS = tuple(shifted_int(LAST, d) for d in DELTA)


def unit_products(q, block, cand_vis, cand_coord, ou, ov, xrow, pbuf, vbuf, acc):
    step = 0.02 / CHANS
    start = 1.0 + (step * CH) * q.astype(f32)
    u, v, w = cand_coord[3 * block], cand_coord[3 * block + 1], cand_coord[3 * block + 2]
    ou = 240.5 - ou.astype(f32)
    ov = 240.5 - ov.astype(f32)
    row = lax.broadcasted_iota(jnp.int32, (32, BLK), 0)

    def wave(d, corner, m, back=0.0):
        return sincos((d * start + corner) * m - back), sincos((d * step) * m)

    row8 = row[:8]
    x, x_turn = wave(
        u, ou, (2 * (row8 % 4) + 1).astype(f32) * (1.0 / 64.0), (row8 // 4).astype(f32) * 0.25
    )
    y, y_turn = wave(v, ov, (2 * row[:16] + 1).astype(f32) * (1.0 / 64.0))
    half, half_turn = wave(u, ou, jnp.full((8, BLK), 0.125, f32))
    a = (row % 8).astype(f32) - 3.5
    e = (row // 8).astype(f32) - 1.5
    rho = 0.0004 * (a * a + e * e)
    shift = -rho / (1.0 + jnp.sqrt(1.0 - rho))
    cycles = u * a + v * e + w * shift - (u + v) * (1.0 / 64.0)
    spin = sincos(cycles * start - (ou + ov) * (1.0 / 64.0))
    spin_turn = sincos(cycles * step)
    state = [x, y, half, spin]
    turns = [x_turn, y_turn, half_turn, spin_turn]
    rows4 = lambda t: jnp.concatenate([t] * 4, axis=0)

    def generate(c, slot, cc):
        x, y, half, spin = state
        xrow[slot, cc] = x[0]
        ys = jnp.concatenate(y, axis=0)
        for r in range(8):
            pbuf[slot, cc, r * 32 : (r + 1) * 32, :] = (
                jnp.broadcast_to(xrow[slot, cc, r : r + 1, :], (32, BLK)) * ys
            ).astype(bf16)
        re = jnp.broadcast_to(cand_vis[block, 0, c : c + 1, :], (32, BLK))
        im = jnp.broadcast_to(cand_vis[block, 1, c : c + 1, :], (32, BLK))
        rotated = cmul((re, im), spin)
        c2, s2 = half
        c1, s1 = c2 * c2 - s2 * s2, 2.0 * (c2 * s2)
        for n, factor in enumerate((c1 * c2, c1 * s2, s1 * c2, s1 * s2)):
            factor = rows4(factor)
            for part in range(2):
                value = rotated[part] * factor
                high = value.astype(bf16)
                at = n * 64 + part * 32
                vbuf[slot, cc, at : at + 32, :] = high
                if LO:
                    vbuf[slot, cc, 256 + at : 288 + at, :] = (value - high.astype(f32)).astype(bf16)
        for n in range(4):
            state[n] = cmul(state[n], turns[n])

    def multiply(k, slot):
        left = jnp.concatenate([vbuf[slot, cc] for cc in range(CHUNK)], axis=1)
        right = jnp.concatenate([pbuf[slot, cc] for cc in range(CHUNK)], axis=1)
        part = lax.dot_general(
            left, right, (((1,), (1,)), ((), ())), preferred_element_type=f32
        )
        acc[...] = part if k == 0 else acc[...] + part

    chunks = CH // CHUNK
    for k in range(chunks + 1):
        for cc in range(CHUNK):
            if k < chunks:
                generate(k * CHUNK + cc, k % 2, cc)
        if k > 0:
            multiply(k - 1, (k - 1) % 2)


def place_results(acc, turned, put):
    for n in range(4):
        for h in range(2):
            rows, lanes = slice(n * 64, (n + 1) * 64), slice(h * 128, (h + 1) * 128)
            value = acc[rows, lanes]
            if LO:
                value = value + acc[256 + n * 64 : 320 + n * 64, lanes]
            turned[(2 * n + h) * 64 : (2 * n + h + 1) * 64, :] = value
    for part in range(2):
        for facet in range(N_FACET):
            put(facet, part, turned[pl.ds(part * 32 + facet, 8, stride=64), :])


def unit_scratch():
    rows = 512 if LO else 256
    return [
        pltpu.VMEM((2, CHUNK, 8, BLK), f32),
        pltpu.VMEM((2, CHUNK, 256, BLK), bf16),
        pltpu.VMEM((2, CHUNK, rows, BLK), bf16),
        pltpu.VMEM((rows, 256), f32),
        pltpu.VMEM((512, 128), f32),
    ]


def pick(index, values):
    out = jnp.int32(values[0])
    for n, v in enumerate(values):
        if n:
            out = jnp.where(index == n, v, out)
    return out


def split(a):
    high = a.astype(bf16)
    return high, (a - high.astype(f32)).astype(bf16)


def dot3(a, b):
    dot = functools.partial(jnp.dot, preferred_element_type=f32)
    return dot(a[0], b[0]) + (dot(a[0], b[1]) + dot(a[1], b[0]))


def lanes_of(values):
    group = lax.broadcasted_iota(jnp.int32, (1, 128), 1) // 32
    tiles = []
    for tile in range(5):
        v = jnp.full((1, 128), values[tile * 4], jnp.int32)
        for g in range(1, 4):
            v = jnp.where(group == g, values[tile * 4 + g], v)
        tiles.append(v)
    return jnp.concatenate(tiles, axis=1)


def prepare_image(q, owners, corners, assign, counts, other, table_t, pre, pim, br, bi):
    first_last = owners[0] == LAST
    corner_u = [corners[j, 0, LAST] for j in range(BPC)] + [corners[j, 0, other] for j in range(BPC)]
    corner_v = [corners[j, 1, LAST] for j in range(BPC)] + [corners[j, 1, other] for j in range(BPC)]
    k_of = lax.broadcasted_iota(jnp.int32, (1, 640), 1) // 32
    block = jnp.where(first_last, k_of, jnp.where(k_of < BPC, k_of + BPC, k_of - BPC))
    weight = jnp.zeros((1, 640), f32)
    count = counts[0]
    for n in range(2 * BPC):
        live = jnp.where(n < count, 1.0, 0.0).astype(f32)
        weight = weight + jnp.where(block == assign[0, n], live, 0.0)
    rows = q * 128 - 256 + lax.broadcasted_iota(jnp.int32, (128, 640), 0)
    turns = jnp.bitwise_and(rows * (2 * lanes_of(corner_u) - 481), 1023)
    c, s = sincos(turns.astype(f32) * (1.0 / 1024.0))
    pre[...] = c * weight
    pim[...] = s * weight
    columns = lax.broadcasted_iota(jnp.int32, (1, G), 1) - 256
    for k in range(2 * BPC):
        turns = jnp.bitwise_and(columns * (2 * corner_v[k] - 481), 1023)
        c, s = sincos(turns.astype(f32) * (1.0 / 1024.0))
        for ref, value in ((br, table_t[...] * c), (bi, table_t[...] * -s)):
            high, low = split(value)
            ref[0, k * 32 : (k + 1) * 32, :] = high
            ref[1, k * 32 : (k + 1) * 32, :] = low


def make_image(q, other, got, table, pre, pim, br, bi, zr, zi, out):
    lane = lax.broadcasted_iota(jnp.int32, (8, 128), 1)
    sub = lax.broadcasted_iota(jnp.int32, (8, 128), 0)
    row_sine = (sub // 4 + (sub // 2) % 2 + sub % 2) % 2 == 1
    lane_sine = lane % 32 >= 16
    two = jnp.logical_and(row_sine, lane_sine)
    one = jnp.logical_and(jnp.logical_or(row_sine, lane_sine), jnp.logical_not(two))
    group = lane // 32
    home = group_at(other)
    for tile in range(5):
        parts = [[None] * 4, [None] * 4]
        for g in range(4):
            k = tile * 4 + g
            j = k % BPC
            if k < BPC:
                block = got[(group_at(LAST) + GROUP[j]) % N_FREQ * SLOTS + PER_SET + RANK[j]]
            else:
                block = got[(home + GROUP[j]) % N_FREQ * SLOTS + RANK[j]]
            re, im = block[:8], block[8:]
            new_re = jnp.where(one, -im, jnp.where(two, -re, re))
            new_im = jnp.where(one, re, jnp.where(two, -im, im))
            for i4 in range(4):
                shift = ((g - i4) * 32) % 128
                for p, value in enumerate((new_re, new_im)):
                    if shift:
                        value = pltpu.roll(value, shift, 1)
                    old = parts[p][i4]
                    parts[p][i4] = value if old is None else jnp.where(group == g, value, old)
        for i4 in range(4):
            zr[i4 * 8 : (i4 + 1) * 8, tile * 128 : (tile + 1) * 128] = parts[0][i4]
            zi[i4 * 8 : (i4 + 1) * 8, tile * 128 : (tile + 1) * 128] = parts[1][i4]
    d = table[pl.ds(pl.multiple_of(q * 128, 128), 128), :]

    def apply(z):
        high, low = split(z)
        return jnp.dot(
            d, jnp.concatenate([high, low, high], axis=0), preferred_element_type=f32
        )

    t_re, t_im = apply(zr[...]), apply(zi[...])
    l_re = t_re * pre[...] - t_im * pim[...]
    l_im = t_re * pim[...] + t_im * pre[...]
    out[0] = dot3(split(l_re), (br[0], br[1])) + dot3(split(l_im), (bi[0], bi[1]))


def fused_kernel(
    vis, coord, owners, corners, assign, counts, table, table_t, out,
    cand_vis, cand_coord, xrow, pbuf, vbuf, acc, turned, res, from_a, from_b, total, got,
    pre, pim, br, bi, zr, zi,
    plane_sem, near_sem, all_sem, move_send, move_recv, send_sem, recv_a, recv_b, peer_send, peer_recv,
):
    f = lax.axis_index("facet")
    q = lax.axis_index("freq")
    group = group_at(f)
    last_block = jnp.int32(-1)
    for j in range(BPC):
        last_block = jnp.where(f == LAST_POS[j], j, last_block)
    is_last = last_block >= 0
    last_rank = pick(last_block, RANK)
    other = jnp.where(owners[0] == LAST, owners[1], owners[0]).astype(jnp.int32)
    barrier = pltpu.get_barrier_semaphore()

    def signal(facet, freq):
        pl.semaphore_signal(barrier, inc=1, device_id=(facet, freq), device_id_type=MESH)

    def peers_of(n):
        return (f, (q + n) % N_FREQ)

    for j in range(1, BPC):
        signal(shifted(f, DELTA[j], -1), q)
    for n in range(1, N_FREQ):
        signal(*peers_of(n))

    def tell(sem, facet, freq):
        pl.semaphore_signal(sem, inc=1, device_id=(facet, freq), device_id_type=MESH)

    own = [
        pltpu.make_async_copy(vis.at[0, 0], cand_vis.at[0], move_recv.at[0, 0]),
        pltpu.make_async_copy(coord.at[pl.ds(0, 3)], cand_coord.at[pl.ds(0, 3)], move_recv.at[0, 1]),
    ]
    for c in own:
        c.start()
    pl.semaphore_wait(barrier, BPC - 1 + N_FREQ - 1)
    moves = []
    for j in range(BPC - 1, 0, -1):
        to = (shifted(f, DELTA[j], 1), q)
        rows = pl.ds(3 * j, 3)
        pairs = ((vis.at[0, j], cand_vis.at[j]), (coord.at[rows], cand_coord.at[rows]))
        for n, (src, dst) in enumerate(pairs):
            moves.append(
                pltpu.make_async_remote_copy(
                    src_ref=src,
                    dst_ref=dst,
                    send_sem=move_send.at[j, n],
                    recv_sem=move_recv.at[j, n],
                    device_id=to,
                    device_id_type=MESH,
                )
            )
            moves[-1].start()
    for delta in ((3, 0, 3), (3, 0, 1), (1, 0, 3)):
        tell(plane_sem, shifted(f, delta, 1), q)
    pl.semaphore_wait(plane_sem, 3)
    tell(near_sem, shifted(f, (0, 1, 0), 1), q)
    for n in range(1, N_FREQ):
        tell(near_sem, *peers_of(n))
    pl.semaphore_wait(near_sem, N_FREQ)
    for n in range(1, N_FREQ):
        tell(all_sem, *peers_of(n))
    for c in own:
        c.wait()
    for c in moves:
        c.wait_recv()

    place = f // 4

    def result_copy(n, facet):
        dst, sem, at = (from_a, recv_a, place) if n == 0 else (from_b, recv_b, last_rank)
        return pltpu.make_async_remote_copy(
            src_ref=res.at[n, facet],
            dst_ref=dst.at[at, q],
            send_sem=send_sem.at[n, facet],
            recv_sem=sem.at[at, q],
            device_id=(facet, group),
            device_id_type=MESH,
        )

    def own_copy(n):
        dst, sem, at = (from_a, recv_a, place) if n == 0 else (from_b, recv_b, last_rank)
        return pltpu.make_async_copy(res.at[n, f], dst.at[at, q], sem.at[at, q])

    def send_all(n):
        for delta in SEND_ORDER:
            result_copy(n, shifted(f, delta, 1)).start()

        @pl.when(group != q)
        def _():
            result_copy(n, f).start()

        @pl.when(group == q)
        def _():
            own_copy(n).start()

    def drain(n):
        def step(facet, carry):
            @pl.when(jnp.logical_not(jnp.logical_and(facet == f, group == q)))
            def _():
                result_copy(n, facet).wait_send()

            return carry

        lax.fori_loop(0, N_FACET, step, 0)

    def unit(n, carry):
        owner = jnp.where(n == 1, LAST, other)
        block = jnp.int32(0)
        for j in range(1, BPC):
            block = jnp.where(shifted(f, DELTA[j], -1) == owner, j, block)
        unit_products(
            q, block, cand_vis, cand_coord, corners[block, 0, owner], corners[block, 1, owner],
            xrow, pbuf, vbuf, acc,
        )

        def put(facet, part, value):
            res[n, facet, part * 8 : (part + 1) * 8, :] = value

        place_results(acc, turned, put)

        @pl.when(n == 0)
        def _():
            pl.semaphore_wait(all_sem, N_FREQ - 1)
            send_all(0)

        @pl.when(n == 1)
        def _():
            send_all(1)

        return carry

    lax.fori_loop(0, 1 + jnp.where(is_last, 1, 0), unit, 0)

    prepare_image(q, owners, corners, assign, counts, other, table_t, pre, pim, br, bi)

    def settle(sem, dst, s):
        for p in range(N_FREQ):
            pltpu.make_async_copy(dst.at[s, p], dst.at[s, p], sem.at[s, p]).wait()

    def share(at):
        rows, copies = pl.ds(at, PER_SET), []
        part = at // PER_SET
        for n in range(1, N_FREQ):
            copies.append(
                pltpu.make_async_remote_copy(
                    src_ref=total.at[rows],
                    dst_ref=got.at[pl.ds(q * SLOTS + at, PER_SET)],
                    send_sem=peer_send.at[part, n],
                    recv_sem=peer_recv.at[part, n],
                    device_id=peers_of(n),
                    device_id_type=MESH,
                )
            )
            copies[-1].start()
        keep = pltpu.make_async_copy(
            total.at[rows], got.at[pl.ds(q * SLOTS + at, PER_SET)], peer_send.at[part, 0]
        )
        keep.start()
        return copies, keep

    for s in range(8):
        settle(recv_a, from_a, s)
    wanted = (q + N_FREQ - group_at(other)) % N_FREQ
    for s in range(PER_SET):
        at = jnp.int32(0)
        for g in range(N_FREQ):
            j = MEMBERS[g][min(s, len(MEMBERS[g]) - 1)]
            at = jnp.where(wanted == g, shifted(other, DELTA[j], 1) // 4, at)
        total[s] = (from_a[at, 0] + from_a[at, 1]) + (from_a[at, 2] + from_a[at, 3])
    first = share(0)
    wanted = (q + N_FREQ - group_at(LAST)) % N_FREQ
    for s in range(PER_SET):
        present = pick(wanted, [int(s < len(m)) for m in MEMBERS]) == 1

        @pl.when(present)
        def _():
            settle(recv_b, from_b, s)
            total[PER_SET + s] = (from_b[s, 0] + from_b[s, 1]) + (from_b[s, 2] + from_b[s, 3])

        @pl.when(jnp.logical_not(present))
        def _():
            total[PER_SET + s] = jnp.zeros((16, 128), f32)

    second = share(PER_SET)
    peers = first[0] + second[0]
    for part, (_, keep) in enumerate((first, second)):
        keep.wait()
        for n in range(1, N_FREQ):
            rows = pl.ds((q + N_FREQ - n) % N_FREQ * SLOTS + part * PER_SET, PER_SET)
            pltpu.make_async_copy(
                total.at[pl.ds(0, PER_SET)], got.at[rows], peer_recv.at[part, n]
            ).wait()
    make_image(q, other, got, table, pre, pim, br, bi, zr, zi, out)
    for c in moves:
        c.wait_send()
    for p in peers:
        p.wait_send()
    drain(0)

    @pl.when(is_last)
    def _():
        drain(1)


def on_device(visibilities, coords, corners, owners, assign, counts):
    d, plain = image_table()
    scale = 1.0 / (SUB * SUB * math.sqrt(2 * BPC * BLK * CHANS))
    high = (d * scale).astype(bf16)
    low = (d * scale - high.astype(np.float64)).astype(bf16)
    smem = pl.BlockSpec(memory_space=pltpu.SMEM)
    vmem = pl.BlockSpec(memory_space=pltpu.VMEM)
    hbm = pl.BlockSpec(memory_space=pl.ANY)
    dma = pltpu.SemaphoreType.DMA
    return pl.pallas_call(
        fused_kernel,
        out_shape=jax.ShapeDtypeStruct((1, G // N_FREQ, G), f32),
        in_specs=[hbm, hbm] + [smem] * 4 + [vmem] * 2,
        out_specs=vmem,
        scratch_shapes=[
            pltpu.VMEM((BPC, 2, CH, BLK), f32),
            pltpu.VMEM((3 * BPC, 1, BLK), f32),
        ]
        + unit_scratch()
        + [
            pltpu.VMEM((2, N_FACET, 16, 128), f32),
            pltpu.VMEM((8, N_FREQ, 16, 128), f32),
            pltpu.VMEM((PER_SET, N_FREQ, 16, 128), f32),
            pltpu.VMEM((SLOTS, 16, 128), f32),
            pltpu.VMEM((N_FREQ * SLOTS, 16, 128), f32),
            pltpu.VMEM((128, 640), f32),
            pltpu.VMEM((128, 640), f32),
            pltpu.VMEM((2, 640, G), bf16),
            pltpu.VMEM((2, 640, G), bf16),
            pltpu.VMEM((32, 640), f32),
            pltpu.VMEM((32, 640), f32),
            pltpu.SemaphoreType.REGULAR,
            pltpu.SemaphoreType.REGULAR,
            pltpu.SemaphoreType.REGULAR,
            dma((BPC, 2)),
            dma((BPC, 2)),
            dma((2, N_FACET)),
            dma((8, N_FREQ)),
            dma((PER_SET, N_FREQ)),
            dma((2, N_FREQ)),
            dma((2, N_FREQ)),
        ],
        compiler_params=pltpu.CompilerParams(collective_id=0, has_side_effects=True),
        name="grid_and_image",
    )(
        visibilities,
        jnp.transpose(coords, (1, 2, 0, 3)).reshape(3 * BPC, 1, BLK),
        owners,
        jnp.transpose(corners, (2, 0, 1)),
        assign,
        counts,
        jnp.asarray(np.concatenate([high, high, low], axis=1)),
        jnp.asarray(plain.T, f32),
    )


def solution(mesh):
    placed = (
        P("facet", None, None, "freq", None),
        P("facet", None, None, None),
        P(),
        P(),
        P("facet", None),
        P("facet"),
    )
    return jax.shard_map(
        on_device, mesh=mesh, in_specs=placed, out_specs=P("facet", "freq", None), check_vma=False
    )
```

```python
import functools
import math

import jax
import jax.numpy as jnp
import numpy as np
from jax import lax
from jax.experimental import pallas as pl
from jax.experimental.pallas import tpu as pltpu
from jax.sharding import PartitionSpec as P

SUB = 32
G = 512
BPC = 10
CH = 32
N_FACET = 32
N_FREQ = 4
BLK = 128
CHANS = CH * N_FREQ
CHUNK = 8
LO = False
MESH = pl.DeviceIdType.MESH
f32 = jnp.float32
bf16 = jnp.bfloat16

DELTA = (
    (0, 0, 0),
    (1, 0, 0),
    (3, 0, 0),
    (0, 0, 1),
    (0, 0, 3),
    (1, 0, 1),
    (1, 0, 3),
    (3, 0, 1),
    (3, 0, 3),
    (0, 1, 0),
)
LAST = N_FACET - 1
PER_SET = 3
SLOTS = 2 * PER_SET
PADDED = 12
WIDE = PADDED * SUB


def fit_sincos():
    s = 0.125 * (1.0 - np.cos(np.pi * (np.arange(400) + 0.5) / 400))
    t = np.sqrt(s)
    poly = np.polynomial.chebyshev
    domain = [0.0, 0.25]
    c = poly.Chebyshev.fit(s, np.cos(2 * np.pi * t), 7, domain=domain)
    n = poly.Chebyshev.fit(s, np.sin(2 * np.pi * t) / t, 7, domain=domain)
    to_power = lambda p: p.convert(kind=np.polynomial.Polynomial).coef
    return [float(v) for v in to_power(c)], [float(v) for v in to_power(n)]


COS_POLY, SIN_POLY = fit_sincos()


def sincos(cycles):
    t = cycles - jnp.floor(cycles + 0.5)
    s = t * t
    c = jnp.full_like(s, COS_POLY[-1])
    for k in COS_POLY[-2::-1]:
        c = c * s + k
    n = jnp.full_like(s, SIN_POLY[-1])
    for k in SIN_POLY[-2::-1]:
        n = n * s + k
    return c, n * t


def cmul(a, b):
    return a[0] * b[0] - a[1] * b[1], a[0] * b[1] + a[1] * b[0]


def both(a, b):
    rr, ii, ri, ir = a[0] * b[0], a[1] * b[1], a[0] * b[1], a[1] * b[0]
    return (rr - ii, ri + ir), (rr + ii, ir - ri)


def image_table():
    x = np.arange(G) - G // 2
    l = np.arange(SUB) - SUB // 2
    n = np.arange(SUB) - SUB // 2
    theta = x[:, None] / G - l[None, :] / SUB
    kernel = np.exp(2j * np.pi * n[None, None, :] * theta[:, :, None]).sum(axis=2)
    real = (kernel * np.exp(1j * np.pi * theta)).real
    real = real * (1.0 - 0.8 * (l / (SUB / 2.0)) ** 2)[None, :]
    upper, lower = real[:, SUB // 2 :], real[:, SUB // 2 - 1 :: -1]
    even, odd = upper + lower, upper - lower
    plain = np.concatenate([even, odd], axis=1)
    table = np.zeros((G, SUB))
    for row in range(SUB):
        m, one, two, t = row // 8, (row // 4) % 2, (row // 2) % 2, row % 2
        for s1 in (1, -1):
            for s2 in (1, -1):
                place = int(8 + s1 * (4 + s2 * (m + 0.5)) - 0.5)
                sign = {
                    (0, 0, 0): 1, (0, 1, 1): -s2, (1, 0, 1): -s1 * s2, (1, 1, 0): -s1,
                    (1, 0, 0): 1, (1, 1, 1): -s2, (0, 1, 0): s1, (0, 0, 1): s1 * s2,
                }[(one, two, t)]
                table[:, row] += sign * ((odd if (one + two + t) % 2 else even)[:, place])
    return table, plain


def shifted(f, delta, sign):
    z, y, x = f // 8, (f // 4) % 2, f % 4
    z = (z + (delta[0] if sign > 0 else 4 - delta[0])) % 4
    y = (y + delta[1]) % 2
    x = (x + (delta[2] if sign > 0 else 4 - delta[2])) % 4
    return z * 8 + y * 4 + x


def shifted_int(f, delta):
    return ((f // 8 + delta[0]) % 4) * 8 + ((f // 4 % 2 + delta[1]) % 2) * 4 + (f % 4 + delta[2]) % 4


def group_of(z, y, x):
    return (z + x + 2 * y) % N_FREQ


def group_at(f):
    return group_of(f // 8, (f // 4) % 2, f % 4)


GROUP = tuple(group_of(*d) for d in DELTA)
MEMBERS = tuple(tuple(j for j in range(BPC) if GROUP[j] == g) for g in range(N_FREQ))
RANK = tuple(MEMBERS[GROUP[j]].index(j) for j in range(BPC))
def hops(delta):
    return min(delta[0], 4 - delta[0]) + 2 * delta[1] + min(delta[2], 4 - delta[2])


SEND_ORDER = tuple(
    sorted(
        ((n * 13 % 32 // 8, n * 13 % 32 // 4 % 2, n * 13 % 4) for n in range(1, N_FACET)),
        key=lambda d: -hops(d),
    )
)
LAST_POS = tuple(shifted_int(LAST, d) for d in DELTA)


def unit_products(q, block, cand_vis, cand_coord, ou, ov, xrow, pbuf, vbuf, acc):
    step = 0.02 / CHANS
    start = 1.0 + (step * CH) * q.astype(f32)
    u, v, w = cand_coord[3 * block], cand_coord[3 * block + 1], cand_coord[3 * block + 2]
    ou = 240.5 - ou.astype(f32)
    ov = 240.5 - ov.astype(f32)
    row = lax.broadcasted_iota(jnp.int32, (32, BLK), 0)

    def wave(d, corner, m, back=0.0):
        return sincos((d * start + corner) * m - back), sincos((d * step) * m)

    row8 = row[:8]
    x, x_turn = wave(
        u, ou, (2 * (row8 % 4) + 1).astype(f32) * (1.0 / 64.0), (row8 // 4).astype(f32) * 0.25
    )
    y, y_turn = wave(v, ov, (2 * row[:16] + 1).astype(f32) * (1.0 / 64.0))
    half, half_turn = wave(u, ou, jnp.full((8, BLK), 0.125, f32))
    a = (row % 8).astype(f32) - 3.5
    e = (row // 8).astype(f32) - 1.5
    rho = 0.0004 * (a * a + e * e)
    shift = -rho / (1.0 + jnp.sqrt(1.0 - rho))
    cycles = u * a + v * e + w * shift - (u + v) * (1.0 / 64.0)
    spin = sincos(cycles * start - (ou + ov) * (1.0 / 64.0))
    spin_turn = sincos(cycles * step)
    state = [x, y, half, spin]
    turns = [x_turn, y_turn, half_turn, spin_turn]
    rows4 = lambda t: jnp.concatenate([t] * 4, axis=0)

    def generate(c, slot, cc):
        x, y, half, spin = state
        xrow[slot, cc] = x[0]
        ys = jnp.concatenate(y, axis=0)
        for r in range(8):
            pbuf[slot, cc, r * 32 : (r + 1) * 32, :] = (
                jnp.broadcast_to(xrow[slot, cc, r : r + 1, :], (32, BLK)) * ys
            ).astype(bf16)
        re = jnp.broadcast_to(cand_vis[block, 0, c : c + 1, :], (32, BLK))
        im = jnp.broadcast_to(cand_vis[block, 1, c : c + 1, :], (32, BLK))
        rotated = cmul((re, im), spin)
        c2, s2 = half
        c1, s1 = c2 * c2 - s2 * s2, 2.0 * (c2 * s2)
        for n, factor in enumerate((c1 * c2, c1 * s2, s1 * c2, s1 * s2)):
            factor = rows4(factor)
            for part in range(2):
                value = rotated[part] * factor
                high = value.astype(bf16)
                at = n * 64 + part * 32
                vbuf[slot, cc, at : at + 32, :] = high
                if LO:
                    vbuf[slot, cc, 256 + at : 288 + at, :] = (value - high.astype(f32)).astype(bf16)
        for n in range(4):
            state[n] = cmul(state[n], turns[n])

    def multiply(k, slot):
        left = jnp.concatenate([vbuf[slot, cc] for cc in range(CHUNK)], axis=1)
        right = jnp.concatenate([pbuf[slot, cc] for cc in range(CHUNK)], axis=1)
        part = lax.dot_general(
            left, right, (((1,), (1,)), ((), ())), preferred_element_type=f32
        )
        acc[...] = part if k == 0 else acc[...] + part

    chunks = CH // CHUNK
    for k in range(chunks + 1):
        for cc in range(CHUNK):
            if k < chunks:
                generate(k * CHUNK + cc, k % 2, cc)
        if k > 0:
            multiply(k - 1, (k - 1) % 2)


def place_results(acc, turned, put):
    for n in range(4):
        for h in range(2):
            rows, lanes = slice(n * 64, (n + 1) * 64), slice(h * 128, (h + 1) * 128)
            value = acc[rows, lanes]
            if LO:
                value = value + acc[256 + n * 64 : 320 + n * 64, lanes]
            turned[(2 * n + h) * 64 : (2 * n + h + 1) * 64, :] = value
    for part in range(2):
        for facet in range(N_FACET):
            put(facet, part, turned[pl.ds(part * 32 + facet, 8, stride=64), :])


def unit_scratch():
    rows = 512 if LO else 256
    return [
        pltpu.VMEM((2, CHUNK, 8, BLK), f32),
        pltpu.VMEM((2, CHUNK, 256, BLK), bf16),
        pltpu.VMEM((2, CHUNK, rows, BLK), bf16),
        pltpu.VMEM((rows, 256), f32),
        pltpu.VMEM((512, 128), f32),
    ]


def pick(index, values):
    out = jnp.int32(values[0])
    for n, v in enumerate(values):
        if n:
            out = jnp.where(index == n, v, out)
    return out


def split(a):
    high = a.astype(bf16)
    return high, (a - high.astype(f32)).astype(bf16)


def dot3(a, b):
    dot = functools.partial(jnp.dot, preferred_element_type=f32)
    return dot(a[0], b[0]) + (dot(a[0], b[1]) + dot(a[1], b[0]))


def lanes_of(values):
    group = lax.broadcasted_iota(jnp.int32, (1, 128), 1) // 32
    tiles = []
    for tile in range(PADDED // 4):
        v = jnp.full((1, 128), values[tile * 4], jnp.int32)
        for g in range(1, 4):
            v = jnp.where(group == g, values[min(tile * 4 + g, BPC - 1)], v)
        tiles.append(v)
    return jnp.concatenate(tiles, axis=1)


def prepare_image(q, owners, corners, assign, counts, other, table_t, pre, pim, br, bi):
    first_last = owners[0] == LAST
    count = counts[0]
    k_of = lax.broadcasted_iota(jnp.int32, (1, WIDE), 1) // 32
    rows = q * 128 - 256 + lax.broadcasted_iota(jnp.int32, (128, WIDE), 0)
    columns = lax.broadcasted_iota(jnp.int32, (1, G), 1) - 256
    for part, owner in enumerate((other, LAST)):
        base = jnp.where(first_last, BPC, 0) if part == 0 else jnp.where(first_last, 0, BPC)
        block = jnp.where(k_of < BPC, base + k_of, -1)
        weight = jnp.zeros((1, WIDE), f32)
        for n in range(2 * BPC):
            live = jnp.where(n < count, 1.0, 0.0).astype(f32)
            weight = weight + jnp.where(block == assign[0, n], live, 0.0)
        corner_u = lanes_of([corners[j, 0, owner] for j in range(BPC)])
        turns = jnp.bitwise_and(rows * (2 * corner_u - 481), 1023)
        c, s = sincos(turns.astype(f32) * (1.0 / 1024.0))
        pre[part] = c * weight
        pim[part] = s * weight
        for k in range(BPC):
            turns = jnp.bitwise_and(columns * (2 * corners[k, 1, owner] - 481), 1023)
            c, s = sincos(turns.astype(f32) * (1.0 / 1024.0))
            for ref, value in ((br, table_t[...] * c), (bi, table_t[...] * -s)):
                high, low = split(value)
                ref[part, 0, k * 32 : (k + 1) * 32, :] = high
                ref[part, 1, k * 32 : (k + 1) * 32, :] = low
        for ref in (br, bi):
            for h in range(2):
                ref[part, h, BPC * 32 : WIDE, :] = jnp.zeros((WIDE - BPC * 32, G), bf16)


def image_part(part, q, other, got, table, pre, pim, br, bi, zr, zi):
    lane = lax.broadcasted_iota(jnp.int32, (8, 128), 1)
    sub = lax.broadcasted_iota(jnp.int32, (8, 128), 0)
    row_sine = (sub // 4 + (sub // 2) % 2 + sub % 2) % 2 == 1
    lane_sine = lane % 32 >= 16
    two = jnp.logical_and(row_sine, lane_sine)
    one = jnp.logical_and(jnp.logical_or(row_sine, lane_sine), jnp.logical_not(two))
    group = lane // 32
    home = group_at(other if part == 0 else LAST)
    nothing = jnp.zeros((8, 128), f32)
    for tile in range(PADDED // 4):
        parts = [[None] * 4, [None] * 4]
        for g in range(4):
            j = tile * 4 + g
            if j >= BPC:
                for i4 in range(4):
                    for p in range(2):
                        parts[p][i4] = jnp.where(group == g, nothing, parts[p][i4])
                continue
            block = got[(home + GROUP[j]) % N_FREQ * PER_SET + RANK[j]]
            re, im = block[:8], block[8:]
            new_re = jnp.where(one, -im, jnp.where(two, -re, re))
            new_im = jnp.where(one, re, jnp.where(two, -im, im))
            for i4 in range(4):
                shift = ((g - i4) * 32) % 128
                for p, value in enumerate((new_re, new_im)):
                    if shift:
                        value = pltpu.roll(value, shift, 1)
                    old = parts[p][i4]
                    parts[p][i4] = value if old is None else jnp.where(group == g, value, old)
        for i4 in range(4):
            zr[i4 * 8 : (i4 + 1) * 8, tile * 128 : (tile + 1) * 128] = parts[0][i4]
            zi[i4 * 8 : (i4 + 1) * 8, tile * 128 : (tile + 1) * 128] = parts[1][i4]
    d = table[pl.ds(pl.multiple_of(q * 128, 128), 128), :]

    def apply(z):
        high, low = split(z)
        return jnp.dot(
            d, jnp.concatenate([high, low, high], axis=0), preferred_element_type=f32
        )

    t_re, t_im = apply(zr[...]), apply(zi[...])
    l_re = t_re * pre[part] - t_im * pim[part]
    l_im = t_re * pim[part] + t_im * pre[part]
    return dot3(split(l_re), (br[part, 0], br[part, 1])) + dot3(
        split(l_im), (bi[part, 0], bi[part, 1])
    )


def fused_kernel(
    vis, coord, owners_in, corners_in, assign_in, counts_in, table_in, table_t_in, out,
    owners, corners, assign, counts, table, table_t,
    cand_vis, cand_coord, xrow, pbuf, vbuf, acc, turned, res, from_a, from_b, total, got_a, got_b,
    pre, pim, br, bi, zr, zi,
    plane_sem, near_sem, all_sem, args_sem, move_send, move_recv, send_sem, recv_a, recv_b, peer_send, peer_recv,
):
    f = lax.axis_index("facet")
    q = lax.axis_index("freq")
    group = group_at(f)
    last_block = jnp.int32(-1)
    for j in range(BPC):
        last_block = jnp.where(f == LAST_POS[j], j, last_block)
    is_last = last_block >= 0
    last_rank = pick(last_block, RANK)
    barrier = pltpu.get_barrier_semaphore()

    def signal(facet, freq):
        pl.semaphore_signal(barrier, inc=1, device_id=(facet, freq), device_id_type=MESH)

    def peers_of(n):
        return (f, (q + n) % N_FREQ)

    for j in range(1, BPC):
        signal(shifted(f, DELTA[j], -1), q)
    for n in range(1, N_FREQ):
        signal(*peers_of(n))

    def tell(sem, facet, freq):
        pl.semaphore_signal(sem, inc=1, device_id=(facet, freq), device_id_type=MESH)

    args = [
        pltpu.make_async_copy(src, dst, args_sem.at[n])
        for n, (src, dst) in enumerate(
            (
                (owners_in, owners),
                (corners_in, corners),
                (assign_in, assign),
                (counts_in, counts),
                (table_in, table),
                (table_t_in, table_t),
            )
        )
    ]
    own = [
        pltpu.make_async_copy(vis.at[0, 0], cand_vis.at[0], move_recv.at[0, 0]),
        pltpu.make_async_copy(coord.at[pl.ds(0, 3)], cand_coord.at[pl.ds(0, 3)], move_recv.at[0, 1]),
    ]
    for c in own + args:
        c.start()
    pl.semaphore_wait(barrier, BPC - 1 + N_FREQ - 1)
    moves = []
    for j in range(BPC - 1, 0, -1):
        to = (shifted(f, DELTA[j], 1), q)
        rows = pl.ds(3 * j, 3)
        pairs = ((vis.at[0, j], cand_vis.at[j]), (coord.at[rows], cand_coord.at[rows]))
        for n, (src, dst) in enumerate(pairs):
            moves.append(
                pltpu.make_async_remote_copy(
                    src_ref=src,
                    dst_ref=dst,
                    send_sem=move_send.at[j, n],
                    recv_sem=move_recv.at[j, n],
                    device_id=to,
                    device_id_type=MESH,
                )
            )
            moves[-1].start()
    for delta in ((3, 0, 3), (3, 0, 1), (1, 0, 3)):
        tell(plane_sem, shifted(f, delta, 1), q)
    pl.semaphore_wait(plane_sem, 3)
    tell(near_sem, shifted(f, (0, 1, 0), 1), q)
    for n in range(1, N_FREQ):
        tell(near_sem, *peers_of(n))
    pl.semaphore_wait(near_sem, N_FREQ)
    for n in range(1, N_FREQ):
        tell(all_sem, *peers_of(n))
    for c in own + args:
        c.wait()
    for c in moves:
        c.wait_recv()

    other = jnp.where(owners[0] == LAST, owners[1], owners[0]).astype(jnp.int32)
    place = f // 4

    def result_copy(n, facet):
        dst, sem, at = (from_a, recv_a, place) if n == 0 else (from_b, recv_b, last_rank)
        return pltpu.make_async_remote_copy(
            src_ref=res.at[n, facet],
            dst_ref=dst.at[at, q],
            send_sem=send_sem.at[n, facet],
            recv_sem=sem.at[at, q],
            device_id=(facet, group),
            device_id_type=MESH,
        )

    def own_copy(n):
        dst, sem, at = (from_a, recv_a, place) if n == 0 else (from_b, recv_b, last_rank)
        return pltpu.make_async_copy(res.at[n, f], dst.at[at, q], sem.at[at, q])

    def send_all(n):
        for delta in SEND_ORDER:
            result_copy(n, shifted(f, delta, 1)).start()

        @pl.when(group != q)
        def _():
            result_copy(n, f).start()

        @pl.when(group == q)
        def _():
            own_copy(n).start()

    def drain(n):
        def step(facet, carry):
            @pl.when(jnp.logical_not(jnp.logical_and(facet == f, group == q)))
            def _():
                result_copy(n, facet).wait_send()

            return carry

        lax.fori_loop(0, N_FACET, step, 0)

    def unit(n, carry):
        owner = jnp.where(n == 1, LAST, other)
        block = jnp.int32(0)
        for j in range(1, BPC):
            block = jnp.where(shifted(f, DELTA[j], -1) == owner, j, block)
        unit_products(
            q, block, cand_vis, cand_coord, corners[block, 0, owner], corners[block, 1, owner],
            xrow, pbuf, vbuf, acc,
        )

        def put(facet, part, value):
            res[n, facet, part * 8 : (part + 1) * 8, :] = value

        place_results(acc, turned, put)

        @pl.when(n == 0)
        def _():
            pl.semaphore_wait(all_sem, N_FREQ - 1)
            send_all(0)

        @pl.when(n == 1)
        def _():
            send_all(1)

        return carry

    lax.fori_loop(0, 1 + jnp.where(is_last, 1, 0), unit, 0)

    prepare_image(q, owners, corners, assign, counts, other, table_t, pre, pim, br, bi)

    def settle(sem, dst, s):
        for p in range(N_FREQ):
            pltpu.make_async_copy(dst.at[s, p], dst.at[s, p], sem.at[s, p]).wait()

    def share(got, at, size, part):
        rows, copies = pl.ds(at, size), []
        for n in (2, 1, 3):
            copies.append(
                pltpu.make_async_remote_copy(
                    src_ref=total.at[rows],
                    dst_ref=got.at[pl.ds(q * PER_SET + at % PER_SET, size)],
                    send_sem=peer_send.at[part, n],
                    recv_sem=peer_recv.at[part, n],
                    device_id=peers_of(n),
                    device_id_type=MESH,
                )
            )
            copies[-1].start()
        keep = pltpu.make_async_copy(
            total.at[rows], got.at[pl.ds(q * PER_SET + at % PER_SET, size)], peer_send.at[part, 0]
        )
        keep.start()
        return copies, keep

    def collect(got, shared, at, size, part):
        shared[1].wait()
        for n in range(1, N_FREQ):
            rows = pl.ds((q + N_FREQ - n) % N_FREQ * PER_SET + at % PER_SET, size)
            pltpu.make_async_copy(
                total.at[pl.ds(0, size)], got.at[rows], peer_recv.at[part, n]
            ).wait()

    for s in range(8):
        settle(recv_a, from_a, s)
    wanted = (q + N_FREQ - group_at(other)) % N_FREQ
    for s in range(PER_SET):
        at = jnp.int32(0)
        for g in range(N_FREQ):
            j = MEMBERS[g][min(s, len(MEMBERS[g]) - 1)]
            at = jnp.where(wanted == g, shifted(other, DELTA[j], 1) // 4, at)
        total[s] = (from_a[at, 0] + from_a[at, 1]) + (from_a[at, 2] + from_a[at, 3])
    first = share(got_a, 0, PER_SET, 0)
    later = []
    wanted = (q + N_FREQ - group_at(LAST)) % N_FREQ
    for s in range(PER_SET):
        present = pick(wanted, [int(s < len(m)) for m in MEMBERS]) == 1

        @pl.when(present)
        def _():
            settle(recv_b, from_b, s)
            total[PER_SET + s] = (from_b[s, 0] + from_b[s, 1]) + (from_b[s, 2] + from_b[s, 3])

        @pl.when(jnp.logical_not(present))
        def _():
            total[PER_SET + s] = jnp.zeros((16, 128), f32)

        later.append(share(got_b, PER_SET + s, 1, 1 + s))

    peers = first[0]
    collect(got_a, first, 0, PER_SET, 0)
    out[0] = image_part(0, q, other, got_a, table, pre, pim, br, bi, zr, zi)
    for s, shared in enumerate(later):
        peers = peers + shared[0]
        collect(got_b, shared, PER_SET + s, 1, 1 + s)
    out[0] = out[0] + image_part(1, q, other, got_b, table, pre, pim, br, bi, zr, zi)
    for c in moves:
        c.wait_send()
    for p in peers:
        p.wait_send()
    drain(0)

    @pl.when(is_last)
    def _():
        drain(1)


def on_device(visibilities, coords, corners, owners, assign, counts):
    d, plain = image_table()
    scale = 1.0 / (SUB * SUB * math.sqrt(2 * BPC * BLK * CHANS))
    high = (d * scale).astype(bf16)
    low = (d * scale - high.astype(np.float64)).astype(bf16)
    vmem = pl.BlockSpec(memory_space=pltpu.VMEM)
    hbm = pl.BlockSpec(memory_space=pl.ANY)
    dma = pltpu.SemaphoreType.DMA
    return pl.pallas_call(
        fused_kernel,
        out_shape=pltpu.VMEM((1, G // N_FREQ, G), f32),
        in_specs=[hbm] * 8,
        out_specs=vmem,
        scratch_shapes=[
            pltpu.SMEM((2,), jnp.int32),
            pltpu.SMEM((BPC, 2, N_FACET), jnp.int32),
            pltpu.SMEM((1, 2 * BPC), jnp.int32),
            pltpu.SMEM((1,), jnp.int32),
            pltpu.VMEM((G, 3 * SUB), bf16),
            pltpu.VMEM((SUB, G), f32),
            pltpu.VMEM((BPC, 2, CH, BLK), f32),
            pltpu.VMEM((3 * BPC, 1, BLK), f32),
        ]
        + unit_scratch()
        + [
            pltpu.VMEM((2, N_FACET, 16, 128), f32),
            pltpu.VMEM((8, N_FREQ, 16, 128), f32),
            pltpu.VMEM((PER_SET, N_FREQ, 16, 128), f32),
            pltpu.VMEM((SLOTS, 16, 128), f32),
            pltpu.VMEM((N_FREQ * PER_SET, 16, 128), f32),
            pltpu.VMEM((N_FREQ * PER_SET, 16, 128), f32),
            pltpu.VMEM((2, 128, WIDE), f32),
            pltpu.VMEM((2, 128, WIDE), f32),
            pltpu.VMEM((2, 2, WIDE, G), bf16),
            pltpu.VMEM((2, 2, WIDE, G), bf16),
            pltpu.VMEM((32, WIDE), f32),
            pltpu.VMEM((32, WIDE), f32),
            pltpu.SemaphoreType.REGULAR,
            pltpu.SemaphoreType.REGULAR,
            pltpu.SemaphoreType.REGULAR,
            dma((6,)),
            dma((BPC, 2)),
            dma((BPC, 2)),
            dma((2, N_FACET)),
            dma((8, N_FREQ)),
            dma((PER_SET, N_FREQ)),
            dma((1 + PER_SET, N_FREQ)),
            dma((1 + PER_SET, N_FREQ)),
        ],
        compiler_params=pltpu.CompilerParams(collective_id=0, has_side_effects=True),
        name="grid_and_image",
    )(
        visibilities,
        jnp.transpose(coords, (1, 2, 0, 3)).reshape(3 * BPC, 1, BLK),
        owners,
        jnp.transpose(corners, (2, 0, 1)),
        assign,
        counts,
        jnp.asarray(np.concatenate([high, high, low], axis=1)),
        jnp.asarray(plain.T, f32),
    )


def solution(mesh):
    placed = (
        P("facet", None, None, "freq", None),
        P("facet", None, None, None),
        P(),
        P(),
        P("facet", None),
        P("facet"),
    )
    return jax.shard_map(
        on_device, mesh=mesh, in_specs=placed, out_specs=P("facet", "freq", None), check_vma=False
    )
```

```python
import functools
import math

import jax
import jax.numpy as jnp
import numpy as np
from jax import lax
from jax.experimental import pallas as pl
from jax.experimental.pallas import tpu as pltpu
from jax.sharding import PartitionSpec as P

SUB = 32
G = 512
BPC = 10
CH = 32
N_FACET = 32
N_FREQ = 4
BLK = 128
CHANS = CH * N_FREQ
CHUNK = 8
LO = False
MESH = pl.DeviceIdType.MESH
f32 = jnp.float32
bf16 = jnp.bfloat16

DELTA = (
    (0, 0, 0),
    (1, 0, 0),
    (3, 0, 0),
    (0, 0, 1),
    (0, 0, 3),
    (1, 0, 1),
    (1, 0, 3),
    (3, 0, 1),
    (3, 0, 3),
    (0, 1, 0),
)
LAST = N_FACET - 1
PER_SET = 3
SLOTS = 2 * PER_SET
PADDED = 12
WIDE = PADDED * SUB


def fit_sincos():
    s = 0.125 * (1.0 - np.cos(np.pi * (np.arange(400) + 0.5) / 400))
    t = np.sqrt(s)
    poly = np.polynomial.chebyshev
    domain = [0.0, 0.25]
    c = poly.Chebyshev.fit(s, np.cos(2 * np.pi * t), 7, domain=domain)
    n = poly.Chebyshev.fit(s, np.sin(2 * np.pi * t) / t, 7, domain=domain)
    to_power = lambda p: p.convert(kind=np.polynomial.Polynomial).coef
    return [float(v) for v in to_power(c)], [float(v) for v in to_power(n)]


COS_POLY, SIN_POLY = fit_sincos()


def sincos(cycles):
    t = cycles - jnp.floor(cycles + 0.5)
    s = t * t
    c = jnp.full_like(s, COS_POLY[-1])
    for k in COS_POLY[-2::-1]:
        c = c * s + k
    n = jnp.full_like(s, SIN_POLY[-1])
    for k in SIN_POLY[-2::-1]:
        n = n * s + k
    return c, n * t


def cmul(a, b):
    return a[0] * b[0] - a[1] * b[1], a[0] * b[1] + a[1] * b[0]


def both(a, b):
    rr, ii, ri, ir = a[0] * b[0], a[1] * b[1], a[0] * b[1], a[1] * b[0]
    return (rr - ii, ri + ir), (rr + ii, ir - ri)


def image_table():
    x = np.arange(G) - G // 2
    l = np.arange(SUB) - SUB // 2
    n = np.arange(SUB) - SUB // 2
    theta = x[:, None] / G - l[None, :] / SUB
    kernel = np.exp(2j * np.pi * n[None, None, :] * theta[:, :, None]).sum(axis=2)
    real = (kernel * np.exp(1j * np.pi * theta)).real
    real = real * (1.0 - 0.8 * (l / (SUB / 2.0)) ** 2)[None, :]
    upper, lower = real[:, SUB // 2 :], real[:, SUB // 2 - 1 :: -1]
    even, odd = upper + lower, upper - lower
    plain = np.concatenate([even, odd], axis=1)
    table = np.zeros((G, SUB))
    for row in range(SUB):
        m, one, two, t = row // 8, (row // 4) % 2, (row // 2) % 2, row % 2
        for s1 in (1, -1):
            for s2 in (1, -1):
                place = int(8 + s1 * (4 + s2 * (m + 0.5)) - 0.5)
                sign = {
                    (0, 0, 0): 1, (0, 1, 1): -s2, (1, 0, 1): -s1 * s2, (1, 1, 0): -s1,
                    (1, 0, 0): 1, (1, 1, 1): -s2, (0, 1, 0): s1, (0, 0, 1): s1 * s2,
                }[(one, two, t)]
                table[:, row] += sign * ((odd if (one + two + t) % 2 else even)[:, place])
    return table, plain


def around(f):
    z, y, x = lax.div(f, 8), lax.rem(lax.div(f, 4), 2), lax.rem(f, 4)
    zs = [lax.rem(z + d, 4) * 8 for d in range(4)]
    ys = [lax.rem(y + d, 2) * 4 for d in range(2)]
    xs = [lax.rem(x + d, 4) for d in range(4)]

    def go(delta, sign):
        return zs[sign * delta[0] % 4] + ys[delta[1]] + xs[sign * delta[2] % 4]

    return go


def shifted_int(f, delta):
    return ((f // 8 + delta[0]) % 4) * 8 + ((f // 4 % 2 + delta[1]) % 2) * 4 + (f % 4 + delta[2]) % 4


def group_of(z, y, x):
    return (z + x + 2 * y) % N_FREQ


def group_at(f):
    if isinstance(f, int):
        return group_of(f // 8, f // 4 % 2, f % 4)
    return lax.rem(lax.div(f, 8) + lax.rem(f, 4) + 2 * lax.rem(lax.div(f, 4), 2), N_FREQ)


GROUP = tuple(group_of(*d) for d in DELTA)
MEMBERS = tuple(tuple(j for j in range(BPC) if GROUP[j] == g) for g in range(N_FREQ))
RANK = tuple(MEMBERS[GROUP[j]].index(j) for j in range(BPC))
def hops(delta):
    return min(delta[0], 4 - delta[0]) + 2 * delta[1] + min(delta[2], 4 - delta[2])


SEND_ORDER = tuple(
    sorted(
        ((n * 13 % 32 // 8, n * 13 % 32 // 4 % 2, n * 13 % 4) for n in range(1, N_FACET)),
        key=lambda d: -hops(d),
    )
)
LAST_POS = tuple(shifted_int(LAST, d) for d in DELTA)


def unit_products(q, block, cand_vis, cand_coord, ou, ov, xrow, pbuf, vbuf, acc):
    step = 0.02 / CHANS
    start = 1.0 + (step * CH) * q.astype(f32)
    u, v, w = cand_coord[3 * block], cand_coord[3 * block + 1], cand_coord[3 * block + 2]
    ou = 240.5 - ou.astype(f32)
    ov = 240.5 - ov.astype(f32)
    row = lax.broadcasted_iota(jnp.int32, (32, BLK), 0)

    def wave(d, corner, m, back=0.0):
        return sincos((d * start + corner) * m - back), sincos((d * step) * m)

    row8 = row[:8]
    x, x_turn = wave(
        u, ou, (2 * (row8 % 4) + 1).astype(f32) * (1.0 / 64.0), (row8 // 4).astype(f32) * 0.25
    )
    y, y_turn = wave(v, ov, (2 * row[:16] + 1).astype(f32) * (1.0 / 64.0))
    half, half_turn = wave(u, ou, jnp.full((8, BLK), 0.125, f32))
    a = (row % 8).astype(f32) - 3.5
    e = (row // 8).astype(f32) - 1.5
    rho = 0.0004 * (a * a + e * e)
    shift = -rho / (1.0 + jnp.sqrt(1.0 - rho))
    cycles = u * a + v * e + w * shift - (u + v) * (1.0 / 64.0)
    spin = sincos(cycles * start - (ou + ov) * (1.0 / 64.0))
    spin_turn = sincos(cycles * step)
    state = [x, y, half, spin]
    turns = [x_turn, y_turn, half_turn, spin_turn]
    rows4 = lambda t: jnp.concatenate([t] * 4, axis=0)

    def generate(c, slot, cc):
        x, y, half, spin = state
        xrow[slot, cc] = x[0]
        ys = jnp.concatenate(y, axis=0)
        for r in range(8):
            pbuf[slot, cc, r * 32 : (r + 1) * 32, :] = (
                jnp.broadcast_to(xrow[slot, cc, r : r + 1, :], (32, BLK)) * ys
            ).astype(bf16)
        re = jnp.broadcast_to(cand_vis[block, 0, c : c + 1, :], (32, BLK))
        im = jnp.broadcast_to(cand_vis[block, 1, c : c + 1, :], (32, BLK))
        rotated = cmul((re, im), spin)
        c2, s2 = half
        c1, s1 = c2 * c2 - s2 * s2, 2.0 * (c2 * s2)
        for n, factor in enumerate((c1 * c2, c1 * s2, s1 * c2, s1 * s2)):
            factor = rows4(factor)
            for part in range(2):
                value = rotated[part] * factor
                high = value.astype(bf16)
                at = n * 64 + part * 32
                vbuf[slot, cc, at : at + 32, :] = high
                if LO:
                    vbuf[slot, cc, 256 + at : 288 + at, :] = (value - high.astype(f32)).astype(bf16)
        for n in range(4):
            state[n] = cmul(state[n], turns[n])

    def multiply(k, slot):
        left = jnp.concatenate([vbuf[slot, cc] for cc in range(CHUNK)], axis=1)
        right = jnp.concatenate([pbuf[slot, cc] for cc in range(CHUNK)], axis=1)
        part = lax.dot_general(
            left, right, (((1,), (1,)), ((), ())), preferred_element_type=f32
        )
        acc[...] = part if k == 0 else acc[...] + part

    chunks = CH // CHUNK
    for k in range(chunks + 1):
        for cc in range(CHUNK):
            if k < chunks:
                generate(k * CHUNK + cc, k % 2, cc)
        if k > 0:
            multiply(k - 1, (k - 1) % 2)


def place_results(acc, turned, put):
    for n in range(4):
        for h in range(2):
            rows, lanes = slice(n * 64, (n + 1) * 64), slice(h * 128, (h + 1) * 128)
            value = acc[rows, lanes]
            if LO:
                value = value + acc[256 + n * 64 : 320 + n * 64, lanes]
            turned[(2 * n + h) * 64 : (2 * n + h + 1) * 64, :] = value
    for part in range(2):
        for facet in range(N_FACET):
            put(facet, part, turned[pl.ds(part * 32 + facet, 8, stride=64), :])


def unit_scratch():
    rows = 512 if LO else 256
    return [
        pltpu.VMEM((2, CHUNK, 8, BLK), f32),
        pltpu.VMEM((2, CHUNK, 256, BLK), bf16),
        pltpu.VMEM((2, CHUNK, rows, BLK), bf16),
        pltpu.VMEM((rows, 256), f32),
        pltpu.VMEM((512, 128), f32),
    ]


def pick(index, values):
    out = jnp.int32(values[0])
    for n, v in enumerate(values):
        if n:
            out = jnp.where(index == n, v, out)
    return out


def split(a):
    high = a.astype(bf16)
    return high, (a - high.astype(f32)).astype(bf16)


def dot3(a, b):
    dot = functools.partial(jnp.dot, preferred_element_type=f32)
    return dot(a[0], b[0]) + (dot(a[0], b[1]) + dot(a[1], b[0]))


def lanes_of(values):
    group = lax.broadcasted_iota(jnp.int32, (1, 128), 1) // 32
    tiles = []
    for tile in range(PADDED // 4):
        v = jnp.full((1, 128), values[tile * 4], jnp.int32)
        for g in range(1, 4):
            v = jnp.where(group == g, values[min(tile * 4 + g, BPC - 1)], v)
        tiles.append(v)
    return jnp.concatenate(tiles, axis=1)


def prepare_image(q, owners, corners, assign, counts, other, table_t, pre, pim, br, bi):
    first_last = owners[0] == LAST
    count = counts[0]
    k_of = lax.broadcasted_iota(jnp.int32, (1, WIDE), 1) // 32
    rows = q * 128 - 256 + lax.broadcasted_iota(jnp.int32, (128, WIDE), 0)
    columns = lax.broadcasted_iota(jnp.int32, (1, G), 1) - 256
    for part, owner in enumerate((other, LAST)):
        base = jnp.where(first_last, BPC, 0) if part == 0 else jnp.where(first_last, 0, BPC)
        block = jnp.where(k_of < BPC, base + k_of, -1)
        weight = jnp.zeros((1, WIDE), f32)
        for n in range(2 * BPC):
            live = jnp.where(n < count, 1.0, 0.0).astype(f32)
            weight = weight + jnp.where(block == assign[0, n], live, 0.0)
        corner_u = lanes_of([corners[j, 0, owner] for j in range(BPC)])
        turns = jnp.bitwise_and(rows * (2 * corner_u - 481), 1023)
        c, s = sincos(turns.astype(f32) * (1.0 / 1024.0))
        pre[part] = c * weight
        pim[part] = s * weight
        for k in range(BPC):
            turns = jnp.bitwise_and(columns * (2 * corners[k, 1, owner] - 481), 1023)
            c, s = sincos(turns.astype(f32) * (1.0 / 1024.0))
            for ref, value in ((br, table_t[...] * c), (bi, table_t[...] * -s)):
                high, low = split(value)
                ref[part, 0, k * 32 : (k + 1) * 32, :] = high
                ref[part, 1, k * 32 : (k + 1) * 32, :] = low
        for ref in (br, bi):
            for h in range(2):
                ref[part, h, BPC * 32 : WIDE, :] = jnp.zeros((WIDE - BPC * 32, G), bf16)


def image_part(part, q, other, got, table, pre, pim, br, bi, zr, zi):
    lane = lax.broadcasted_iota(jnp.int32, (8, 128), 1)
    sub = lax.broadcasted_iota(jnp.int32, (8, 128), 0)
    row_sine = (sub // 4 + (sub // 2) % 2 + sub % 2) % 2 == 1
    lane_sine = lane % 32 >= 16
    two = jnp.logical_and(row_sine, lane_sine)
    one = jnp.logical_and(jnp.logical_or(row_sine, lane_sine), jnp.logical_not(two))
    group = lane // 32
    home = group_at(other if part == 0 else LAST)
    nothing = jnp.zeros((8, 128), f32)
    for tile in range(PADDED // 4):
        parts = [[None] * 4, [None] * 4]
        for g in range(4):
            j = tile * 4 + g
            if j >= BPC:
                for i4 in range(4):
                    for p in range(2):
                        parts[p][i4] = jnp.where(group == g, nothing, parts[p][i4])
                continue
            block = got[((home + GROUP[j]) % N_FREQ if part else lax.rem(home + GROUP[j], N_FREQ)) * PER_SET + RANK[j]]
            re, im = block[:8], block[8:]
            new_re = jnp.where(one, -im, jnp.where(two, -re, re))
            new_im = jnp.where(one, re, jnp.where(two, -im, im))
            for i4 in range(4):
                shift = ((g - i4) * 32) % 128
                for p, value in enumerate((new_re, new_im)):
                    if shift:
                        value = pltpu.roll(value, shift, 1)
                    old = parts[p][i4]
                    parts[p][i4] = value if old is None else jnp.where(group == g, value, old)
        for i4 in range(4):
            zr[i4 * 8 : (i4 + 1) * 8, tile * 128 : (tile + 1) * 128] = parts[0][i4]
            zi[i4 * 8 : (i4 + 1) * 8, tile * 128 : (tile + 1) * 128] = parts[1][i4]
    d = table[pl.ds(pl.multiple_of(q * 128, 128), 128), :]

    def apply(z):
        high, low = split(z)
        return jnp.dot(
            d, jnp.concatenate([high, low, high], axis=0), preferred_element_type=f32
        )

    t_re, t_im = apply(zr[...]), apply(zi[...])
    l_re = t_re * pre[part] - t_im * pim[part]
    l_im = t_re * pim[part] + t_im * pre[part]
    return dot3(split(l_re), (br[part, 0], br[part, 1])) + dot3(
        split(l_im), (bi[part, 0], bi[part, 1])
    )


def fused_kernel(
    vis, coord, owners_in, corners_in, assign_in, counts_in, table_in, table_t_in, out,
    owners, corners, assign, counts, table, table_t,
    cand_vis, cand_coord, xrow, pbuf, vbuf, acc, turned, res, from_a, from_b, total, got_a, got_b,
    pre, pim, br, bi, zr, zi,
    plane_sem, near_sem, all_sem, args_sem, move_send, move_recv, send_sem, recv_a, recv_b, peer_send, peer_recv,
):
    f = lax.axis_index("facet")
    q = lax.axis_index("freq")
    here = around(f)
    group = group_at(f)
    last_block = jnp.int32(-1)
    for j in range(BPC):
        last_block = jnp.where(f == LAST_POS[j], j, last_block)
    is_last = last_block >= 0
    last_rank = pick(last_block, RANK)
    barrier = pltpu.get_barrier_semaphore()

    def signal(facet, freq):
        pl.semaphore_signal(barrier, inc=1, device_id=(facet, freq), device_id_type=MESH)

    def peers_of(n):
        return (f, lax.rem(q + n, N_FREQ))

    for j in range(1, BPC):
        signal(here(DELTA[j], -1), q)
    for n in range(1, N_FREQ):
        signal(*peers_of(n))

    def tell(sem, facet, freq):
        pl.semaphore_signal(sem, inc=1, device_id=(facet, freq), device_id_type=MESH)

    args = [
        pltpu.make_async_copy(src, dst, args_sem.at[n])
        for n, (src, dst) in enumerate(
            (
                (owners_in, owners),
                (corners_in, corners),
                (assign_in, assign),
                (counts_in, counts),
                (table_in, table),
                (table_t_in, table_t),
            )
        )
    ]
    own = [
        pltpu.make_async_copy(vis.at[0, 0], cand_vis.at[0], move_recv.at[0, 0]),
        pltpu.make_async_copy(coord.at[pl.ds(0, 3)], cand_coord.at[pl.ds(0, 3)], move_recv.at[0, 1]),
    ]
    for c in own + args:
        c.start()
    pl.semaphore_wait(barrier, BPC - 1 + N_FREQ - 1)
    moves = []
    for j in range(BPC - 1, 0, -1):
        to = (here(DELTA[j], 1), q)
        rows = pl.ds(3 * j, 3)
        pairs = ((vis.at[0, j], cand_vis.at[j]), (coord.at[rows], cand_coord.at[rows]))
        for n, (src, dst) in enumerate(pairs):
            moves.append(
                pltpu.make_async_remote_copy(
                    src_ref=src,
                    dst_ref=dst,
                    send_sem=move_send.at[j, n],
                    recv_sem=move_recv.at[j, n],
                    device_id=to,
                    device_id_type=MESH,
                )
            )
            moves[-1].start()
    for delta in ((3, 0, 3), (3, 0, 1), (1, 0, 3)):
        tell(plane_sem, here(delta, 1), q)
    pl.semaphore_wait(plane_sem, 3)
    tell(near_sem, here((0, 1, 0), 1), q)
    for n in range(1, N_FREQ):
        tell(near_sem, *peers_of(n))
    pl.semaphore_wait(near_sem, N_FREQ)
    for n in range(1, N_FREQ):
        tell(all_sem, *peers_of(n))
    for c in own + args:
        c.wait()
    for c in moves:
        c.wait_recv()

    other = jnp.where(owners[0] == LAST, owners[1], owners[0]).astype(jnp.int32)
    there = around(other)
    place = lax.div(f, 4)

    def result_copy(n, facet):
        dst, sem, at = (from_a, recv_a, place) if n == 0 else (from_b, recv_b, last_rank)
        return pltpu.make_async_remote_copy(
            src_ref=res.at[n, facet],
            dst_ref=dst.at[at, q],
            send_sem=send_sem.at[n],
            recv_sem=sem.at[at] if n else sem,
            device_id=(facet, group),
            device_id_type=MESH,
        )

    def own_copy(n):
        dst, sem, at = (from_a, recv_a, place) if n == 0 else (from_b, recv_b, last_rank)
        return pltpu.make_async_copy(res.at[n, f], dst.at[at, q], sem.at[at] if n else sem)

    def send_all(n):
        for delta in SEND_ORDER:
            result_copy(n, here(delta, 1)).start()

        @pl.when(group != q)
        def _():
            result_copy(n, f).start()

        @pl.when(group == q)
        def _():
            own_copy(n).start()

    def drain(n):
        @pl.when(group != q)
        def _():
            pltpu.make_async_copy(res.at[n], res.at[n], send_sem.at[n]).wait()

        @pl.when(group == q)
        def _():
            sent = res.at[n, pl.ds(0, N_FACET - 1)]
            pltpu.make_async_copy(sent, sent, send_sem.at[n]).wait()

    def unit(n, carry):
        owner = jnp.where(n == 1, LAST, other)
        block = jnp.int32(0)
        for j in range(1, BPC):
            block = jnp.where(here(DELTA[j], -1) == owner, j, block)
        unit_products(
            q, block, cand_vis, cand_coord, corners[block, 0, owner], corners[block, 1, owner],
            xrow, pbuf, vbuf, acc,
        )

        def put(facet, part, value):
            res[n, facet, part * 8 : (part + 1) * 8, :] = value

        place_results(acc, turned, put)

        @pl.when(n == 0)
        def _():
            pl.semaphore_wait(all_sem, N_FREQ - 1)
            send_all(0)

        @pl.when(n == 1)
        def _():
            send_all(1)

        return carry

    lax.fori_loop(0, 1 + jnp.where(is_last, 1, 0), unit, 0)

    for c in moves:
        c.wait_send()
    prepare_image(q, owners, corners, assign, counts, other, table_t, pre, pim, br, bi)

    def share(got, at, size, part):
        rows, copies = pl.ds(at, size), []
        for n in (2, 1, 3):
            copies.append(
                pltpu.make_async_remote_copy(
                    src_ref=total.at[rows],
                    dst_ref=got.at[pl.ds(q * PER_SET + at % PER_SET, size)],
                    send_sem=peer_send.at[part, n],
                    recv_sem=peer_recv.at[part, n],
                    device_id=peers_of(n),
                    device_id_type=MESH,
                )
            )
            copies[-1].start()
        keep = pltpu.make_async_copy(
            total.at[rows], got.at[pl.ds(q * PER_SET + at % PER_SET, size)], peer_send.at[part, 0]
        )
        keep.start()
        return copies, keep

    def collect(got, shared, at, size, part):
        shared[1].wait()
        for n in range(1, N_FREQ):
            rows = pl.ds(lax.rem(q + N_FREQ - n, N_FREQ) * PER_SET + at % PER_SET, size)
            pltpu.make_async_copy(
                total.at[pl.ds(0, size)], got.at[rows], peer_recv.at[part, n]
            ).wait()

    pltpu.make_async_copy(from_a, from_a, recv_a).wait()
    wanted = lax.rem(q + N_FREQ - group_at(other), N_FREQ)
    for s in range(PER_SET):
        at = jnp.int32(0)
        for g in range(N_FREQ):
            j = MEMBERS[g][min(s, len(MEMBERS[g]) - 1)]
            at = jnp.where(wanted == g, lax.div(there(DELTA[j], 1), 4), at)
        total[s] = (from_a[at, 0] + from_a[at, 1]) + (from_a[at, 2] + from_a[at, 3])
    first = share(got_a, 0, PER_SET, 0)
    later = []
    wanted = lax.rem(q + N_FREQ - group_at(LAST), N_FREQ)
    for s in range(PER_SET):
        present = pick(wanted, [int(s < len(m)) for m in MEMBERS]) == 1

        @pl.when(present)
        def _():
            pltpu.make_async_copy(from_b.at[s], from_b.at[s], recv_b.at[s]).wait()
            total[PER_SET + s] = (from_b[s, 0] + from_b[s, 1]) + (from_b[s, 2] + from_b[s, 3])

        @pl.when(jnp.logical_not(present))
        def _():
            total[PER_SET + s] = jnp.zeros((16, 128), f32)

        later.append(share(got_b, PER_SET + s, 1, 1 + s))

    peers = first[0]
    collect(got_a, first, 0, PER_SET, 0)
    out[0] = image_part(0, q, other, got_a, table, pre, pim, br, bi, zr, zi)
    for s, shared in enumerate(later):
        peers = peers + shared[0]
        collect(got_b, shared, PER_SET + s, 1, 1 + s)
    out[0] = out[0] + image_part(1, q, other, got_b, table, pre, pim, br, bi, zr, zi)
    for p in peers:
        p.wait_send()
    drain(0)

    @pl.when(is_last)
    def _():
        drain(1)


def on_device(visibilities, coords, corners, owners, assign, counts):
    d, plain = image_table()
    scale = 1.0 / (SUB * SUB * math.sqrt(2 * BPC * BLK * CHANS))
    high = (d * scale).astype(bf16)
    low = (d * scale - high.astype(np.float64)).astype(bf16)
    vmem = pl.BlockSpec(memory_space=pltpu.VMEM)
    hbm = pl.BlockSpec(memory_space=pl.ANY)
    dma = pltpu.SemaphoreType.DMA
    return pl.pallas_call(
        fused_kernel,
        out_shape=pltpu.VMEM((1, G // N_FREQ, G), f32),
        in_specs=[hbm] * 8,
        out_specs=vmem,
        scratch_shapes=[
            pltpu.SMEM((2,), jnp.int32),
            pltpu.SMEM((BPC, 2, N_FACET), jnp.int32),
            pltpu.SMEM((1, 2 * BPC), jnp.int32),
            pltpu.SMEM((1,), jnp.int32),
            pltpu.VMEM((G, 3 * SUB), bf16),
            pltpu.VMEM((SUB, G), f32),
            pltpu.VMEM((BPC, 2, CH, BLK), f32),
            pltpu.VMEM((3 * BPC, 1, BLK), f32),
        ]
        + unit_scratch()
        + [
            pltpu.VMEM((2, N_FACET, 16, 128), f32),
            pltpu.VMEM((8, N_FREQ, 16, 128), f32),
            pltpu.VMEM((PER_SET, N_FREQ, 16, 128), f32),
            pltpu.VMEM((SLOTS, 16, 128), f32),
            pltpu.VMEM((N_FREQ * PER_SET, 16, 128), f32),
            pltpu.VMEM((N_FREQ * PER_SET, 16, 128), f32),
            pltpu.VMEM((2, 128, WIDE), f32),
            pltpu.VMEM((2, 128, WIDE), f32),
            pltpu.VMEM((2, 2, WIDE, G), bf16),
            pltpu.VMEM((2, 2, WIDE, G), bf16),
            pltpu.VMEM((32, WIDE), f32),
            pltpu.VMEM((32, WIDE), f32),
            pltpu.SemaphoreType.REGULAR,
            pltpu.SemaphoreType.REGULAR,
            pltpu.SemaphoreType.REGULAR,
            dma((6,)),
            dma((BPC, 2)),
            dma((BPC, 2)),
            dma((2,)),
            dma,
            dma((PER_SET,)),
            dma((1 + PER_SET, N_FREQ)),
            dma((1 + PER_SET, N_FREQ)),
        ],
        compiler_params=pltpu.CompilerParams(collective_id=0, has_side_effects=True),
        name="grid_and_image",
    )(
        visibilities,
        jnp.transpose(coords, (1, 2, 0, 3)).reshape(3 * BPC, 1, BLK),
        owners,
        jnp.transpose(corners, (2, 0, 1)),
        assign,
        counts,
        jnp.asarray(np.concatenate([high, high, low], axis=1)),
        jnp.asarray(plain.T, f32),
    )


def solution(mesh):
    placed = (
        P("facet", None, None, "freq", None),
        P("facet", None, None, None),
        P(),
        P(),
        P("facet", None),
        P("facet"),
    )
    return jax.shard_map(
        on_device, mesh=mesh, in_specs=placed, out_specs=P("facet", "freq", None), check_vma=False
    )
```

```python
import functools
import math

import jax
import jax.numpy as jnp
import numpy as np
from jax import lax
from jax.experimental import pallas as pl
from jax.experimental.pallas import tpu as pltpu
from jax.sharding import PartitionSpec as P

SUB = 32
G = 512
BPC = 10
CH = 32
N_FACET = 32
N_FREQ = 4
BLK = 128
CHANS = CH * N_FREQ
CHUNK = 16
LO = False
MESH = pl.DeviceIdType.MESH
f32 = jnp.float32
bf16 = jnp.bfloat16

DELTA = (
    (0, 0, 0),
    (1, 0, 0),
    (3, 0, 0),
    (0, 0, 1),
    (0, 0, 3),
    (1, 0, 1),
    (1, 0, 3),
    (3, 0, 1),
    (3, 0, 3),
    (0, 1, 0),
)
LAST = N_FACET - 1
PER_SET = 3
SLOTS = 2 * PER_SET
PADDED = 12
WIDE = PADDED * SUB


def fit_sincos():
    s = 0.125 * (1.0 - np.cos(np.pi * (np.arange(400) + 0.5) / 400))
    t = np.sqrt(s)
    poly = np.polynomial.chebyshev
    domain = [0.0, 0.25]
    c = poly.Chebyshev.fit(s, np.cos(2 * np.pi * t), 7, domain=domain)
    n = poly.Chebyshev.fit(s, np.sin(2 * np.pi * t) / t, 7, domain=domain)
    to_power = lambda p: p.convert(kind=np.polynomial.Polynomial).coef
    return [float(v) for v in to_power(c)], [float(v) for v in to_power(n)]


COS_POLY, SIN_POLY = fit_sincos()


def sincos(cycles):
    t = cycles - jnp.floor(cycles + 0.5)
    s = t * t
    c = jnp.full_like(s, COS_POLY[-1])
    for k in COS_POLY[-2::-1]:
        c = c * s + k
    n = jnp.full_like(s, SIN_POLY[-1])
    for k in SIN_POLY[-2::-1]:
        n = n * s + k
    return c, n * t


def cmul(a, b):
    return a[0] * b[0] - a[1] * b[1], a[0] * b[1] + a[1] * b[0]


def both(a, b):
    rr, ii, ri, ir = a[0] * b[0], a[1] * b[1], a[0] * b[1], a[1] * b[0]
    return (rr - ii, ri + ir), (rr + ii, ir - ri)


def image_table():
    x = np.arange(G) - G // 2
    l = np.arange(SUB) - SUB // 2
    n = np.arange(SUB) - SUB // 2
    theta = x[:, None] / G - l[None, :] / SUB
    kernel = np.exp(2j * np.pi * n[None, None, :] * theta[:, :, None]).sum(axis=2)
    real = (kernel * np.exp(1j * np.pi * theta)).real
    real = real * (1.0 - 0.8 * (l / (SUB / 2.0)) ** 2)[None, :]
    upper, lower = real[:, SUB // 2 :], real[:, SUB // 2 - 1 :: -1]
    even, odd = upper + lower, upper - lower
    plain = np.concatenate([even, odd], axis=1)
    table = np.zeros((G, SUB))
    for row in range(SUB):
        m, one, two, t = row // 8, (row // 4) % 2, (row // 2) % 2, row % 2
        for s1 in (1, -1):
            for s2 in (1, -1):
                place = int(8 + s1 * (4 + s2 * (m + 0.5)) - 0.5)
                sign = {
                    (0, 0, 0): 1, (0, 1, 1): -s2, (1, 0, 1): -s1 * s2, (1, 1, 0): -s1,
                    (1, 0, 0): 1, (1, 1, 1): -s2, (0, 1, 0): s1, (0, 0, 1): s1 * s2,
                }[(one, two, t)]
                table[:, row] += sign * ((odd if (one + two + t) % 2 else even)[:, place])
    return table, plain


def around(f):
    z, y, x = lax.div(f, 8), lax.rem(lax.div(f, 4), 2), lax.rem(f, 4)
    zs = [lax.rem(z + d, 4) * 8 for d in range(4)]
    ys = [lax.rem(y + d, 2) * 4 for d in range(2)]
    xs = [lax.rem(x + d, 4) for d in range(4)]

    def go(delta, sign):
        return zs[sign * delta[0] % 4] + ys[delta[1]] + xs[sign * delta[2] % 4]

    return go


def shifted_int(f, delta):
    return ((f // 8 + delta[0]) % 4) * 8 + ((f // 4 % 2 + delta[1]) % 2) * 4 + (f % 4 + delta[2]) % 4


def group_of(z, y, x):
    return (z + x + 2 * y) % N_FREQ


def group_at(f):
    if isinstance(f, int):
        return group_of(f // 8, f // 4 % 2, f % 4)
    return lax.rem(lax.div(f, 8) + lax.rem(f, 4) + 2 * lax.rem(lax.div(f, 4), 2), N_FREQ)


GROUP = tuple(group_of(*d) for d in DELTA)
MEMBERS = tuple(tuple(j for j in range(BPC) if GROUP[j] == g) for g in range(N_FREQ))
RANK = tuple(MEMBERS[GROUP[j]].index(j) for j in range(BPC))
def hops(delta):
    return min(delta[0], 4 - delta[0]) + 2 * delta[1] + min(delta[2], 4 - delta[2])


SEND_ORDER = tuple(
    sorted(
        ((n * 13 % 32 // 8, n * 13 % 32 // 4 % 2, n * 13 % 4) for n in range(1, N_FACET)),
        key=lambda d: -hops(d),
    )
)
LAST_POS = tuple(shifted_int(LAST, d) for d in DELTA)


def unit_products(q, block, cand_vis, cand_coord, ou, ov, xrow, pbuf, vbuf, acc):
    step = 0.02 / CHANS
    start = 1.0 + (step * CH) * q.astype(f32)
    u, v, w = cand_coord[3 * block], cand_coord[3 * block + 1], cand_coord[3 * block + 2]
    ou = 240.5 - ou.astype(f32)
    ov = 240.5 - ov.astype(f32)
    row = lax.broadcasted_iota(jnp.int32, (32, BLK), 0)

    def wave(d, corner, m, back=0.0):
        return sincos((d * start + corner) * m - back), sincos((d * step) * m)

    row8 = row[:8]
    x, x_turn = wave(
        u, ou, (2 * (row8 % 4) + 1).astype(f32) * (1.0 / 64.0), (row8 // 4).astype(f32) * 0.25
    )
    y, y_turn = wave(v, ov, (2 * row[:16] + 1).astype(f32) * (1.0 / 64.0))
    half, half_turn = wave(u, ou, jnp.full((8, BLK), 0.125, f32))
    a = (row % 8).astype(f32) - 3.5
    e = (row // 8).astype(f32) - 1.5
    rho = 0.0004 * (a * a + e * e)
    shift = -rho / (1.0 + jnp.sqrt(1.0 - rho))
    cycles = u * a + v * e + w * shift - (u + v) * (1.0 / 64.0)
    spin = sincos(cycles * start - (ou + ov) * (1.0 / 64.0))
    spin_turn = sincos(cycles * step)
    state = [x, y, half, spin]
    turns = [x_turn, y_turn, half_turn, spin_turn]
    rows4 = lambda t: jnp.concatenate([t] * 4, axis=0)

    def generate(c, slot, cc):
        x, y, half, spin = state
        xrow[slot, cc] = x[0]
        ys = jnp.concatenate(y, axis=0)
        for r in range(8):
            pbuf[slot, cc, r * 32 : (r + 1) * 32, :] = (
                jnp.broadcast_to(xrow[slot, cc, r : r + 1, :], (32, BLK)) * ys
            ).astype(bf16)
        re = jnp.broadcast_to(cand_vis[block, 0, c : c + 1, :], (32, BLK))
        im = jnp.broadcast_to(cand_vis[block, 1, c : c + 1, :], (32, BLK))
        rotated = cmul((re, im), spin)
        c2, s2 = half
        c1, s1 = c2 * c2 - s2 * s2, 2.0 * (c2 * s2)
        for n, factor in enumerate((c1 * c2, c1 * s2, s1 * c2, s1 * s2)):
            factor = rows4(factor)
            for part in range(2):
                value = rotated[part] * factor
                high = value.astype(bf16)
                at = n * 64 + part * 32
                vbuf[slot, cc, at : at + 32, :] = high
                if LO:
                    vbuf[slot, cc, 256 + at : 288 + at, :] = (value - high.astype(f32)).astype(bf16)
        for n in range(4):
            state[n] = cmul(state[n], turns[n])

    def multiply(k, slot):
        left = jnp.concatenate([vbuf[slot, cc] for cc in range(CHUNK)], axis=1)
        right = jnp.concatenate([pbuf[slot, cc] for cc in range(CHUNK)], axis=1)
        part = lax.dot_general(
            left, right, (((1,), (1,)), ((), ())), preferred_element_type=f32
        )
        acc[...] = part if k == 0 else acc[...] + part

    chunks = CH // CHUNK
    for k in range(chunks + 1):
        for cc in range(CHUNK):
            if k < chunks:
                generate(k * CHUNK + cc, k % 2, cc)
        if k > 0:
            multiply(k - 1, (k - 1) % 2)


def place_results(acc, turned, put):
    for n in range(4):
        for h in range(2):
            rows, lanes = slice(n * 64, (n + 1) * 64), slice(h * 128, (h + 1) * 128)
            value = acc[rows, lanes]
            if LO:
                value = value + acc[256 + n * 64 : 320 + n * 64, lanes]
            turned[(2 * n + h) * 64 : (2 * n + h + 1) * 64, :] = value
    for part in range(2):
        for facet in range(N_FACET):
            put(facet, part, turned[pl.ds(part * 32 + facet, 8, stride=64), :])


def unit_scratch():
    rows = 512 if LO else 256
    return [
        pltpu.VMEM((2, CHUNK, 8, BLK), f32),
        pltpu.VMEM((2, CHUNK, 256, BLK), bf16),
        pltpu.VMEM((2, CHUNK, rows, BLK), bf16),
        pltpu.VMEM((rows, 256), f32),
        pltpu.VMEM((512, 128), f32),
    ]


def pick(index, values):
    out = jnp.int32(values[0])
    for n, v in enumerate(values):
        if n:
            out = jnp.where(index == n, v, out)
    return out


def split(a):
    high = a.astype(bf16)
    return high, (a - high.astype(f32)).astype(bf16)


def dot3(a, b):
    dot = functools.partial(jnp.dot, preferred_element_type=f32)
    return dot(a[0], b[0]) + (dot(a[0], b[1]) + dot(a[1], b[0]))


def lanes_of(values):
    group = lax.broadcasted_iota(jnp.int32, (1, 128), 1) // 32
    tiles = []
    for tile in range(PADDED // 4):
        v = jnp.full((1, 128), values[tile * 4], jnp.int32)
        for g in range(1, 4):
            v = jnp.where(group == g, values[min(tile * 4 + g, BPC - 1)], v)
        tiles.append(v)
    return jnp.concatenate(tiles, axis=1)


def prepare_image(q, owners, corners, assign, counts, other, table_t, pre, pim, br, bi):
    first_last = owners[0] == LAST
    count = counts[0]
    k_of = lax.broadcasted_iota(jnp.int32, (1, WIDE), 1) // 32
    rows = q * 128 - 256 + lax.broadcasted_iota(jnp.int32, (128, WIDE), 0)
    columns = lax.broadcasted_iota(jnp.int32, (1, G), 1) - 256
    for part, owner in enumerate((other, LAST)):
        base = jnp.where(first_last, BPC, 0) if part == 0 else jnp.where(first_last, 0, BPC)
        block = jnp.where(k_of < BPC, base + k_of, -1)
        weight = jnp.zeros((1, WIDE), f32)
        for n in range(2 * BPC):
            live = jnp.where(n < count, 1.0, 0.0).astype(f32)
            weight = weight + jnp.where(block == assign[0, n], live, 0.0)
        corner_u = lanes_of([corners[j, 0, owner] for j in range(BPC)])
        turns = jnp.bitwise_and(rows * (2 * corner_u - 481), 1023)
        c, s = sincos(turns.astype(f32) * (1.0 / 1024.0))
        pre[part] = c * weight
        pim[part] = s * weight
        for k in range(BPC):
            turns = jnp.bitwise_and(columns * (2 * corners[k, 1, owner] - 481), 1023)
            c, s = sincos(turns.astype(f32) * (1.0 / 1024.0))
            for ref, value in ((br, table_t[...] * c), (bi, table_t[...] * -s)):
                high, low = split(value)
                ref[part, 0, k * 32 : (k + 1) * 32, :] = high
                ref[part, 1, k * 32 : (k + 1) * 32, :] = low
        for ref in (br, bi):
            for h in range(2):
                ref[part, h, BPC * 32 : WIDE, :] = jnp.zeros((WIDE - BPC * 32, G), bf16)


def image_part(part, q, other, got, table, pre, pim, br, bi, zr, zi):
    lane = lax.broadcasted_iota(jnp.int32, (8, 128), 1)
    sub = lax.broadcasted_iota(jnp.int32, (8, 128), 0)
    row_sine = (sub // 4 + (sub // 2) % 2 + sub % 2) % 2 == 1
    lane_sine = lane % 32 >= 16
    two = jnp.logical_and(row_sine, lane_sine)
    one = jnp.logical_and(jnp.logical_or(row_sine, lane_sine), jnp.logical_not(two))
    group = lane // 32
    home = group_at(other if part == 0 else LAST)
    nothing = jnp.zeros((8, 128), f32)
    for tile in range(PADDED // 4):
        parts = [[None] * 4, [None] * 4]
        for g in range(4):
            j = tile * 4 + g
            if j >= BPC:
                for i4 in range(4):
                    for p in range(2):
                        parts[p][i4] = jnp.where(group == g, nothing, parts[p][i4])
                continue
            block = got[((home + GROUP[j]) % N_FREQ if part else lax.rem(home + GROUP[j], N_FREQ)) * PER_SET + RANK[j]]
            re, im = block[:8], block[8:]
            new_re = jnp.where(one, -im, jnp.where(two, -re, re))
            new_im = jnp.where(one, re, jnp.where(two, -im, im))
            for i4 in range(4):
                shift = ((g - i4) * 32) % 128
                for p, value in enumerate((new_re, new_im)):
                    if shift:
                        value = pltpu.roll(value, shift, 1)
                    old = parts[p][i4]
                    parts[p][i4] = value if old is None else jnp.where(group == g, value, old)
        for i4 in range(4):
            zr[i4 * 8 : (i4 + 1) * 8, tile * 128 : (tile + 1) * 128] = parts[0][i4]
            zi[i4 * 8 : (i4 + 1) * 8, tile * 128 : (tile + 1) * 128] = parts[1][i4]
    d = table[pl.ds(pl.multiple_of(q * 128, 128), 128), :]

    def apply(z):
        high, low = split(z)
        return jnp.dot(
            d, jnp.concatenate([high, low, high], axis=0), preferred_element_type=f32
        )

    t_re, t_im = apply(zr[...]), apply(zi[...])
    l_re = t_re * pre[part] - t_im * pim[part]
    l_im = t_re * pim[part] + t_im * pre[part]
    return dot3(split(l_re), (br[part, 0], br[part, 1])) + dot3(
        split(l_im), (bi[part, 0], bi[part, 1])
    )


def fused_kernel(
    vis, coord, owners_in, corners_in, assign_in, counts_in, table_in, table_t_in, out,
    owners, corners, assign, counts, table, table_t,
    cand_vis, cand_coord, xrow, pbuf, vbuf, acc, turned, res, from_a, from_b, total, got_a, got_b,
    pre, pim, br, bi, zr, zi,
    plane_sem, near_sem, all_sem, args_sem, move_send, move_recv, send_sem, recv_a, recv_b, peer_send, peer_recv,
):
    f = lax.axis_index("facet")
    q = lax.axis_index("freq")
    here = around(f)
    group = group_at(f)
    last_block = jnp.int32(-1)
    for j in range(BPC):
        last_block = jnp.where(f == LAST_POS[j], j, last_block)
    is_last = last_block >= 0
    last_rank = pick(last_block, RANK)
    barrier = pltpu.get_barrier_semaphore()

    def signal(facet, freq):
        pl.semaphore_signal(barrier, inc=1, device_id=(facet, freq), device_id_type=MESH)

    def peers_of(n):
        return (f, lax.rem(q + n, N_FREQ))

    for j in range(1, BPC):
        signal(here(DELTA[j], -1), q)
    for n in range(1, N_FREQ):
        signal(*peers_of(n))

    def tell(sem, facet, freq):
        pl.semaphore_signal(sem, inc=1, device_id=(facet, freq), device_id_type=MESH)

    args = [
        pltpu.make_async_copy(src, dst, args_sem.at[n])
        for n, (src, dst) in enumerate(
            (
                (owners_in, owners),
                (corners_in, corners),
                (assign_in, assign),
                (counts_in, counts),
                (table_in, table),
                (table_t_in, table_t),
            )
        )
    ]
    own = [
        pltpu.make_async_copy(vis.at[0, 0], cand_vis.at[0], move_recv.at[0, 0]),
        pltpu.make_async_copy(coord.at[pl.ds(0, 3)], cand_coord.at[pl.ds(0, 3)], move_recv.at[0, 1]),
    ]
    for c in own + args:
        c.start()
    pl.semaphore_wait(barrier, BPC - 1 + N_FREQ - 1)
    moves = []
    for j in range(BPC - 1, 0, -1):
        to = (here(DELTA[j], 1), q)
        rows = pl.ds(3 * j, 3)
        pairs = ((vis.at[0, j], cand_vis.at[j]), (coord.at[rows], cand_coord.at[rows]))
        for n, (src, dst) in enumerate(pairs):
            moves.append(
                pltpu.make_async_remote_copy(
                    src_ref=src,
                    dst_ref=dst,
                    send_sem=move_send.at[j, n],
                    recv_sem=move_recv.at[j, n],
                    device_id=to,
                    device_id_type=MESH,
                )
            )
            moves[-1].start()
    for delta in ((3, 0, 3), (3, 0, 1), (1, 0, 3)):
        tell(plane_sem, here(delta, 1), q)
    pl.semaphore_wait(plane_sem, 3)
    tell(near_sem, here((0, 1, 0), 1), q)
    for n in range(1, N_FREQ):
        tell(near_sem, *peers_of(n))
    pl.semaphore_wait(near_sem, N_FREQ)
    for n in range(1, N_FREQ):
        tell(all_sem, *peers_of(n))
    for c in own + args:
        c.wait()
    for c in moves:
        c.wait_recv()

    other = jnp.where(owners[0] == LAST, owners[1], owners[0]).astype(jnp.int32)
    there = around(other)
    place = lax.div(f, 4)

    def result_copy(n, facet):
        dst, sem, at = (from_a, recv_a, place) if n == 0 else (from_b, recv_b, last_rank)
        return pltpu.make_async_remote_copy(
            src_ref=res.at[n, facet],
            dst_ref=dst.at[at, q],
            send_sem=send_sem.at[n],
            recv_sem=sem.at[at] if n else sem,
            device_id=(facet, group),
            device_id_type=MESH,
        )

    def own_copy(n):
        dst, sem, at = (from_a, recv_a, place) if n == 0 else (from_b, recv_b, last_rank)
        return pltpu.make_async_copy(res.at[n, f], dst.at[at, q], sem.at[at] if n else sem)

    def send_all(n):
        for delta in SEND_ORDER:
            result_copy(n, here(delta, 1)).start()

        @pl.when(group != q)
        def _():
            result_copy(n, f).start()

        @pl.when(group == q)
        def _():
            own_copy(n).start()

    def drain(n):
        @pl.when(group != q)
        def _():
            pltpu.make_async_copy(res.at[n], res.at[n], send_sem.at[n]).wait()

        @pl.when(group == q)
        def _():
            sent = res.at[n, pl.ds(0, N_FACET - 1)]
            pltpu.make_async_copy(sent, sent, send_sem.at[n]).wait()

    def unit(n, carry):
        owner = jnp.where(n == 1, LAST, other)
        block = jnp.int32(0)
        for j in range(1, BPC):
            block = jnp.where(here(DELTA[j], -1) == owner, j, block)
        unit_products(
            q, block, cand_vis, cand_coord, corners[block, 0, owner], corners[block, 1, owner],
            xrow, pbuf, vbuf, acc,
        )

        def put(facet, part, value):
            res[n, facet, part * 8 : (part + 1) * 8, :] = value

        place_results(acc, turned, put)

        @pl.when(n == 0)
        def _():
            pl.semaphore_wait(all_sem, N_FREQ - 1)
            send_all(0)

        @pl.when(n == 1)
        def _():
            send_all(1)

        return carry

    lax.fori_loop(0, 1 + jnp.where(is_last, 1, 0), unit, 0)

    for c in moves:
        c.wait_send()
    prepare_image(q, owners, corners, assign, counts, other, table_t, pre, pim, br, bi)

    def share(got, at, size, part):
        rows, copies = pl.ds(at, size), []
        for n in (2, 1, 3):
            copies.append(
                pltpu.make_async_remote_copy(
                    src_ref=total.at[rows],
                    dst_ref=got.at[pl.ds(q * PER_SET + at % PER_SET, size)],
                    send_sem=peer_send.at[part, n],
                    recv_sem=peer_recv.at[part, n],
                    device_id=peers_of(n),
                    device_id_type=MESH,
                )
            )
            copies[-1].start()
        keep = pltpu.make_async_copy(
            total.at[rows], got.at[pl.ds(q * PER_SET + at % PER_SET, size)], peer_send.at[part, 0]
        )
        keep.start()
        return copies, keep

    def collect(got, shared, at, size, part):
        shared[1].wait()
        for n in range(1, N_FREQ):
            rows = pl.ds(lax.rem(q + N_FREQ - n, N_FREQ) * PER_SET + at % PER_SET, size)
            pltpu.make_async_copy(
                total.at[pl.ds(0, size)], got.at[rows], peer_recv.at[part, n]
            ).wait()

    pltpu.make_async_copy(from_a, from_a, recv_a).wait()
    wanted = lax.rem(q + N_FREQ - group_at(other), N_FREQ)
    for s in range(PER_SET):
        at = jnp.int32(0)
        for g in range(N_FREQ):
            j = MEMBERS[g][min(s, len(MEMBERS[g]) - 1)]
            at = jnp.where(wanted == g, lax.div(there(DELTA[j], 1), 4), at)
        total[s] = (from_a[at, 0] + from_a[at, 1]) + (from_a[at, 2] + from_a[at, 3])
    first = share(got_a, 0, PER_SET, 0)
    later = []
    wanted = lax.rem(q + N_FREQ - group_at(LAST), N_FREQ)
    for s in range(PER_SET):
        present = pick(wanted, [int(s < len(m)) for m in MEMBERS]) == 1

        @pl.when(present)
        def _():
            pltpu.make_async_copy(from_b.at[s], from_b.at[s], recv_b.at[s]).wait()
            total[PER_SET + s] = (from_b[s, 0] + from_b[s, 1]) + (from_b[s, 2] + from_b[s, 3])

        @pl.when(jnp.logical_not(present))
        def _():
            total[PER_SET + s] = jnp.zeros((16, 128), f32)

        later.append(share(got_b, PER_SET + s, 1, 1 + s))

    peers = first[0]
    collect(got_a, first, 0, PER_SET, 0)
    out[0] = image_part(0, q, other, got_a, table, pre, pim, br, bi, zr, zi)
    for s, shared in enumerate(later):
        peers = peers + shared[0]
        collect(got_b, shared, PER_SET + s, 1, 1 + s)
    out[0] = out[0] + image_part(1, q, other, got_b, table, pre, pim, br, bi, zr, zi)
    for p in peers:
        p.wait_send()
    drain(0)

    @pl.when(is_last)
    def _():
        drain(1)


def on_device(visibilities, coords, corners, owners, assign, counts):
    d, plain = image_table()
    scale = 1.0 / (SUB * SUB * math.sqrt(2 * BPC * BLK * CHANS))
    high = (d * scale).astype(bf16)
    low = (d * scale - high.astype(np.float64)).astype(bf16)
    vmem = pl.BlockSpec(memory_space=pltpu.VMEM)
    hbm = pl.BlockSpec(memory_space=pl.ANY)
    dma = pltpu.SemaphoreType.DMA
    return pl.pallas_call(
        fused_kernel,
        out_shape=pltpu.VMEM((1, G // N_FREQ, G), f32),
        in_specs=[hbm] * 8,
        out_specs=vmem,
        scratch_shapes=[
            pltpu.SMEM((2,), jnp.int32),
            pltpu.SMEM((BPC, 2, N_FACET), jnp.int32),
            pltpu.SMEM((1, 2 * BPC), jnp.int32),
            pltpu.SMEM((1,), jnp.int32),
            pltpu.VMEM((G, 3 * SUB), bf16),
            pltpu.VMEM((SUB, G), f32),
            pltpu.VMEM((BPC, 2, CH, BLK), f32),
            pltpu.VMEM((3 * BPC, 1, BLK), f32),
        ]
        + unit_scratch()
        + [
            pltpu.VMEM((2, N_FACET, 16, 128), f32),
            pltpu.VMEM((8, N_FREQ, 16, 128), f32),
            pltpu.VMEM((PER_SET, N_FREQ, 16, 128), f32),
            pltpu.VMEM((SLOTS, 16, 128), f32),
            pltpu.VMEM((N_FREQ * PER_SET, 16, 128), f32),
            pltpu.VMEM((N_FREQ * PER_SET, 16, 128), f32),
            pltpu.VMEM((2, 128, WIDE), f32),
            pltpu.VMEM((2, 128, WIDE), f32),
            pltpu.VMEM((2, 2, WIDE, G), bf16),
            pltpu.VMEM((2, 2, WIDE, G), bf16),
            pltpu.VMEM((32, WIDE), f32),
            pltpu.VMEM((32, WIDE), f32),
            pltpu.SemaphoreType.REGULAR,
            pltpu.SemaphoreType.REGULAR,
            pltpu.SemaphoreType.REGULAR,
            dma((6,)),
            dma((BPC, 2)),
            dma((BPC, 2)),
            dma((2,)),
            dma,
            dma((PER_SET,)),
            dma((1 + PER_SET, N_FREQ)),
            dma((1 + PER_SET, N_FREQ)),
        ],
        compiler_params=pltpu.CompilerParams(collective_id=0, has_side_effects=True),
        name="grid_and_image",
    )(
        visibilities,
        jnp.transpose(coords, (1, 2, 0, 3)).reshape(3 * BPC, 1, BLK),
        owners,
        jnp.transpose(corners, (2, 0, 1)),
        assign,
        counts,
        jnp.asarray(np.concatenate([high, high, low], axis=1)),
        jnp.asarray(plain.T, f32),
    )


def solution(mesh):
    placed = (
        P("facet", None, None, "freq", None),
        P("facet", None, None, None),
        P(),
        P(),
        P("facet", None),
        P("facet"),
    )
    return jax.shard_map(
        on_device, mesh=mesh, in_specs=placed, out_specs=P("facet", "freq", None), check_vma=False
    )
```

```python
import functools
import math

import jax
import jax.numpy as jnp
import numpy as np
from jax import lax
from jax.experimental import pallas as pl
from jax.experimental.pallas import tpu as pltpu
from jax.sharding import PartitionSpec as P

SUB = 32
G = 512
BPC = 10
CH = 32
N_FACET = 32
N_FREQ = 4
BLK = 128
CHANS = CH * N_FREQ
CHUNK = 16
LO = False
MESH = pl.DeviceIdType.MESH
f32 = jnp.float32
bf16 = jnp.bfloat16

DELTA = (
    (0, 0, 0),
    (1, 0, 0),
    (3, 0, 0),
    (0, 0, 1),
    (0, 0, 3),
    (1, 0, 1),
    (1, 0, 3),
    (3, 0, 1),
    (3, 0, 3),
    (0, 1, 0),
)
LAST = N_FACET - 1
PER_SET = 3
SLOTS = 2 * PER_SET
PADDED = 12
WIDE = PADDED * SUB


def fit_sincos():
    s = 0.125 * (1.0 - np.cos(np.pi * (np.arange(400) + 0.5) / 400))
    t = np.sqrt(s)
    poly = np.polynomial.chebyshev
    domain = [0.0, 0.25]
    c = poly.Chebyshev.fit(s, np.cos(2 * np.pi * t), 7, domain=domain)
    n = poly.Chebyshev.fit(s, np.sin(2 * np.pi * t) / t, 7, domain=domain)
    to_power = lambda p: p.convert(kind=np.polynomial.Polynomial).coef
    return [float(v) for v in to_power(c)], [float(v) for v in to_power(n)]


COS_POLY, SIN_POLY = fit_sincos()


def sincos(cycles):
    t = cycles - jnp.floor(cycles + 0.5)
    s = t * t
    c = jnp.full_like(s, COS_POLY[-1])
    for k in COS_POLY[-2::-1]:
        c = c * s + k
    n = jnp.full_like(s, SIN_POLY[-1])
    for k in SIN_POLY[-2::-1]:
        n = n * s + k
    return c, n * t


def cmul(a, b):
    return a[0] * b[0] - a[1] * b[1], a[0] * b[1] + a[1] * b[0]


def both(a, b):
    rr, ii, ri, ir = a[0] * b[0], a[1] * b[1], a[0] * b[1], a[1] * b[0]
    return (rr - ii, ri + ir), (rr + ii, ir - ri)


def image_table():
    x = np.arange(G) - G // 2
    l = np.arange(SUB) - SUB // 2
    n = np.arange(SUB) - SUB // 2
    theta = x[:, None] / G - l[None, :] / SUB
    kernel = np.exp(2j * np.pi * n[None, None, :] * theta[:, :, None]).sum(axis=2)
    real = (kernel * np.exp(1j * np.pi * theta)).real
    real = real * (1.0 - 0.8 * (l / (SUB / 2.0)) ** 2)[None, :]
    upper, lower = real[:, SUB // 2 :], real[:, SUB // 2 - 1 :: -1]
    even, odd = upper + lower, upper - lower
    plain = np.concatenate([even, odd], axis=1)
    table = np.zeros((G, SUB))
    for row in range(SUB):
        m, one, two, t = row // 8, (row // 4) % 2, (row // 2) % 2, row % 2
        for s1 in (1, -1):
            for s2 in (1, -1):
                place = int(8 + s1 * (4 + s2 * (m + 0.5)) - 0.5)
                sign = {
                    (0, 0, 0): 1, (0, 1, 1): -s2, (1, 0, 1): -s1 * s2, (1, 1, 0): -s1,
                    (1, 0, 0): 1, (1, 1, 1): -s2, (0, 1, 0): s1, (0, 0, 1): s1 * s2,
                }[(one, two, t)]
                table[:, row] += sign * ((odd if (one + two + t) % 2 else even)[:, place])
    return table, plain


def around(f):
    z, y, x = lax.div(f, 8), lax.rem(lax.div(f, 4), 2), lax.rem(f, 4)
    zs = [lax.rem(z + d, 4) * 8 for d in range(4)]
    ys = [lax.rem(y + d, 2) * 4 for d in range(2)]
    xs = [lax.rem(x + d, 4) for d in range(4)]

    def go(delta, sign):
        return zs[sign * delta[0] % 4] + ys[delta[1]] + xs[sign * delta[2] % 4]

    return go


def shifted_int(f, delta):
    return ((f // 8 + delta[0]) % 4) * 8 + ((f // 4 % 2 + delta[1]) % 2) * 4 + (f % 4 + delta[2]) % 4


def group_of(z, y, x):
    return (z + x + 2 * y) % N_FREQ


def group_at(f):
    if isinstance(f, int):
        return group_of(f // 8, f // 4 % 2, f % 4)
    return lax.rem(lax.div(f, 8) + lax.rem(f, 4) + 2 * lax.rem(lax.div(f, 4), 2), N_FREQ)


GROUP = tuple(group_of(*d) for d in DELTA)
MEMBERS = tuple(tuple(j for j in range(BPC) if GROUP[j] == g) for g in range(N_FREQ))
RANK = tuple(MEMBERS[GROUP[j]].index(j) for j in range(BPC))
def hops(delta):
    return min(delta[0], 4 - delta[0]) + 2 * delta[1] + min(delta[2], 4 - delta[2])


SEND_ORDER = tuple(
    sorted(
        ((n * 13 % 32 // 8, n * 13 % 32 // 4 % 2, n * 13 % 4) for n in range(1, N_FACET)),
        key=lambda d: -hops(d),
    )
)
LAST_POS = tuple(shifted_int(LAST, d) for d in DELTA)


def unit_products(q, block, cand_vis, cand_coord, ou, ov, xrow, pbuf, vbuf, acc):
    step = 0.02 / CHANS
    start = 1.0 + (step * CH) * q.astype(f32)
    u, v, w = cand_coord[3 * block], cand_coord[3 * block + 1], cand_coord[3 * block + 2]
    ou = 240.5 - ou.astype(f32)
    ov = 240.5 - ov.astype(f32)
    row = lax.broadcasted_iota(jnp.int32, (32, BLK), 0)

    def wave(d, corner, m, back=0.0):
        return sincos((d * start + corner) * m - back), sincos((d * step) * m)

    row8 = row[:8]
    x, x_turn = wave(
        u, ou, (2 * (row8 % 4) + 1).astype(f32) * (1.0 / 64.0), (row8 // 4).astype(f32) * 0.25
    )
    y, y_turn = wave(v, ov, (2 * row[:16] + 1).astype(f32) * (1.0 / 64.0))
    half, half_turn = wave(u, ou, jnp.full((8, BLK), 0.125, f32))
    a = (row % 8).astype(f32) - 3.5
    e = (row // 8).astype(f32) - 1.5
    rho = 0.0004 * (a * a + e * e)
    shift = -rho / (1.0 + jnp.sqrt(1.0 - rho))
    cycles = u * a + v * e + w * shift - (u + v) * (1.0 / 64.0)
    spin = sincos(cycles * start - (ou + ov) * (1.0 / 64.0))
    spin_turn = sincos(cycles * step)
    state = [x, y, half, spin]
    turns = [x_turn, y_turn, half_turn, spin_turn]
    rows4 = lambda t: jnp.concatenate([t] * 4, axis=0)

    def generate(c, slot, cc):
        x, y, half, spin = state
        xrow[slot, cc] = x[0]
        ys = jnp.concatenate(y, axis=0)
        for r in range(8):
            pbuf[slot, cc, r * 32 : (r + 1) * 32, :] = (
                jnp.broadcast_to(xrow[slot, cc, r : r + 1, :], (32, BLK)) * ys
            ).astype(bf16)
        re = jnp.broadcast_to(cand_vis[block, 0, c : c + 1, :], (32, BLK))
        im = jnp.broadcast_to(cand_vis[block, 1, c : c + 1, :], (32, BLK))
        rotated = cmul((re, im), spin)
        c2, s2 = half
        c1, s1 = c2 * c2 - s2 * s2, 2.0 * (c2 * s2)
        for n, factor in enumerate((c1 * c2, c1 * s2, s1 * c2, s1 * s2)):
            factor = rows4(factor)
            for part in range(2):
                value = rotated[part] * factor
                high = value.astype(bf16)
                at = n * 64 + part * 32
                vbuf[slot, cc, at : at + 32, :] = high
                if LO:
                    vbuf[slot, cc, 256 + at : 288 + at, :] = (value - high.astype(f32)).astype(bf16)
        for n in range(4):
            state[n] = cmul(state[n], turns[n])

    def multiply(k, slot):
        left = jnp.concatenate([vbuf[slot, cc] for cc in range(CHUNK)], axis=1)
        right = jnp.concatenate([pbuf[slot, cc] for cc in range(CHUNK)], axis=1)
        part = lax.dot_general(
            left, right, (((1,), (1,)), ((), ())), preferred_element_type=f32
        )
        acc[...] = part if k == 0 else acc[...] + part

    chunks = CH // CHUNK
    for k in range(chunks + 1):
        for cc in range(CHUNK):
            if k < chunks:
                generate(k * CHUNK + cc, k % 2, cc)
        if k > 0:
            multiply(k - 1, (k - 1) % 2)


def place_results(acc, turned, put):
    for n in range(4):
        for h in range(2):
            rows, lanes = slice(n * 64, (n + 1) * 64), slice(h * 128, (h + 1) * 128)
            value = acc[rows, lanes]
            if LO:
                value = value + acc[256 + n * 64 : 320 + n * 64, lanes]
            turned[(2 * n + h) * 64 : (2 * n + h + 1) * 64, :] = value
    for part in range(2):
        for facet in range(N_FACET):
            put(facet, part, turned[pl.ds(part * 32 + facet, 8, stride=64), :])


def unit_scratch():
    rows = 512 if LO else 256
    return [
        pltpu.VMEM((2, CHUNK, 8, BLK), f32),
        pltpu.VMEM((2, CHUNK, 256, BLK), bf16),
        pltpu.VMEM((2, CHUNK, rows, BLK), bf16),
        pltpu.VMEM((rows, 256), f32),
        pltpu.VMEM((512, 128), f32),
    ]


def pick(index, values):
    out = jnp.int32(values[0])
    for n, v in enumerate(values):
        if n:
            out = jnp.where(index == n, v, out)
    return out


def split(a):
    high = a.astype(bf16)
    return high, (a - high.astype(f32)).astype(bf16)


def dot3(a, b):
    dot = functools.partial(jnp.dot, preferred_element_type=f32)
    return dot(a[0], b[0]) + (dot(a[0], b[1]) + dot(a[1], b[0]))


def lanes_of(values):
    group = lax.broadcasted_iota(jnp.int32, (1, 128), 1) // 32
    tiles = []
    for tile in range(PADDED // 4):
        v = jnp.full((1, 128), values[tile * 4], jnp.int32)
        for g in range(1, 4):
            v = jnp.where(group == g, values[min(tile * 4 + g, BPC - 1)], v)
        tiles.append(v)
    return jnp.concatenate(tiles, axis=1)


def prepare_image(q, owners, corners, assign, counts, other, table_t, pre, pim, br, bi):
    first_last = owners[0] == LAST
    count = counts[0]
    k_of = lax.broadcasted_iota(jnp.int32, (1, WIDE), 1) // 32
    rows = q * 128 - 256 + lax.broadcasted_iota(jnp.int32, (128, WIDE), 0)
    columns = lax.broadcasted_iota(jnp.int32, (1, G), 1) - 256
    for part, owner in enumerate((other, LAST)):
        base = jnp.where(first_last, BPC, 0) if part == 0 else jnp.where(first_last, 0, BPC)
        block = jnp.where(k_of < BPC, base + k_of, -1)
        weight = jnp.zeros((1, WIDE), f32)
        for n in range(2 * BPC):
            live = jnp.where(n < count, 1.0, 0.0).astype(f32)
            weight = weight + jnp.where(block == assign[0, n], live, 0.0)
        corner_u = lanes_of([corners[j, 0, owner] for j in range(BPC)])
        turns = jnp.bitwise_and(rows * (2 * corner_u - 481), 1023)
        c, s = sincos(turns.astype(f32) * (1.0 / 1024.0))
        pre[part] = c * weight
        pim[part] = s * weight
        for k in range(BPC):
            turns = jnp.bitwise_and(columns * (2 * corners[k, 1, owner] - 481), 1023)
            c, s = sincos(turns.astype(f32) * (1.0 / 1024.0))
            for ref, value in ((br, table_t[...] * c), (bi, table_t[...] * -s)):
                high, low = split(value)
                ref[part, 0, k * 32 : (k + 1) * 32, :] = high
                ref[part, 1, k * 32 : (k + 1) * 32, :] = low
        for ref in (br, bi):
            for h in range(2):
                ref[part, h, BPC * 32 : WIDE, :] = jnp.zeros((WIDE - BPC * 32, G), bf16)


def image_part(part, q, other, got, table, pre, pim, br, bi, zr, zi):
    lane = lax.broadcasted_iota(jnp.int32, (8, 128), 1)
    sub = lax.broadcasted_iota(jnp.int32, (8, 128), 0)
    row_sine = (sub // 4 + (sub // 2) % 2 + sub % 2) % 2 == 1
    lane_sine = lane % 32 >= 16
    two = jnp.logical_and(row_sine, lane_sine)
    one = jnp.logical_and(jnp.logical_or(row_sine, lane_sine), jnp.logical_not(two))
    group = lane // 32
    home = group_at(other if part == 0 else LAST)
    nothing = jnp.zeros((8, 128), f32)
    for tile in range(PADDED // 4):
        parts = [[None] * 4, [None] * 4]
        for g in range(4):
            j = tile * 4 + g
            if j >= BPC:
                for i4 in range(4):
                    for p in range(2):
                        parts[p][i4] = jnp.where(group == g, nothing, parts[p][i4])
                continue
            block = got[((home + GROUP[j]) % N_FREQ if part else lax.rem(home + GROUP[j], N_FREQ)) * PER_SET + RANK[j]]
            re, im = block[:8], block[8:]
            new_re = jnp.where(one, -im, jnp.where(two, -re, re))
            new_im = jnp.where(one, re, jnp.where(two, -im, im))
            for i4 in range(4):
                shift = ((g - i4) * 32) % 128
                for p, value in enumerate((new_re, new_im)):
                    if shift:
                        value = pltpu.roll(value, shift, 1)
                    old = parts[p][i4]
                    parts[p][i4] = value if old is None else jnp.where(group == g, value, old)
        for i4 in range(4):
            zr[i4 * 8 : (i4 + 1) * 8, tile * 128 : (tile + 1) * 128] = parts[0][i4]
            zi[i4 * 8 : (i4 + 1) * 8, tile * 128 : (tile + 1) * 128] = parts[1][i4]
    d = table[pl.ds(pl.multiple_of(q * 128, 128), 128), :]

    def apply(z):
        high, low = split(z)
        return jnp.dot(
            d, jnp.concatenate([high, low, high], axis=0), preferred_element_type=f32
        )

    t_re, t_im = apply(zr[...]), apply(zi[...])
    l_re = t_re * pre[part] - t_im * pim[part]
    l_im = t_re * pim[part] + t_im * pre[part]
    return dot3(split(l_re), (br[part, 0], br[part, 1])) + dot3(
        split(l_im), (bi[part, 0], bi[part, 1])
    )


def fused_kernel(
    vis, coord, owners_in, corners_in, assign_in, counts_in, table_in, table_t_in, out,
    owners, corners, assign, counts, table, table_t,
    cand_vis, cand_coord, xrow, pbuf, vbuf, acc, turned, res, from_a, from_b, total, got_a, got_b,
    pre, pim, br, bi, zr, zi,
    plane_sem, near_sem, all_sem, args_sem, move_send, move_recv, send_sem, recv_a, recv_b, peer_send, peer_recv,
):
    f = lax.axis_index("facet")
    q = lax.axis_index("freq")
    here = around(f)
    group = group_at(f)
    last_block = jnp.int32(-1)
    for j in range(BPC):
        last_block = jnp.where(f == LAST_POS[j], j, last_block)
    is_last = last_block >= 0
    last_rank = pick(last_block, RANK)
    barrier = pltpu.get_barrier_semaphore()

    def signal(facet, freq):
        pl.semaphore_signal(barrier, inc=1, device_id=(facet, freq), device_id_type=MESH)

    def peers_of(n):
        return (f, lax.rem(q + n, N_FREQ))

    for j in range(BPC - 1, 0, -1):
        signal(here(DELTA[j], -1), q)
    for n in range(1, N_FREQ):
        signal(*peers_of(n))

    def tell(sem, facet, freq):
        pl.semaphore_signal(sem, inc=1, device_id=(facet, freq), device_id_type=MESH)

    args = [
        pltpu.make_async_copy(src, dst, args_sem.at[n])
        for n, (src, dst) in enumerate(
            (
                (owners_in, owners),
                (corners_in, corners),
                (assign_in, assign),
                (counts_in, counts),
                (table_in, table),
                (table_t_in, table_t),
            )
        )
    ]
    own = [
        pltpu.make_async_copy(vis.at[0, 0], cand_vis.at[0], move_recv.at[0, 0]),
        pltpu.make_async_copy(coord.at[pl.ds(0, 3)], cand_coord.at[pl.ds(0, 3)], move_recv.at[0, 1]),
    ]
    for c in own + args:
        c.start()
    pl.semaphore_wait(barrier, BPC - 1 + N_FREQ - 1)
    moves = []
    for j in range(BPC - 1, 0, -1):
        to = (here(DELTA[j], 1), q)
        rows = pl.ds(3 * j, 3)
        pairs = ((vis.at[0, j], cand_vis.at[j]), (coord.at[rows], cand_coord.at[rows]))
        for n, (src, dst) in enumerate(pairs):
            moves.append(
                pltpu.make_async_remote_copy(
                    src_ref=src,
                    dst_ref=dst,
                    send_sem=move_send.at[j, n],
                    recv_sem=move_recv.at[j, n],
                    device_id=to,
                    device_id_type=MESH,
                )
            )
            moves[-1].start()
    for delta in ((3, 0, 3), (3, 0, 1), (1, 0, 3)):
        tell(plane_sem, here(delta, 1), q)
    pl.semaphore_wait(plane_sem, 3)
    tell(near_sem, here((0, 1, 0), 1), q)
    for n in range(1, N_FREQ):
        tell(near_sem, *peers_of(n))
    pl.semaphore_wait(near_sem, N_FREQ)
    for n in range(1, N_FREQ):
        tell(all_sem, *peers_of(n))
    for c in own + args:
        c.wait()
    for c in moves:
        c.wait_recv()

    other = jnp.where(owners[0] == LAST, owners[1], owners[0]).astype(jnp.int32)
    there = around(other)
    place = lax.div(f, 4)

    def result_copy(n, facet):
        dst, sem, at = (from_a, recv_a, place) if n == 0 else (from_b, recv_b, last_rank)
        return pltpu.make_async_remote_copy(
            src_ref=res.at[n, facet],
            dst_ref=dst.at[at, q],
            send_sem=send_sem.at[n],
            recv_sem=sem.at[at] if n else sem,
            device_id=(facet, group),
            device_id_type=MESH,
        )

    def own_copy(n):
        dst, sem, at = (from_a, recv_a, place) if n == 0 else (from_b, recv_b, last_rank)
        return pltpu.make_async_copy(res.at[n, f], dst.at[at, q], sem.at[at] if n else sem)

    def send_all(n):
        for delta in SEND_ORDER:
            result_copy(n, here(delta, 1)).start()

        @pl.when(group != q)
        def _():
            result_copy(n, f).start()

        @pl.when(group == q)
        def _():
            own_copy(n).start()

    def drain(n):
        @pl.when(group != q)
        def _():
            pltpu.make_async_copy(res.at[n], res.at[n], send_sem.at[n]).wait()

        @pl.when(group == q)
        def _():
            sent = res.at[n, pl.ds(0, N_FACET - 1)]
            pltpu.make_async_copy(sent, sent, send_sem.at[n]).wait()

    def unit(n, carry):
        owner = jnp.where(n == 1, LAST, other)
        block = jnp.int32(0)
        for j in range(1, BPC):
            block = jnp.where(here(DELTA[j], -1) == owner, j, block)
        unit_products(
            q, block, cand_vis, cand_coord, corners[block, 0, owner], corners[block, 1, owner],
            xrow, pbuf, vbuf, acc,
        )

        def put(facet, part, value):
            res[n, facet, part * 8 : (part + 1) * 8, :] = value

        place_results(acc, turned, put)

        @pl.when(n == 0)
        def _():
            pl.semaphore_wait(all_sem, N_FREQ - 1)
            send_all(0)

        @pl.when(n == 1)
        def _():
            send_all(1)

        return carry

    lax.fori_loop(0, 1 + jnp.where(is_last, 1, 0), unit, 0)

    for c in moves:
        c.wait_send()
    prepare_image(q, owners, corners, assign, counts, other, table_t, pre, pim, br, bi)

    def share(got, at, size, part):
        rows, copies = pl.ds(at, size), []
        for n in (2, 1, 3):
            copies.append(
                pltpu.make_async_remote_copy(
                    src_ref=total.at[rows],
                    dst_ref=got.at[pl.ds(q * PER_SET + at % PER_SET, size)],
                    send_sem=peer_send.at[part, n],
                    recv_sem=peer_recv.at[part, n],
                    device_id=peers_of(n),
                    device_id_type=MESH,
                )
            )
            copies[-1].start()
        keep = pltpu.make_async_copy(
            total.at[rows], got.at[pl.ds(q * PER_SET + at % PER_SET, size)], peer_send.at[part, 0]
        )
        keep.start()
        return copies, keep

    def collect(got, shared, at, size, part):
        shared[1].wait()
        for n in range(1, N_FREQ):
            rows = pl.ds(lax.rem(q + N_FREQ - n, N_FREQ) * PER_SET + at % PER_SET, size)
            pltpu.make_async_copy(
                total.at[pl.ds(0, size)], got.at[rows], peer_recv.at[part, n]
            ).wait()

    pltpu.make_async_copy(from_a, from_a, recv_a).wait()
    wanted = lax.rem(q + N_FREQ - group_at(other), N_FREQ)
    for s in range(PER_SET):
        at = jnp.int32(0)
        for g in range(N_FREQ):
            j = MEMBERS[g][min(s, len(MEMBERS[g]) - 1)]
            at = jnp.where(wanted == g, lax.div(there(DELTA[j], 1), 4), at)
        total[s] = (from_a[at, 0] + from_a[at, 1]) + (from_a[at, 2] + from_a[at, 3])
    first = share(got_a, 0, PER_SET, 0)
    later = []
    wanted = lax.rem(q + N_FREQ - group_at(LAST), N_FREQ)
    for s in range(PER_SET):
        present = pick(wanted, [int(s < len(m)) for m in MEMBERS]) == 1

        @pl.when(present)
        def _():
            pltpu.make_async_copy(from_b.at[s], from_b.at[s], recv_b.at[s]).wait()
            total[PER_SET + s] = (from_b[s, 0] + from_b[s, 1]) + (from_b[s, 2] + from_b[s, 3])

        @pl.when(jnp.logical_not(present))
        def _():
            total[PER_SET + s] = jnp.zeros((16, 128), f32)

        later.append(share(got_b, PER_SET + s, 1, 1 + s))

    peers = first[0]
    collect(got_a, first, 0, PER_SET, 0)
    out[0] = image_part(0, q, other, got_a, table, pre, pim, br, bi, zr, zi)
    drain(0)

    @pl.when(is_last)
    def _():
        drain(1)

    for s, shared in enumerate(later):
        peers = peers + shared[0]
        collect(got_b, shared, PER_SET + s, 1, 1 + s)
    for p in peers:
        p.wait_send()
    out[0] = out[0] + image_part(1, q, other, got_b, table, pre, pim, br, bi, zr, zi)


def on_device(visibilities, coords, corners, owners, assign, counts):
    d, plain = image_table()
    scale = 1.0 / (SUB * SUB * math.sqrt(2 * BPC * BLK * CHANS))
    high = (d * scale).astype(bf16)
    low = (d * scale - high.astype(np.float64)).astype(bf16)
    vmem = pl.BlockSpec(memory_space=pltpu.VMEM)
    hbm = pl.BlockSpec(memory_space=pl.ANY)
    dma = pltpu.SemaphoreType.DMA
    return pl.pallas_call(
        fused_kernel,
        out_shape=pltpu.VMEM((1, G // N_FREQ, G), f32),
        in_specs=[hbm] * 8,
        out_specs=vmem,
        scratch_shapes=[
            pltpu.SMEM((2,), jnp.int32),
            pltpu.SMEM((BPC, 2, N_FACET), jnp.int32),
            pltpu.SMEM((1, 2 * BPC), jnp.int32),
            pltpu.SMEM((1,), jnp.int32),
            pltpu.VMEM((G, 3 * SUB), bf16),
            pltpu.VMEM((SUB, G), f32),
            pltpu.VMEM((BPC, 2, CH, BLK), f32),
            pltpu.VMEM((3 * BPC, 1, BLK), f32),
        ]
        + unit_scratch()
        + [
            pltpu.VMEM((2, N_FACET, 16, 128), f32),
            pltpu.VMEM((8, N_FREQ, 16, 128), f32),
            pltpu.VMEM((PER_SET, N_FREQ, 16, 128), f32),
            pltpu.VMEM((SLOTS, 16, 128), f32),
            pltpu.VMEM((N_FREQ * PER_SET, 16, 128), f32),
            pltpu.VMEM((N_FREQ * PER_SET, 16, 128), f32),
            pltpu.VMEM((2, 128, WIDE), f32),
            pltpu.VMEM((2, 128, WIDE), f32),
            pltpu.VMEM((2, 2, WIDE, G), bf16),
            pltpu.VMEM((2, 2, WIDE, G), bf16),
            pltpu.VMEM((32, WIDE), f32),
            pltpu.VMEM((32, WIDE), f32),
            pltpu.SemaphoreType.REGULAR,
            pltpu.SemaphoreType.REGULAR,
            pltpu.SemaphoreType.REGULAR,
            dma((6,)),
            dma((BPC, 2)),
            dma((BPC, 2)),
            dma((2,)),
            dma,
            dma((PER_SET,)),
            dma((1 + PER_SET, N_FREQ)),
            dma((1 + PER_SET, N_FREQ)),
        ],
        compiler_params=pltpu.CompilerParams(collective_id=0, has_side_effects=True),
        name="grid_and_image",
    )(
        visibilities,
        jnp.transpose(coords, (1, 2, 0, 3)).reshape(3 * BPC, 1, BLK),
        owners,
        jnp.transpose(corners, (2, 0, 1)),
        assign,
        counts,
        jnp.asarray(np.concatenate([high, high, low], axis=1)),
        jnp.asarray(plain.T, f32),
    )


def solution(mesh):
    placed = (
        P("facet", None, None, "freq", None),
        P("facet", None, None, None),
        P(),
        P(),
        P("facet", None),
        P("facet"),
    )
    return jax.shard_map(
        on_device, mesh=mesh, in_specs=placed, out_specs=P("facet", "freq", None), check_vma=False
    )
```
